32 devices in a mesh: wl: 4 (over x, core), row: 4 (over z), col: 2 (over y).
Axes of the slice: x: 2, y: 2, z: 4, core: 2. Of those that a mesh axis runs over, the one named last changes fastest.
Arguments:
- cotangent: bfloat16 [4, 2, 4096, 4096], P('wl', None, 'row', 'col'), may hold values from -6 to 6
- incident: bfloat16 [4, 4096, 4096], P('wl', 'row', 'col'), may hold values from 0.5 to 1.5
- aperture_tiles: int32 [32, 32], P('row', 'col'), may hold values 0 or 1
- charge: int32 [4], P('wl'), may hold values from 2 to 8
- wl_index: int32 [4], P('wl'), may hold values from 0 to 16
Outputs:
- gradient: bfloat16 [4096, 4096], P('row', 'col')
The draws below stay inside these ranges and needn't reach their ends.
All inputs are finite; a program needn't handle non-finite values. No bound on the sum of `aperture_tiles` on one device may be relied on, other than what follows from the above.
Results may differ from the reference program's by a relative error of at most 0.013.
Values may be sent and summed in bfloat16 or wider, within the bound.
No kernel may reach another device: no remote copies, remote signals or barrier semaphores. Data moves between devices by JAX's collectives and lax.ppermute only.
A program may use at most 128 MiB of HBM per device.

```python
import math
import jax
import jax.numpy as jnp
from jax import lax

N = 4096
M = 512
TILE = 128
NW = 4
N_COL = 2


def plant(result, stream_key, low, top_value):
    dims = result.shape
    place = [jax.random.randint(jax.random.fold_in(stream_key, axis), (), 0, dims[axis]) for axis in range(len(dims))]
    result = result.at[tuple(place)].set(low)
    longest = dims.index(max(dims))
    place[longest] = (place[longest] + 1) % dims[longest]
    return result.at[tuple(place)].set(top_value)


def steps_of(stream_key, shape, cuts, least, top_value):
    gain, own = 1.0, jax.random.fold_in(stream_key, 6)
    for position, blocks in cuts:
        draws = jnp.exp(jax.random.uniform(jax.random.fold_in(own, position), (blocks,), jnp.float32, least / len(cuts), top_value / len(cuts)))
        gain = gain * jnp.repeat(draws, shape[position] // blocks).reshape([-1 if axis == position else 1 for axis in range(len(shape))])
    return gain


def scatter_about(stream_key, shape, scale, most, split=(), held_as=jnp.bfloat16):
    factor_of = steps_of(stream_key, shape, split, -0.22, 0.18) if split else 1.0
    drawn = jax.random.normal(stream_key, shape, jnp.float32) * scale * factor_of
    return jnp.minimum(jnp.maximum(drawn, -most), most).astype(held_as)


def setup_inputs(seed: int = 0) -> dict:
    seeds = jax.random.split(jax.random.key(seed), 6)
    return {
        "cotangent": scatter_about(seeds[0], (NW, 2, N, N), 1.0, 6.0, ((0, 4), (2, 4), (3, 2))),
        "incident": jnp.clip(0.5 + 1.0 * jax.random.uniform(seeds[1], (NW, N, N), jnp.float32) ** steps_of(seeds[1], (NW, N, N), ((0, 4), (1, 4), (2, 2)), -0.2, 0.2), 0.5, 1.5).astype(jnp.bfloat16),
        "aperture_tiles": plant((jax.random.randint(seeds[2], (N // TILE, N // TILE), 0, 4) < 3).astype(jnp.int32), jax.random.fold_in(seeds[2], 1), 0, 1),
        "charge": plant(jax.random.randint(seeds[3], (NW,), 2, 9), jax.random.fold_in(seeds[3], 1), 2, 8).astype(jnp.int32),
        "wl_index": plant(jax.random.randint(seeds[4], (NW,), 0, 17), jax.random.fold_in(seeds[4], 1), 0, 16).astype(jnp.int32),
    }


def phase_grid(offset, amount, extent, size_m, index_value, transpose):
    pupil_pos = 2 * (offset + jnp.arange(amount, dtype=jnp.int32)) - extent + 1
    focal_pos = 2 * jnp.arange(size_m, dtype=jnp.int32) - size_m + 1
    if transpose:
        product = focal_pos[:, None] * pupil_pos[None, :]
    else:
        product = pupil_pos[:, None] * focal_pos[None, :]
    period = (size_m * (32 + index_value)).astype(jnp.int32)
    remainder = jnp.remainder(4 * product, period)
    return remainder.astype(jnp.float32) * (jnp.float32(2.0 * math.pi) / period.astype(jnp.float32))

def vortex(focal_re, focal_im, row_offset, charge_value):
    size_m = focal_re.shape[1]
    row_count = focal_re.shape[0]
    row_pos = (2 * (row_offset + jnp.arange(row_count, dtype=jnp.int32)) - size_m + 1).astype(jnp.float32)
    col_pos = (2 * jnp.arange(size_m, dtype=jnp.int32) - size_m + 1).astype(jnp.float32)
    angles = jnp.arctan2(col_pos[None, :], row_pos[:, None]) * charge_value.astype(jnp.float32)
    cosine = jnp.cos(angles)
    sine_value = jnp.sin(angles)
    turned_re = focal_re * cosine + focal_im * sine_value
    turned_im = focal_im * cosine - focal_re * sine_value
    return jnp.concatenate([turned_re, turned_im], axis=1).astype(jnp.bfloat16)

def rounded(values):
    return lax.optimization_barrier(values.astype(jnp.bfloat16)).astype(jnp.float32)

def reference(cotangent, incident, aperture_tiles, charge, wl_index):
    extent = cotangent.shape[2]
    tile_rows = aperture_tiles.shape[0]
    tile_size = extent // tile_rows
    open_tiles = (aperture_tiles == 1).astype(jnp.float32)
    live_cells = jnp.broadcast_to(open_tiles[:, None, :, None], (tile_rows, tile_size, tile_rows, tile_size)).reshape(extent, extent)
    block_width = extent // N_COL
    norm_fwd = 1.0 / math.sqrt(extent)
    norm_back = 1.0 / math.sqrt(M)
    highest = lax.Precision.HIGHEST
    contract_first = (((0,), (0,)), ((), ()))

    def one_wave(accumulated, inputs):
        cot_wave, inc_wave, charge_wave, index_wave = inputs
        phase = phase_grid(0, extent, extent, M, index_wave, False)
        fwd_cos = rounded(jnp.cos(phase) * norm_fwd)
        fwd_sin = rounded(jnp.sin(phase) * norm_fwd)
        back_cos = rounded(jnp.cos(phase) * norm_back)
        back_sin = rounded(jnp.sin(phase) * norm_back)
        grad_re = cot_wave[0].astype(jnp.float32) * live_cells
        grad_im = cot_wave[1].astype(jnp.float32) * live_cells
        fwd_table = jnp.concatenate([fwd_cos, fwd_sin], axis=1)

        def add_block(total_inner, block_index):
            column_start = (block_index * block_width).astype(jnp.int32)
            part_re = lax.dynamic_slice_in_dim(grad_re, column_start, block_width, 1)
            part_im = lax.dynamic_slice_in_dim(grad_im, column_start, block_width, 1)
            table_rows = lax.dynamic_slice_in_dim(fwd_table, column_start, block_width, 0)
            prod_re = jnp.dot(part_re, table_rows, precision=highest)
            prod_im = jnp.dot(part_im, table_rows, precision=highest)
            inner_re = prod_re[:, :M] - prod_im[:, M:]
            inner_im = prod_re[:, M:] + prod_im[:, :M]
            return (total_inner + rounded(jnp.concatenate([inner_re, inner_im], axis=1)), None)
        summed, _ = lax.scan(add_block, jnp.zeros((extent, 2 * M), jnp.float32), jnp.arange(N_COL, dtype=jnp.int32))
        with_cos = lax.dot_general(fwd_cos, summed, contract_first, precision=highest)
        with_sin = lax.dot_general(fwd_sin, summed, contract_first, precision=highest)
        focal_re = with_cos[:, :M] - with_sin[:, M:]
        focal_im = with_cos[:, M:] + with_sin[:, :M]
        turned = lax.optimization_barrier(vortex(focal_re, focal_im, 0, charge_wave)).astype(jnp.float32)
        first_part = jnp.dot(back_cos, turned, precision=highest)
        second_part = jnp.dot(back_sin, turned, precision=highest)
        back_y = rounded(jnp.concatenate([first_part[:, :M] + second_part[:, M:], first_part[:, M:] - second_part[:, :M]], axis=1))
        back_stack = jnp.concatenate([back_cos.T, back_sin.T], axis=0)
        back_real = jnp.dot(back_y, back_stack, precision=highest)
        wave_term = rounded(back_real * inc_wave.astype(jnp.float32) * live_cells)
        return (accumulated + wave_term, None)
    total, _ = lax.scan(one_wave, jnp.zeros((extent, extent), jnp.float32), (cotangent, incident, charge, wl_index))
    return total.astype(jnp.bfloat16)
```

```python
import math

import jax
import jax.numpy as jnp
from jax import lax
from jax.experimental import pallas as pl
from jax.experimental.pallas import tpu as pltpu
from jax.sharding import PartitionSpec as P

M = 512
HALF = M // 2
F32 = jnp.float32
BF16 = jnp.bfloat16


def iota(shape, axis):
    return lax.broadcasted_iota(jnp.int32, shape, axis).astype(F32)


def unit_phasor(product, period):
    turns = jnp.floor(product / period + 0.5)
    rest = product - turns * period
    quarter = jnp.floor(4.0 * rest / period + 0.5)
    theta = (4.0 * rest - quarter * period) / period * (0.5 * math.pi)
    sq = theta * theta
    sin_p = theta * (
        1.0 + sq * (-1.0 / 6.0 + sq * (1.0 / 120.0 + sq * (-1.0 / 5040.0 + sq / 362880.0)))
    )
    cos_p = 1.0 + sq * (
        -0.5 + sq * (1.0 / 24.0 + sq * (-1.0 / 720.0 + sq * (1.0 / 40320.0 - sq / 3628800.0)))
    )
    size = jnp.abs(quarter)
    odd = size == 1.0
    flip = jnp.where(size == 2.0, -1.0, 1.0)
    side = jnp.where(quarter < 0.0, -1.0, 1.0)
    cosine = jnp.where(odd, -side * sin_p, flip * cos_p)
    sine = jnp.where(odd, side * cos_p, flip * sin_p)
    return cosine, sine


def turn(first, second):
    c1, s1 = first
    c2, s2 = second
    return c1 * c2 - s1 * s2, s1 * c2 + c1 * s2


def quarter_period(index_value):
    return ((index_value + 32) * (M // 4)).astype(F32)


def table_focal_lanes(write, period, first, extent, amount, fine_ref, lanes=None, lane_count=HALF):
    block = 256
    focal = 2.0 * iota((16, lane_count), 1) + 1.0 if lanes is None else lanes
    step = iota((16, lane_count), 0)
    fine = unit_phasor(2.0 * step * focal, jnp.full((16, lane_count), period, F32))
    mid = unit_phasor(32.0 * step * focal, jnp.full((16, lane_count), period, F32))
    for b in range(16):
        re, im = turn((mid[0][b : b + 1], mid[1][b : b + 1]), fine)
        fine_ref[0, 16 * b : 16 * b + 16, :] = re
        fine_ref[1, 16 * b : 16 * b + 16, :] = im
    count = amount // block
    start = (2 * first - extent + 1).astype(F32)
    top = -(-count // 8) * 8
    focal_top = 2.0 * iota((top, lane_count), 1) + 1.0 if lanes is None else jnp.broadcast_to(lanes[:1], (top, lane_count))
    coarse = unit_phasor(
        (start + 2.0 * block * iota((top, lane_count), 0)) * focal_top,
        jnp.full((top, lane_count), period, F32),
    )
    for a in range(count):
        for part in range(0, block, 64):
            re, im = turn(
                (coarse[0][a : a + 1], coarse[1][a : a + 1]),
                (fine_ref[0, part : part + 64, :], fine_ref[1, part : part + 64, :]),
            )
            write(a * block + part, 64, re.astype(BF16), im.astype(BF16))


def table_pupil_lanes(write, period, first, extent, amount, fine_ref, focal_first, focal_count):
    count = amount // 128
    shape = (focal_count, 128)
    focal = 2.0 * (focal_first + iota(shape, 0)) + 1.0
    lane = iota(shape, 1)
    full = jnp.full(shape, period, F32)
    fine = unit_phasor(2.0 * lane * focal, full)
    fine_ref[0, :focal_count, :128] = fine[0]
    fine_ref[1, :focal_count, :128] = fine[1]
    start = (2 * first - extent + 1).astype(F32)
    coarse = unit_phasor((start + 256.0 * lane) * focal, full)
    fine_ref[0, :focal_count, 128:] = coarse[0]
    fine_ref[1, :focal_count, 128:] = coarse[1]
    for a in range(count):
        for part in range(0, focal_count, 64):
            rows = slice(part, min(part + 64, focal_count))
            re, im = turn(
                (fine_ref[0, rows, 128 + a : 129 + a], fine_ref[1, rows, 128 + a : 129 + a]),
                (fine_ref[0, rows, :128], fine_ref[1, rows, :128]),
            )
            write(part, a * 128, re.astype(BF16), im.astype(BF16))


def live_row(tiles_ref, tile_row, cells):
    tile_cols = tiles_ref.shape[1]
    width = cells // tile_cols
    parts = [
        jnp.full((1, width), jnp.where(tiles_ref[tile_row, j] == 1, 1.0, 0.0), F32)
        for j in range(tile_cols)
    ]
    return jnp.concatenate(parts, axis=1)


def forward_kernel(index_ref, charge_ref, tiles_ref, cot_ref, *refs, rows, cols, n_row, n_col, piecewise):
    outs, (col_tab, row_tab, inner, fine_ref, t_ref) = refs[:-5], refs[-5:]
    step = pl.program_id(0)
    block = cot_ref.shape[2]
    extent = rows * n_row
    row_at = lax.axis_index("row")
    col_at = lax.axis_index("col")
    tile_size = rows // tiles_ref.shape[0]

    @pl.when(step == 0)
    def _():
        period = quarter_period(index_ref[0])

        def write_col(at, amount, re, im):
            col_tab[at : at + amount, :HALF] = re
            col_tab[at : at + amount, HALF:] = im

        table_focal_lanes(write_col, period, col_at * cols, extent, cols, fine_ref)

        def write_row(part, at, re, im):
            row_tab[part : part + 64, at : at + 128] = re
            row_tab[HALF + part : HALF + part + 64, at : at + 128] = im

        table_pupil_lanes(write_row, period, row_at * rows, extent, rows, fine_ref, 0.0, HALF)

    halves = []
    for part in range(2):
        for h in range(block // tile_size):
            mask = live_row(tiles_ref, step * (block // tile_size) + h, cols).astype(BF16)
            halves.append(cot_ref[0, part, h * tile_size : (h + 1) * tile_size, :] * mask)
    prod = jnp.dot(jnp.concatenate(halves, axis=0), col_tab[...], preferred_element_type=F32)
    at = pl.ds(pl.multiple_of(step * block, block), block)
    inner[at, :M] = prod[:block].astype(BF16)
    inner[at, M:] = prod[block:].astype(BF16)

    @pl.when(step == pl.num_programs(0) - 1)
    def _():
        charge = charge_ref[0]
        even = jnp.where(charge % 2 == 0, 1.0, 0.0).astype(F32)
        odd = 1.0 - even
        scale = 4.0 / (extent * M)
        chunk = 64
        shape = (chunk, HALF)
        for ub in range(HALF // chunk):
            q_c = jnp.dot(row_tab[ub * chunk : (ub + 1) * chunk, :], inner[...], preferred_element_type=F32)
            q_s = jnp.dot(
                row_tab[HALF + ub * chunk : HALF + (ub + 1) * chunk, :], inner[...], preferred_element_type=F32
            )
            u = 2.0 * (iota(shape, 0) + float(ub * chunk)) + 1.0
            v = 2.0 * iota(shape, 1) + 1.0
            inv = 1.0 / jnp.sqrt(u * u + v * v)
            power = (u * inv, v * inv)
            total = (jnp.full(shape, scale, F32), jnp.zeros(shape, F32))
            for bit in range(4):
                taken = (charge >> bit) % 2 == 1
                multiplied = turn(total, power)
                total = tuple(jnp.where(taken, new, old) for new, old in zip(multiplied, total))
                power = turn(power, power)
            c, s = total
            ce, se, co, so = c * even, s * even, c * odd, s * odd
            ca, cb, cc, cd = (q_c[:, k * HALF : (k + 1) * HALF] for k in range(4))
            sa, sb, sc, sd = (q_s[:, k * HALF : (k + 1) * HALF] for k in range(4))
            t_ee = ce * ca - se * sd + so * cb - co * sc
            t_eo = ce * cb + se * sc - so * ca - co * sd
            t_oe = ce * sa + se * cd + co * cc + so * sb
            t_oo = ce * sb - se * cc + co * cd - so * sa
            per = t_ref.shape[1]
            for j in range(chunk // per if per < chunk else 1):
                span = min(per, chunk)
                rows_j = slice(j * span, (j + 1) * span)
                first = ub * chunk + j * span
                to = slice(first % per, first % per + span)
                t_ref[first // per, to, :HALF] = t_ee[rows_j]
                t_ref[first // per, to, HALF:] = t_eo[rows_j]
                first += HALF
                to = slice(first % per, first % per + span)
                t_ref[first // per, to, :HALF] = t_oe[rows_j]
                t_ref[first // per, to, HALF:] = t_oo[rows_j]
        for ky in range(n_col):
            for kz in range(n_row):
                source = lax.rem(col_at + ky, n_col) * n_row + lax.rem(row_at + kz, n_row)
                value = t_ref[source].astype(BF16)
                if piecewise:
                    outs[ky * n_row + kz][...] = value
                else:
                    outs[ky][kz] = value


def forward(index, charge, tiles, cotangent, n_row, n_col):
    rows, cols = cotangent.shape[2:]
    block = min(256, rows)
    per = M // (n_row * n_col)
    piecewise = per >= 16
    if piecewise:
        out_shape = [jax.ShapeDtypeStruct((per, M), BF16)] * (n_row * n_col)
        out_specs = [pl.BlockSpec((per, M), lambda i: (0, 0))] * (n_row * n_col)
    else:
        out_shape = [jax.ShapeDtypeStruct((n_row, per, M), BF16)] * n_col
        out_specs = [pl.BlockSpec((n_row, per, M), lambda i: (0, 0, 0))] * n_col

    def kernel(*refs):
        forward_kernel(*refs, rows=rows, cols=cols, n_row=n_row, n_col=n_col, piecewise=piecewise)

    smem = pl.BlockSpec(memory_space=pltpu.SMEM)
    outs = pl.pallas_call(
        kernel,
        grid=(rows // block,),
        in_specs=[smem, smem, smem, pl.BlockSpec((1, 2, block, cols), lambda i: (0, 0, i, 0))],
        out_specs=out_specs,
        out_shape=out_shape,
        scratch_shapes=[
            pltpu.VMEM((cols, M), BF16),
            pltpu.VMEM((M, rows), BF16),
            pltpu.VMEM((rows, 2 * M), BF16),
            pltpu.VMEM((2, HALF, HALF), F32),
            pltpu.VMEM((n_row * n_col, per, M), F32),
        ],
        compiler_params=pltpu.CompilerParams(vmem_limit_bytes=40 << 20),
        cost_estimate=pl.CostEstimate(
            flops=2 * rows * 2 * M * (cols + M), bytes_accessed=4 * rows * cols, transcendentals=0
        ),
        name="forward",
    )(index, charge, tiles, cotangent)
    if piecewise:
        return [outs[ky * n_row : (ky + 1) * n_row] for ky in range(n_col)]
    return [[out] for out in outs]


def shift(value, axis, amount):
    size = lax.axis_size(axis)
    return lax.ppermute(value, axis, [(i, (i + amount) % size) for i in range(size)])


def swap(value, axis, bit):
    size = lax.axis_size(axis)
    return lax.ppermute(value, axis, [(i, i ^ bit) for i in range(size)])


def add_up(parts):
    total = parts[0].astype(F32)
    for part in parts[1:]:
        total = total + part.astype(F32)
    return total


def reduce_and_gather(parts, n_row, n_col):
    here = []
    arrived = [[shift(piece, "col", ky) for piece in parts[ky]] for ky in range(1, n_col)]
    for kz in range(len(parts[0])):
        here.append(add_up([parts[0][kz]] + [a[kz] for a in arrived]).astype(BF16))
    if len(here) == 1 and n_row > 1:
        here = [here[0][kz] for kz in range(n_row)]
    moved = [shift(here[kz], "row", kz) for kz in range(1, n_row)]
    mine = add_up([here[0]] + moved).astype(BF16)
    gathered = [mine] + [shift(mine, "row", kz) for kz in range(1, n_row)]
    if mine.shape[0] < 16:
        gathered = [jnp.concatenate(gathered, axis=0)]
    return [gathered] + [[shift(piece, "col", ky) for piece in gathered] for ky in range(1, n_col)]


def table_kernel(index_ref, *refs, rows, cols, n_row, n_col, full_rows, waves, own_rows):
    row_tab, col_tab, fine_ref = refs
    extent = full_rows * n_row
    row_at = lax.axis_index("row")
    col_at = lax.axis_index("col")
    half_at = lax.rem(lax.axis_index("wl"), 2)
    per = M // (n_row * n_col)
    for w in range(waves):
        period = quarter_period(index_ref[w])

        def write_col(part, at, re, im):
            col_tab[w, part : part + 64, at : at + 128] = re
            col_tab[w, HALF + part : HALF + part + 64, at : at + 128] = im

        table_pupil_lanes(write_col, period, col_at * cols, extent, cols, fine_ref, 0.0, HALF)

        lane = lax.broadcasted_iota(jnp.int32, (16, M), 1)
        block = lane // per
        from_col = block // n_row
        from_row = block % n_row
        owner = ((col_at - from_col + n_col) % n_col) * n_row + (row_at - from_row + n_row) % n_row
        place = owner * per + lane % per
        is_sin = place >= HALF
        focal = 2.0 * jnp.where(is_sin, place - HALF, place).astype(F32) + 1.0
        for side in range(2):
            lanes = slice(side * HALF, (side + 1) * HALF)
            sine = is_sin[:1, lanes]

            def write_row(at, amount, re, im, lanes=lanes, sine=sine):
                row_tab[w, at : at + amount, lanes] = jnp.where(
                    sine, im.astype(F32), re.astype(F32)
                ).astype(BF16)

            table_focal_lanes(
                write_row,
                period,
                row_at * full_rows + half_at * rows,
                extent,
                own_rows,
                fine_ref,
                lanes=focal[:, lanes],
            )


def make_tables(indices, rows, cols, n_row, n_col, full_rows, waves):
    own_rows = max(rows, 256)

    def kernel(*refs):
        table_kernel(
            *refs, rows=rows, cols=cols, n_row=n_row, n_col=n_col, full_rows=full_rows, waves=waves, own_rows=own_rows
        )

    return pl.pallas_call(
        kernel,
        in_specs=[pl.BlockSpec(memory_space=pltpu.SMEM)],
        out_specs=[pl.BlockSpec(memory_space=pltpu.VMEM)] * 2,
        out_shape=[
            jax.ShapeDtypeStruct((waves, own_rows, M), BF16),
            jax.ShapeDtypeStruct((waves, M, cols), BF16),
        ],
        scratch_shapes=[pltpu.VMEM((2, HALF, HALF), F32)],
        cost_estimate=pl.CostEstimate(flops=40 * M * cols, bytes_accessed=4 * M * cols, transcendentals=0),
        name="tables",
    )(indices)


def backward_kernel(tiles_ref, *refs, n_pieces, starts, waves, chunk_rows, tile_size, rows, base):
    pieces = refs[: waves * n_pieces]
    row_tab, col_tab, own_inc, other_inc, out_ref, t_ref = refs[waves * n_pieces :]
    step = pl.program_id(0)
    half_at = lax.rem(lax.axis_index("wl"), 2)

    @pl.when(step == 0)
    def _():
        for w in range(waves):
            for k in range(n_pieces):
                piece = pieces[w * n_pieces + k]
                t_ref[w, starts[k] : starts[k] + piece.shape[0], :] = piece[...]

    at = base + step * chunk_rows
    cols = out_ref.shape[1]
    first_tile = (half_at * rows + at) // tile_size
    incidents = (own_inc, other_inc)
    total = None
    for w in range(waves):
        from_rows = pl.ds(pl.multiple_of(at, chunk_rows), chunk_rows)
        back_y = jnp.dot(row_tab[w, from_rows, :], t_ref[w], preferred_element_type=F32).astype(BF16)
        back = jnp.dot(back_y, col_tab[w], preferred_element_type=F32)
        inc = incidents[w]
        term = back * inc[...].reshape(chunk_rows, cols).astype(F32)
        total = term if total is None else total + term
    if chunk_rows <= tile_size:
        total = total * live_row(tiles_ref, first_tile, cols)
        out_ref[...] = total.astype(BF16)
    else:
        for h in range(chunk_rows // tile_size):
            span = slice(h * tile_size, (h + 1) * tile_size)
            out_ref[span, :] = (total[span] * live_row(tiles_ref, first_tile + h, cols)).astype(BF16)


def backward(tiles, pieces, tables, own_inc, other_inc, base, amount, chunk_rows, tile_size):
    rows, cols = own_inc.shape
    waves = len(pieces)
    n_pieces = len(pieces[0])
    starts = []
    at = 0
    for piece in pieces[0]:
        starts.append(at)
        at += piece.shape[0]

    def kernel(*refs):
        backward_kernel(
            *refs,
            n_pieces=n_pieces,
            starts=starts,
            waves=waves,
            chunk_rows=chunk_rows,
            tile_size=tile_size,
            rows=rows,
            base=base,
        )

    vmem = pl.BlockSpec(memory_space=pltpu.VMEM)
    inc_spec = pl.BlockSpec((chunk_rows, cols), lambda i: (i + base // chunk_rows, 0))
    flat = [piece for wave in pieces for piece in wave]
    return pl.pallas_call(
        kernel,
        grid=(amount // chunk_rows,),
        in_specs=[pl.BlockSpec(memory_space=pltpu.SMEM)]
        + [vmem] * len(flat)
        + [vmem, vmem, inc_spec, inc_spec],
        out_specs=pl.BlockSpec((chunk_rows, cols), lambda i: (i, 0)),
        out_shape=jax.ShapeDtypeStruct((amount, cols), BF16),
        scratch_shapes=[pltpu.VMEM((waves, M, M), BF16)],
        compiler_params=pltpu.CompilerParams(vmem_limit_bytes=40 << 20),
        cost_estimate=pl.CostEstimate(
            flops=2 * waves * amount * M * (cols + M), bytes_accessed=6 * amount * cols, transcendentals=0
        ),
        name="backward",
    )(tiles, *flat, *tables, own_inc, other_inc)


def per_device(cotangent, incident, aperture_tiles, charge, wl_index):
    rows, cols = cotangent.shape[2:]
    n_row = lax.axis_size("row")
    n_col = lax.axis_size("col")
    n_wl = lax.axis_size("wl")
    tile_size = rows // aperture_tiles.shape[0]
    half = rows // 2
    core = lax.axis_index("wl") % 2

    parts = forward(wl_index, charge, aperture_tiles, cotangent, n_row, n_col)
    indices = jnp.concatenate([wl_index, swap(wl_index, "wl", 1)])
    tables = make_tables(indices, half, cols, n_row, n_col, rows, 2)
    own_inc = lax.dynamic_slice_in_dim(incident[0], core * half, half, 0)
    other_inc = swap(lax.dynamic_slice_in_dim(incident[0], (1 - core) * half, half, 0), "wl", 1)

    gathered = [piece for group in reduce_and_gather(parts, n_row, n_col) for piece in group]
    partner = [swap(piece, "wl", 1) for piece in gathered]
    if gathered[0].shape[0] % 16:
        gathered = [jnp.concatenate(gathered, axis=0)]
        partner = [jnp.concatenate(partner, axis=0)]

    chunk = min(128, half)
    result = jnp.zeros((rows, cols), BF16)
    for base in range(0, half, chunk):
        pair = backward(
            aperture_tiles, [gathered, partner], tables, own_inc, other_inc, base, chunk, chunk, tile_size
        )
        bit = 2
        while bit < n_wl:
            pair = add_up([pair, swap(pair, "wl", bit)]).astype(BF16)
            bit *= 2
        back = swap(pair, "wl", 1)
        result = lax.dynamic_update_slice(result, pair, (core * half + base, 0))
        result = lax.dynamic_update_slice(result, back, ((1 - core) * half + base, 0))
    return result


def solution(mesh):
    return jax.shard_map(
        per_device,
        mesh=mesh,
        in_specs=(
            P("wl", None, "row", "col"),
            P("wl", "row", "col"),
            P("row", "col"),
            P("wl"),
            P("wl"),
        ),
        out_specs=P("row", "col"),
        check_vma=False,
    )
```

```python
import math

import jax
import jax.numpy as jnp
from jax import lax
from jax.experimental import pallas as pl
from jax.experimental.pallas import tpu as pltpu
from jax.sharding import PartitionSpec as P

M = 512
HALF = M // 2
F32 = jnp.float32
BF16 = jnp.bfloat16


def iota(shape, axis):
    return lax.broadcasted_iota(jnp.int32, shape, axis).astype(F32)


def unit_phasor(product, period):
    turns = jnp.floor(product / period + 0.5)
    rest = product - turns * period
    quarter = jnp.floor(4.0 * rest / period + 0.5)
    theta = (4.0 * rest - quarter * period) / period * (0.5 * math.pi)
    sq = theta * theta
    sin_p = theta * (
        1.0 + sq * (-1.0 / 6.0 + sq * (1.0 / 120.0 + sq * (-1.0 / 5040.0 + sq / 362880.0)))
    )
    cos_p = 1.0 + sq * (
        -0.5 + sq * (1.0 / 24.0 + sq * (-1.0 / 720.0 + sq * (1.0 / 40320.0 - sq / 3628800.0)))
    )
    size = jnp.abs(quarter)
    odd = size == 1.0
    flip = jnp.where(size == 2.0, -1.0, 1.0)
    side = jnp.where(quarter < 0.0, -1.0, 1.0)
    cosine = jnp.where(odd, -side * sin_p, flip * cos_p)
    sine = jnp.where(odd, side * cos_p, flip * sin_p)
    return cosine, sine


def turn(first, second):
    c1, s1 = first
    c2, s2 = second
    return c1 * c2 - s1 * s2, s1 * c2 + c1 * s2


def quarter_period(index_value):
    return ((index_value + 32) * (M // 4)).astype(F32)


def table_focal_lanes(write, period, first, extent, amount, fine_ref, lanes=None, lane_count=HALF):
    block = 256
    focal = 2.0 * iota((16, lane_count), 1) + 1.0 if lanes is None else lanes
    step = iota((16, lane_count), 0)
    fine = unit_phasor(2.0 * step * focal, jnp.full((16, lane_count), period, F32))
    mid = unit_phasor(32.0 * step * focal, jnp.full((16, lane_count), period, F32))
    for b in range(16):
        re, im = turn((mid[0][b : b + 1], mid[1][b : b + 1]), fine)
        fine_ref[0, 16 * b : 16 * b + 16, :] = re
        fine_ref[1, 16 * b : 16 * b + 16, :] = im
    count = amount // block
    start = (2 * first - extent + 1).astype(F32)
    top = -(-count // 8) * 8
    focal_top = 2.0 * iota((top, lane_count), 1) + 1.0 if lanes is None else jnp.broadcast_to(lanes[:1], (top, lane_count))
    coarse = unit_phasor(
        (start + 2.0 * block * iota((top, lane_count), 0)) * focal_top,
        jnp.full((top, lane_count), period, F32),
    )
    for a in range(count):
        for part in range(0, block, 64):
            re, im = turn(
                (coarse[0][a : a + 1], coarse[1][a : a + 1]),
                (fine_ref[0, part : part + 64, :], fine_ref[1, part : part + 64, :]),
            )
            write(a * block + part, 64, re.astype(BF16), im.astype(BF16))


def table_pupil_lanes(write, period, first, extent, amount, fine_ref, focal_first, focal_count):
    count = amount // 128
    shape = (focal_count, 128)
    focal = 2.0 * (focal_first + iota(shape, 0)) + 1.0
    lane = iota(shape, 1)
    full = jnp.full(shape, period, F32)
    fine = unit_phasor(2.0 * lane * focal, full)
    fine_ref[0, :focal_count, :128] = fine[0]
    fine_ref[1, :focal_count, :128] = fine[1]
    start = (2 * first - extent + 1).astype(F32)
    coarse = unit_phasor((start + 256.0 * lane) * focal, full)
    fine_ref[0, :focal_count, 128:] = coarse[0]
    fine_ref[1, :focal_count, 128:] = coarse[1]
    for a in range(count):
        for part in range(0, focal_count, 64):
            rows = slice(part, min(part + 64, focal_count))
            re, im = turn(
                (fine_ref[0, rows, 128 + a : 129 + a], fine_ref[1, rows, 128 + a : 129 + a]),
                (fine_ref[0, rows, :128], fine_ref[1, rows, :128]),
            )
            write(part, a * 128, re.astype(BF16), im.astype(BF16))


def live_row(tiles_ref, tile_row, cells):
    tile_cols = tiles_ref.shape[1]
    width = cells // tile_cols
    parts = [
        jnp.full((1, width), jnp.where(tiles_ref[tile_row, j] == 1, 1.0, 0.0), F32)
        for j in range(tile_cols)
    ]
    return jnp.concatenate(parts, axis=1)


def forward_kernel(index_ref, charge_ref, tiles_ref, cot_ref, *refs, rows, cols, n_row, n_col, groups):
    outs, col_tab = refs[:-5], refs[-5]
    row_tab, inner, fine_ref, t_ref = refs[-4:]
    step = pl.program_id(0)
    block = cot_ref.shape[2]
    extent = rows * n_row
    row_at = lax.axis_index("row")
    col_at = lax.axis_index("col")
    tile_size = rows // tiles_ref.shape[0]

    @pl.when(step == 0)
    def _():
        period = quarter_period(index_ref[0])

        def write_col(at, amount, re, im):
            col_tab[at : at + amount, :HALF] = re
            col_tab[at : at + amount, HALF:] = im

        table_focal_lanes(write_col, period, col_at * cols, extent, cols, fine_ref)

        def write_row(part, at, re, im):
            row_tab[part : part + 64, at : at + 128] = re
            row_tab[HALF + part : HALF + part + 64, at : at + 128] = im

        table_pupil_lanes(write_row, period, row_at * rows, extent, rows, fine_ref, 0.0, HALF)

    halves = []
    for part in range(2):
        for h in range(block // tile_size):
            mask = live_row(tiles_ref, step * (block // tile_size) + h, cols).astype(BF16)
            halves.append(cot_ref[0, part, h * tile_size : (h + 1) * tile_size, :] * mask)
    prod = jnp.dot(jnp.concatenate(halves, axis=0), col_tab[...], preferred_element_type=F32)
    at = pl.ds(pl.multiple_of(step * block, block), block)
    inner[at, :M] = prod[:block].astype(BF16)
    inner[at, M:] = prod[block:].astype(BF16)

    @pl.when(step == pl.num_programs(0) - 1)
    def _():
        charge = charge_ref[0]
        even = jnp.where(charge % 2 == 0, 1.0, 0.0).astype(F32)
        odd = 1.0 - even
        scale = 4.0 / (extent * M)
        chunk = 64
        shape = (chunk, HALF)
        for ub in range(HALF // chunk):
            q_c = jnp.dot(row_tab[ub * chunk : (ub + 1) * chunk, :], inner[...], preferred_element_type=F32)
            q_s = jnp.dot(
                row_tab[HALF + ub * chunk : HALF + (ub + 1) * chunk, :], inner[...], preferred_element_type=F32
            )
            u = 2.0 * (iota(shape, 0) + float(ub * chunk)) + 1.0
            v = 2.0 * iota(shape, 1) + 1.0
            inv = 1.0 / jnp.sqrt(u * u + v * v)
            power = (u * inv, v * inv)
            total = (jnp.full(shape, scale, F32), jnp.zeros(shape, F32))
            for bit in range(4):
                taken = (charge >> bit) % 2 == 1
                multiplied = turn(total, power)
                total = tuple(jnp.where(taken, new, old) for new, old in zip(multiplied, total))
                power = turn(power, power)
            c, s = total
            ce, se, co, so = c * even, s * even, c * odd, s * odd
            ca, cb, cc, cd = (q_c[:, k * HALF : (k + 1) * HALF] for k in range(4))
            sa, sb, sc, sd = (q_s[:, k * HALF : (k + 1) * HALF] for k in range(4))
            t_ee = ce * ca - se * sd + so * cb - co * sc
            t_eo = ce * cb + se * sc - so * ca - co * sd
            t_oe = ce * sa + se * cd + co * cc + so * sb
            t_oo = ce * sb - se * cc + co * cd - so * sa
            per = t_ref.shape[1]
            for j in range(chunk // per if per < chunk else 1):
                span = min(per, chunk)
                rows_j = slice(j * span, (j + 1) * span)
                first = ub * chunk + j * span
                to = slice(first % per, first % per + span)
                t_ref[first // per, to, :HALF] = t_ee[rows_j]
                t_ref[first // per, to, HALF:] = t_eo[rows_j]
                first += HALF
                to = slice(first % per, first % per + span)
                t_ref[first // per, to, :HALF] = t_oe[rows_j]
                t_ref[first // per, to, HALF:] = t_oo[rows_j]
        for out, (ky, slots) in zip(outs, groups):
            for k, kz in enumerate(slots):
                source = lax.rem(col_at + ky, n_col) * n_row + lax.rem(row_at + kz, n_row)
                out[k] = t_ref[source].astype(BF16)


def forward(index, charge, tiles, cotangent, n_row, n_col, groups):
    rows, cols = cotangent.shape[2:]
    block = min(256, rows)
    per = M // (n_row * n_col)
    out_shape = [jax.ShapeDtypeStruct((len(slots), per, M), BF16) for _, slots in groups]
    out_specs = [pl.BlockSpec((len(slots), per, M), lambda i: (0, 0, 0)) for _, slots in groups]
    out_shape.append(jax.ShapeDtypeStruct((cols, M), BF16))
    out_specs.append(pl.BlockSpec((cols, M), lambda i: (0, 0), pipeline_mode=pl.Buffered(1)))

    def kernel(*refs):
        forward_kernel(*refs, rows=rows, cols=cols, n_row=n_row, n_col=n_col, groups=groups)

    smem = pl.BlockSpec(memory_space=pltpu.SMEM)
    outs = pl.pallas_call(
        kernel,
        grid=(rows // block,),
        in_specs=[smem, smem, smem, pl.BlockSpec((1, 2, block, cols), lambda i: (0, 0, i, 0))],
        out_specs=out_specs,
        out_shape=out_shape,
        scratch_shapes=[
            pltpu.VMEM((M, rows), BF16),
            pltpu.VMEM((rows, 2 * M), BF16),
            pltpu.VMEM((2, HALF, HALF), F32),
            pltpu.VMEM((n_row * n_col, per, M), F32),
        ],
        compiler_params=pltpu.CompilerParams(vmem_limit_bytes=58 << 20),
        cost_estimate=pl.CostEstimate(
            flops=2 * rows * 2 * M * (cols + M), bytes_accessed=4 * rows * cols, transcendentals=0
        ),
        name="forward",
    )(index, charge, tiles, cotangent)
    return outs[:-1], outs[-1]


def shift(value, axis, amount):
    size = lax.axis_size(axis)
    return lax.ppermute(value, axis, [(i, (i + amount) % size) for i in range(size)])


def swap(value, axis, bit):
    size = lax.axis_size(axis)
    return lax.ppermute(value, axis, [(i, i ^ bit) for i in range(size)])


def add_up(parts):
    total = parts[0].astype(F32)
    for part in parts[1:]:
        total = total + part.astype(F32)
    return total


def slot_groups(n_row, n_col):
    order = list(range(1, n_row)) + [0]
    cut = (n_row + 1) // 2
    halves = [order[:cut], order[cut:]] if n_row > 1 else [order]
    return [(ky, tuple(slots)) for ky in range(n_col) for slots in halves]


def reduce_and_gather(parts, groups, n_row, n_col):
    reduced = {}
    for own, (ky, slots) in zip(parts, groups):
        if ky:
            continue
        terms = [own]
        for other, (step, other_slots) in zip(parts, groups):
            if step and other_slots == slots:
                terms.append(shift(other, "col", step))
        total = add_up(terms).astype(BF16)
        for k, kz in enumerate(slots):
            reduced[kz] = total[k]
    moved = [shift(reduced[kz], "row", kz) for kz in range(1, n_row)]
    mine = add_up([reduced[0]] + moved).astype(BF16)
    rest = [shift(mine, "row", kz) for kz in range(1, n_row)]
    here = [mine] + ([jnp.concatenate(rest, axis=0)] if rest else [])
    out = list(here)
    for ky in range(1, n_col):
        out += [shift(piece, "col", ky) for piece in here]
    return out


def row_table_kernel(index_ref, row_tab, fine_ref, *, rows, n_row, n_col, full_rows, waves):
    extent = full_rows * n_row
    row_at = lax.axis_index("row")
    col_at = lax.axis_index("col")
    half_at = lax.rem(lax.axis_index("wl"), 2)
    per = M // (n_row * n_col)
    lane = lax.broadcasted_iota(jnp.int32, (16, M), 1)
    block = lane // per
    from_col = block // n_row
    from_row = block % n_row
    owner = ((col_at - from_col + n_col) % n_col) * n_row + (row_at - from_row + n_row) % n_row
    place = owner * per + lane % per
    is_sin = place >= HALF
    focal = 2.0 * jnp.where(is_sin, place - HALF, place).astype(F32) + 1.0
    for w in range(waves):
        period = quarter_period(index_ref[w])
        for side in range(2):
            lanes = slice(side * HALF, (side + 1) * HALF)
            sine = is_sin[:1, lanes]

            def write_row(at, amount, re, im, w=w, lanes=lanes, sine=sine):
                row_tab[w, at : at + amount, lanes] = jnp.where(
                    sine, im.astype(F32), re.astype(F32)
                ).astype(BF16)

            table_focal_lanes(
                write_row,
                period,
                row_at * full_rows + half_at * rows,
                extent,
                row_tab.shape[1],
                fine_ref,
                lanes=focal[:, lanes],
            )


def row_tables(indices, rows, n_row, n_col, full_rows):
    waves = indices.shape[0]
    own_rows = max(rows, 256)

    def kernel(*refs):
        row_table_kernel(*refs, rows=rows, n_row=n_row, n_col=n_col, full_rows=full_rows, waves=waves)

    return pl.pallas_call(
        kernel,
        in_specs=[pl.BlockSpec(memory_space=pltpu.SMEM)],
        out_specs=pl.BlockSpec(memory_space=pltpu.VMEM),
        out_shape=jax.ShapeDtypeStruct((waves, own_rows, M), BF16),
        scratch_shapes=[pltpu.VMEM((2, HALF, HALF), F32)],
        compiler_params=pltpu.CompilerParams(vmem_limit_bytes=16 << 20),
        cost_estimate=pl.CostEstimate(flops=40 * M * own_rows, bytes_accessed=4 * M * own_rows, transcendentals=0),
        name="row_tables",
    )(indices)


def backward_kernel(tiles_ref, *refs, count, starts, waves, chunks, tile_size, rows):
    sources = refs[:count]
    rest = refs[count:]
    row_tab, col_tabs, incidents = rest[0], rest[1 : 1 + waves], rest[1 + waves : 1 + 2 * waves]
    outs = rest[1 + 2 * waves : 1 + 2 * waves + len(chunks)]
    rest = rest[1 + 2 * waves + len(chunks) :]
    if starts:
        t_ref, held, sems = rest
    else:
        t_ref = sources[0]
        held, sems = rest
    half_at = lax.rem(lax.axis_index("wl"), 2)
    first = chunks[0][0]
    copies = []
    for k, (at, amount) in enumerate(chunks):
        for w in range(waves):
            source = incidents[w].at[0, pl.ds(pl.multiple_of(half_at * rows + at, amount), amount), :]
            copy = pltpu.make_async_copy(source, held.at[w, pl.ds(at - first, amount), :], sems.at[k, w])
            copy.start()
            copies.append(copy)
    for w in range(waves):
        for k, begin in enumerate(starts):
            piece = sources[w * len(starts) + k]
            t_ref[w, begin : begin + piece.shape[0], :] = piece[...]
    cols = outs[0].shape[1]
    wide = min(512, cols)
    for k, (at, amount) in enumerate(chunks):
        back_y = [
            jnp.dot(row_tab[w, at : at + amount, :], t_ref[w], preferred_element_type=F32).astype(BF16)
            for w in range(waves)
        ]
        mask = live_row(tiles_ref, (half_at * rows + at) // tile_size, cols)
        for w in range(waves):
            copies[k * waves + w].wait()
        for part in range(0, cols, wide):
            span = slice(part, part + wide)
            total = None
            for w in range(waves):
                back = lax.dot_general(
                    back_y[w], col_tabs[w][span, :], (((1,), (1,)), ((), ())), preferred_element_type=F32
                )
                term = back * held[w, at - first : at - first + amount, span].astype(F32)
                total = term if total is None else total + term
            outs[k][:, span] = (total * mask[:, span]).astype(BF16)


def backward(tiles, matrix, row_tab, col_tabs, incidents, chunks, tile_size):
    rows, cols = incidents[0].shape[1] // 2, incidents[0].shape[2]
    waves = len(col_tabs)
    assembled = not isinstance(matrix, list)
    starts = []
    if assembled:
        flat = [matrix]
    else:
        at = 0
        for piece in matrix[0]:
            starts.append(at)
            at += piece.shape[0]
        flat = [piece for wave in matrix for piece in wave]
    amount = sum(n for _, n in chunks)

    def kernel(*refs):
        backward_kernel(
            *refs, count=len(flat), starts=starts, waves=waves, chunks=chunks, tile_size=tile_size, rows=rows
        )

    vmem = pl.BlockSpec(memory_space=pltpu.VMEM)
    hbm = pl.BlockSpec(memory_space=pl.ANY)
    out_shape = [jax.ShapeDtypeStruct((n, cols), BF16) for _, n in chunks]
    if not assembled:
        out_shape.append(jax.ShapeDtypeStruct((waves, M, M), BF16))
    outs = pl.pallas_call(
        kernel,
        in_specs=[pl.BlockSpec(memory_space=pltpu.SMEM)]
        + [vmem] * (len(flat) + 1 + waves)
        + [hbm] * waves,
        out_specs=[vmem] * len(out_shape),
        out_shape=out_shape,
        scratch_shapes=[
            pltpu.VMEM((waves, amount, cols), BF16),
            pltpu.SemaphoreType.DMA((len(chunks), waves)),
        ],
        compiler_params=pltpu.CompilerParams(vmem_limit_bytes=24 << 20),
        cost_estimate=pl.CostEstimate(
            flops=2 * waves * amount * M * (cols + M), bytes_accessed=6 * amount * cols, transcendentals=0
        ),
        name="backward_rest" if assembled else "backward_first",
    )(tiles, *flat, row_tab, *col_tabs, *incidents)
    return outs if assembled else (outs[:-1], outs[-1])


def place_kernel(*refs, chunks, rows, aliased):
    count = 2 * len(chunks)
    sources = refs[:count]
    out, sems = refs[-2:]
    half_at = lax.rem(lax.axis_index("wl"), 2)
    copies = []
    for k, (at, amount) in enumerate(chunks):
        for side in range(2):
            where = half_at if side == 0 else 1 - half_at
            target = out.at[pl.ds(pl.multiple_of(where * rows + at, amount), amount), :]
            copies.append(pltpu.make_async_copy(sources[2 * k + side], target, sems.at[k, side]))
    for copy in copies:
        copy.start()
    for copy in copies:
        copy.wait()


def place(done, chunks, rows, into=None):
    flat = [part for pair in done for part in pair]
    cols = flat[0].shape[1]
    operands = flat + ([into] if into is not None else [])

    def kernel(*refs):
        place_kernel(*refs, chunks=chunks, rows=rows, aliased=into is not None)

    hbm = pl.BlockSpec(memory_space=pl.ANY)
    return pl.pallas_call(
        kernel,
        in_specs=[hbm] * len(operands),
        out_specs=hbm,
        out_shape=jax.ShapeDtypeStruct((2 * rows, cols), BF16),
        scratch_shapes=[pltpu.SemaphoreType.DMA((len(chunks), 2))],
        input_output_aliases={len(flat): 0} if into is not None else {},
        compiler_params=pltpu.CompilerParams(vmem_limit_bytes=1 << 20),
        cost_estimate=pl.CostEstimate(flops=0, bytes_accessed=8 * len(flat), transcendentals=0),
        name="place",
    )(*operands)


def per_device(cotangent, incident, aperture_tiles, charge, wl_index):
    rows, cols = cotangent.shape[2:]
    n_row = lax.axis_size("row")
    n_col = lax.axis_size("col")
    n_wl = lax.axis_size("wl")
    tile_size = rows // aperture_tiles.shape[0]
    half = rows // 2

    groups = slot_groups(n_row, n_col)
    parts, col_tab = forward(wl_index, charge, aperture_tiles, cotangent, n_row, n_col, groups)
    indices = jnp.concatenate([wl_index, swap(wl_index, "wl", 1)])
    other_inc = swap(incident, "wl", 1)
    row_tab = row_tables(indices, half, n_row, n_col, rows)
    col_tabs = [col_tab, swap(col_tab, "wl", 1)]

    gathered = reduce_and_gather(parts, groups, n_row, n_col)
    partner = [swap(piece, "wl", 1) for piece in gathered]
    if any(piece.shape[0] % 16 for piece in gathered):
        gathered = [jnp.concatenate(gathered, axis=0)]
        partner = [jnp.concatenate(partner, axis=0)]

    unit = half // 8
    chunks = []
    at = 0
    for size in (2, 2, 2, 1, 1):
        chunks.append((at, size * unit))
        at += size * unit
    first, matrix = backward(
        aperture_tiles, [gathered, partner], row_tab, col_tabs, [incident, other_inc], chunks[:1], tile_size
    )
    rest = backward(aperture_tiles, matrix, row_tab, col_tabs, [incident, other_inc], chunks[1:], tile_size)
    done = []
    for pair in list(first) + list(rest):
        bit = 2
        while bit < n_wl:
            pair = add_up([pair, swap(pair, "wl", bit)]).astype(BF16)
            bit *= 2
        done.append((pair, swap(pair, "wl", 1)))
    result = place(done[:-1], chunks[:-1], half)
    return place(done[-1:], chunks[-1:], half, result)


def solution(mesh):
    return jax.shard_map(
        per_device,
        mesh=mesh,
        in_specs=(
            P("wl", None, "row", "col"),
            P("wl", "row", "col"),
            P("row", "col"),
            P("wl"),
            P("wl"),
        ),
        out_specs=P("row", "col"),
        check_vma=False,
    )
```

```python
import math

import jax
import jax.numpy as jnp
from jax import lax
from jax.experimental import pallas as pl
from jax.experimental.pallas import tpu as pltpu
from jax.sharding import PartitionSpec as P


M = 512
HALF = M // 2
F32 = jnp.float32
BF16 = jnp.bfloat16


def iota(shape, axis):
    return lax.broadcasted_iota(jnp.int32, shape, axis).astype(F32)


def unit_phasor(product, period):
    turns = jnp.floor(product / period + 0.5)
    rest = product - turns * period
    quarter = jnp.floor(4.0 * rest / period + 0.5)
    theta = (4.0 * rest - quarter * period) / period * (0.5 * math.pi)
    sq = theta * theta
    sin_p = theta * (
        1.0 + sq * (-1.0 / 6.0 + sq * (1.0 / 120.0 + sq * (-1.0 / 5040.0 + sq / 362880.0)))
    )
    cos_p = 1.0 + sq * (
        -0.5 + sq * (1.0 / 24.0 + sq * (-1.0 / 720.0 + sq * (1.0 / 40320.0 - sq / 3628800.0)))
    )
    size = jnp.abs(quarter)
    odd = size == 1.0
    flip = jnp.where(size == 2.0, -1.0, 1.0)
    side = jnp.where(quarter < 0.0, -1.0, 1.0)
    cosine = jnp.where(odd, -side * sin_p, flip * cos_p)
    sine = jnp.where(odd, side * cos_p, flip * sin_p)
    return cosine, sine


def turn(first, second):
    c1, s1 = first
    c2, s2 = second
    return c1 * c2 - s1 * s2, s1 * c2 + c1 * s2


def quarter_period(index_value):
    return ((index_value + 32) * (M // 4)).astype(F32)


def table_focal_lanes(write, period, first, extent, amount, fine_ref, lanes=None, lane_count=HALF):
    block = 256
    focal = 2.0 * iota((16, lane_count), 1) + 1.0 if lanes is None else lanes
    step = iota((16, lane_count), 0)
    fine = unit_phasor(2.0 * step * focal, jnp.full((16, lane_count), period, F32))
    mid = unit_phasor(32.0 * step * focal, jnp.full((16, lane_count), period, F32))
    for b in range(16):
        re, im = turn((mid[0][b : b + 1], mid[1][b : b + 1]), fine)
        fine_ref[0, 16 * b : 16 * b + 16, :] = re
        fine_ref[1, 16 * b : 16 * b + 16, :] = im
    count = amount // block
    start = (2 * first - extent + 1).astype(F32)
    top = -(-count // 8) * 8
    focal_top = 2.0 * iota((top, lane_count), 1) + 1.0 if lanes is None else jnp.broadcast_to(lanes[:1], (top, lane_count))
    coarse = unit_phasor(
        (start + 2.0 * block * iota((top, lane_count), 0)) * focal_top,
        jnp.full((top, lane_count), period, F32),
    )
    for a in range(count):
        for part in range(0, block, 64):
            re, im = turn(
                (coarse[0][a : a + 1], coarse[1][a : a + 1]),
                (fine_ref[0, part : part + 64, :], fine_ref[1, part : part + 64, :]),
            )
            write(a * block + part, 64, re.astype(BF16), im.astype(BF16))


def table_pupil_lanes(write, period, first, extent, amount, fine_ref, focal_first, focal_count):
    count = amount // 128
    shape = (focal_count, 128)
    focal = 2.0 * (focal_first + iota(shape, 0)) + 1.0
    lane = iota(shape, 1)
    full = jnp.full(shape, period, F32)
    fine = unit_phasor(2.0 * lane * focal, full)
    fine_ref[0, :focal_count, :128] = fine[0]
    fine_ref[1, :focal_count, :128] = fine[1]
    start = (2 * first - extent + 1).astype(F32)
    coarse = unit_phasor((start + 256.0 * lane) * focal, full)
    fine_ref[0, :focal_count, 128:] = coarse[0]
    fine_ref[1, :focal_count, 128:] = coarse[1]
    for a in range(count):
        for part in range(0, focal_count, 64):
            rows = slice(part, min(part + 64, focal_count))
            re, im = turn(
                (fine_ref[0, rows, 128 + a : 129 + a], fine_ref[1, rows, 128 + a : 129 + a]),
                (fine_ref[0, rows, :128], fine_ref[1, rows, :128]),
            )
            write(part, a * 128, re.astype(BF16), im.astype(BF16))


def live_row(tiles_ref, tile_row, cells):
    tile_cols = tiles_ref.shape[1]
    width = cells // tile_cols
    parts = [
        jnp.full((1, width), jnp.where(tiles_ref[tile_row, j] == 1, 1.0, 0.0), F32)
        for j in range(tile_cols)
    ]
    return jnp.concatenate(parts, axis=1)


def forward_kernel(index_ref, charge_ref, tiles_ref, cot_ref, *refs, rows, cols, n_row, groups):
    outs, col_tab = refs[:-7], refs[-7]
    row_tab, inner, fine_ref, t_ref, held, sems = refs[-6:]
    block = min(256, rows)
    extent = rows * n_row
    row_at = lax.axis_index("row")
    col_at = lax.axis_index("col")
    tile_size = rows // tiles_ref.shape[0]
    copies = []
    for step in range(rows // block):
        span = pl.ds(step * block, block)
        copies.append(pltpu.make_async_copy(cot_ref.at[0, :, span, :], held.at[:, span, :], sems.at[step]))
        copies[-1].start()
    period = quarter_period(index_ref[0])

    def write_col(at, amount, re, im):
        col_tab[at : at + amount, :HALF] = re
        col_tab[at : at + amount, HALF:] = im

    table_focal_lanes(write_col, period, col_at * cols, extent, cols, fine_ref)

    def write_row(part, at, re, im):
        row_tab[part : part + 64, at : at + 128] = re
        row_tab[HALF + part : HALF + part + 64, at : at + 128] = im

    table_pupil_lanes(write_row, period, row_at * rows, extent, rows, fine_ref, 0.0, HALF)

    for step in range(rows // block):
        copies[step].wait()
        halves = []
        for part in range(2):
            for at in range(step * block, (step + 1) * block, tile_size):
                mask = live_row(tiles_ref, at // tile_size, cols).astype(BF16)
                halves.append(held[part, at : at + tile_size, :] * mask)
        prod = jnp.dot(jnp.concatenate(halves, axis=0), col_tab[...], preferred_element_type=F32)
        at = step * block
        inner[at : at + block, :M] = prod[:block].astype(BF16)
        inner[at : at + block, M:] = prod[block:].astype(BF16)

    charge = charge_ref[0]
    even = jnp.where(charge % 2 == 0, 1.0, 0.0).astype(F32)
    odd = 1.0 - even
    scale = 4.0 / (extent * M)
    chunk = 128
    shape = (chunk, HALF)
    for ub in range(HALF // chunk):
        both = jnp.concatenate(
            [row_tab[ub * chunk : (ub + 1) * chunk, :], row_tab[HALF + ub * chunk : HALF + (ub + 1) * chunk, :]],
            axis=0,
        )
        q = jnp.dot(both, inner[...], preferred_element_type=F32)
        q_c, q_s = q[:chunk], q[chunk:]
        u = 2.0 * (iota(shape, 0) + float(ub * chunk)) + 1.0
        v = 2.0 * iota(shape, 1) + 1.0
        inv = 1.0 / jnp.sqrt(u * u + v * v)
        power = (u * inv, v * inv)
        total = (jnp.full(shape, scale, F32), jnp.zeros(shape, F32))
        for bit in range(4):
            taken = (charge >> bit) % 2 == 1
            multiplied = turn(total, power)
            total = tuple(jnp.where(taken, new, old) for new, old in zip(multiplied, total))
            power = turn(power, power)
        c, s = total
        ce, se, co, so = c * even, s * even, c * odd, s * odd
        ca, cb, cc, cd = (q_c[:, k * HALF : (k + 1) * HALF] for k in range(4))
        sa, sb, sc, sd = (q_s[:, k * HALF : (k + 1) * HALF] for k in range(4))
        t_ee = ce * ca - se * sd + so * cb - co * sc
        t_eo = ce * cb + se * sc - so * ca - co * sd
        t_oe = ce * sa + se * cd + co * cc + so * sb
        t_oo = ce * sb - se * cc + co * cd - so * sa
        per = t_ref.shape[1]
        span = min(per, chunk)
        for j in range(chunk // span):
            rows_j = slice(j * span, (j + 1) * span)
            for first, left, right in (
                (ub * chunk + j * span, t_ee, t_eo),
                (HALF + ub * chunk + j * span, t_oe, t_oo),
            ):
                to = slice(first % per, first % per + span)
                t_ref[first // per, to, :HALF] = left[rows_j]
                t_ref[first // per, to, HALF:] = right[rows_j]
    for out, (ky, slots) in zip(outs, groups):
        for k, kz in enumerate(slots):
            source = (col_at ^ ky) * n_row + (row_at ^ kz)
            out[k] = t_ref[source].astype(BF16)


def forward(index, charge, tiles, cotangent, n_row, n_col, groups):
    rows, cols = cotangent.shape[2:]
    block = min(256, rows)
    per = M // (n_row * n_col)
    out_shape = [jax.ShapeDtypeStruct((len(slots), per, M), BF16) for _, slots in groups]
    out_shape.append(jax.ShapeDtypeStruct((cols, M), BF16))

    def kernel(*refs):
        forward_kernel(*refs, rows=rows, cols=cols, n_row=n_row, groups=groups)

    smem = pl.BlockSpec(memory_space=pltpu.SMEM)
    outs = pl.pallas_call(
        kernel,
        in_specs=[smem, smem, smem, pl.BlockSpec(memory_space=pltpu.HBM)],
        out_specs=[pl.BlockSpec(memory_space=pltpu.VMEM)] * len(out_shape),
        out_shape=out_shape,
        scratch_shapes=[
            pltpu.VMEM((M, rows), BF16),
            pltpu.VMEM((rows, 2 * M), BF16),
            pltpu.VMEM((2, HALF, HALF), F32),
            pltpu.VMEM((n_row * n_col, per, M), F32),
            pltpu.VMEM((2, rows, cols), BF16),
            pltpu.SemaphoreType.DMA((rows // block,)),
        ],
        compiler_params=pltpu.CompilerParams(vmem_limit_bytes=55 << 20),
        cost_estimate=pl.CostEstimate(
            flops=2 * rows * 2 * M * (cols + M), bytes_accessed=4 * rows * cols, transcendentals=0
        ),
        name="forward",
    )(index, charge, tiles, cotangent)
    return outs[:-1], outs[-1]


def swap(value, axis, bits):
    size = lax.axis_size(axis)
    return lax.ppermute(value, axis, [(i, i ^ bits) for i in range(size)])


def add_up(parts):
    total = parts[0].astype(F32)
    for part in parts[1:]:
        total = total + part.astype(F32)
    return total


def hop_order(n_row):
    return sorted(range(1, n_row), key=lambda k: -(k & -k))


def slot_groups(n_row, n_col):
    order = hop_order(n_row) + [0]
    if n_row <= 4:
        parts = [[kz] for kz in order]
    else:
        parts = [order[: n_row // 2], order[n_row // 2 :]]
    return [(ky, tuple(slots)) for slots in parts for ky in range(n_col)]


def reduce_blocks(parts, groups, n_row):
    reduced = {}
    for own, (ky, slots) in zip(parts, groups):
        if ky:
            continue
        terms = [own]
        for other, (step, other_slots) in zip(parts, groups):
            if step and other_slots == slots:
                terms.append(swap(other, "col", step))
        total = add_up(terms).astype(BF16)
        for k, kz in enumerate(slots):
            reduced[kz] = total[k]
    moved = [swap(reduced[kz], "row", kz) for kz in hop_order(n_row)]
    return add_up([reduced[0]] + moved).astype(BF16)


def gather_row(mine, n_row):
    found = {0: mine}
    for kz in hop_order(n_row):
        found[kz] = swap(mine, "row", kz)
    return [found[kz] for kz in range(n_row)]


def aligned(pieces):
    if any(piece.shape[0] % 16 for piece in pieces):
        return [jnp.concatenate(pieces, axis=0)]
    return pieces


def row_table_kernel(index_ref, row_tab, fine_ref, *, rows, n_row, n_col, full_rows, waves):
    extent = full_rows * n_row
    row_at = lax.axis_index("row")
    col_at = lax.axis_index("col")
    half_at = lax.rem(lax.axis_index("wl"), 2)
    per = M // (n_row * n_col)
    lane = lax.broadcasted_iota(jnp.int32, (16, M), 1)
    block = lane // per
    owner = ((block // n_row) ^ col_at) * n_row + ((block % n_row) ^ row_at)
    place = owner * per + lane % per
    is_sin = place >= HALF
    focal = 2.0 * jnp.where(is_sin, place - HALF, place).astype(F32) + 1.0
    for w in range(waves):
        period = quarter_period(index_ref[w])
        for side in range(2):
            lanes = slice(side * HALF, (side + 1) * HALF)
            sine = is_sin[:1, lanes]

            def write_row(at, amount, re, im, w=w, lanes=lanes, sine=sine):
                row_tab[w, at : at + amount, lanes] = jnp.where(
                    sine, im.astype(F32), re.astype(F32)
                ).astype(BF16)

            table_focal_lanes(
                write_row,
                period,
                row_at * full_rows + half_at * rows,
                extent,
                row_tab.shape[1],
                fine_ref,
                lanes=focal[:, lanes],
            )


def row_tables(indices, rows, n_row, n_col, full_rows):
    waves = indices.shape[0]
    own_rows = max(rows, 256)

    def kernel(*refs):
        row_table_kernel(*refs, rows=rows, n_row=n_row, n_col=n_col, full_rows=full_rows, waves=waves)

    return pl.pallas_call(
        kernel,
        in_specs=[pl.BlockSpec(memory_space=pltpu.SMEM)],
        out_specs=pl.BlockSpec(memory_space=pltpu.VMEM),
        out_shape=jax.ShapeDtypeStruct((waves, own_rows, M), BF16),
        scratch_shapes=[pltpu.VMEM((2, HALF, HALF), F32)],
        compiler_params=pltpu.CompilerParams(vmem_limit_bytes=16 << 20),
        cost_estimate=pl.CostEstimate(flops=40 * M * own_rows, bytes_accessed=4 * M * own_rows, transcendentals=0),
        name="row_tables",
    )(indices)


def col_table(index, cols, n_col):
    def kernel(index_ref, col_tab, fine_ref):
        def write_col(at, amount, re, im):
            col_tab[at : at + amount, :HALF] = re
            col_tab[at : at + amount, HALF:] = im

        table_focal_lanes(
            write_col,
            quarter_period(index_ref[0]),
            lax.axis_index("col") * cols,
            cols * n_col,
            cols,
            fine_ref,
        )

    return pl.pallas_call(
        kernel,
        in_specs=[pl.BlockSpec(memory_space=pltpu.SMEM)],
        out_specs=pl.BlockSpec(memory_space=pltpu.VMEM),
        out_shape=jax.ShapeDtypeStruct((cols, M), BF16),
        scratch_shapes=[pltpu.VMEM((2, HALF, HALF), F32)],
        compiler_params=pltpu.CompilerParams(vmem_limit_bytes=16 << 20),
        cost_estimate=pl.CostEstimate(flops=20 * M * cols, bytes_accessed=4 * M * cols, transcendentals=0),
        name="col_table",
    )(index)


def backward_kernel(tiles_ref, *refs, counts, wave_ids, part_first, chunks, tile_size, rows):
    waves = len(counts)
    total_pieces = sum(counts)
    sources, refs = refs[:total_pieces], refs[total_pieces:]
    row_tab, refs = refs[0], refs[1:]
    col_tabs, refs = refs[:waves], refs[waves:]
    incidents, refs = refs[:waves], refs[waves:]
    outs, refs = refs[: len(chunks)], refs[len(chunks) :]
    matrices, (held, sems) = list(refs[:-2]), refs[-2:]
    half_at = lax.rem(lax.axis_index("wl"), 2)
    first = chunks[0][0]
    copies = []
    for k, (at, amount) in enumerate(chunks):
        for w in range(waves):
            if part_first[w] is None:
                span = pl.ds(pl.multiple_of(half_at * rows + at, amount), amount)
                source = incidents[w].at[0, span, :]
            else:
                source = incidents[w].at[pl.ds(at - part_first[w], amount), :]
            copies.append(
                pltpu.make_async_copy(source, held.at[w, pl.ds(at - first, amount), :], sems.at[k, w])
            )
            copies[-1].start()
    ready = []
    for w in range(waves):
        pieces, sources = sources[: counts[w]], sources[counts[w] :]
        if counts[w] == 1:
            ready.append(pieces[0])
            continue
        target = matrices.pop(0)
        at = 0
        for piece in pieces:
            target[at : at + piece.shape[0], :] = piece[...]
            at += piece.shape[0]
        ready.append(target)
    cols = outs[0].shape[1]
    wide = min(512, cols)
    for k, (at, amount) in enumerate(chunks):
        back_y = [
            jnp.dot(row_tab[wave_ids[w], at : at + amount, :], ready[w][...], preferred_element_type=F32).astype(BF16)
            for w in range(waves)
        ]
        masks = [live_row(tiles_ref, (half_at * rows + at + h) // tile_size, cols) for h in range(0, amount, tile_size)]
        for w in range(waves):
            copies[k * waves + w].wait()
        for part in range(0, cols, wide):
            span = slice(part, part + wide)
            total = None
            for w in range(waves):
                back = lax.dot_general(
                    back_y[w], col_tabs[w][span, :], (((1,), (1,)), ((), ())), preferred_element_type=F32
                )
                term = back * held[w, at - first : at - first + amount, span].astype(F32)
                total = term if total is None else total + term
            for h, mask in enumerate(masks):
                some = slice(h * tile_size, min((h + 1) * tile_size, amount))
                outs[k][some, span] = (total[some] * mask[:, span]).astype(BF16)


def backward(tiles, waves, row_tab, chunks, tile_size, rows):
    cols = tiles.shape[1] * tile_size
    flat = [piece for wave in waves for piece in wave[0]]
    amount = sum(n for _, n in chunks)
    counts = [len(wave[0]) for wave in waves]
    emit = sum(count > 1 for count in counts)

    def kernel(*refs):
        backward_kernel(
            *refs,
            counts=counts,
            wave_ids=[wave[1] for wave in waves],
            part_first=[wave[4] for wave in waves],
            chunks=chunks,
            tile_size=tile_size,
            rows=rows,
        )

    vmem = pl.BlockSpec(memory_space=pltpu.VMEM)
    hbm = pl.BlockSpec(memory_space=pl.ANY)
    out_shape = [jax.ShapeDtypeStruct((n, cols), BF16) for _, n in chunks]
    out_shape += [jax.ShapeDtypeStruct((M, M), BF16)] * emit
    outs = pl.pallas_call(
        kernel,
        in_specs=[pl.BlockSpec(memory_space=pltpu.SMEM)]
        + [vmem] * (len(flat) + 1 + len(waves))
        + [hbm] * len(waves),
        out_specs=[vmem] * len(out_shape),
        out_shape=out_shape,
        scratch_shapes=[
            pltpu.VMEM((len(waves), amount, cols), BF16),
            pltpu.SemaphoreType.DMA((len(chunks), len(waves))),
        ],
        compiler_params=pltpu.CompilerParams(vmem_limit_bytes=24 << 20),
        cost_estimate=pl.CostEstimate(
            flops=2 * len(waves) * amount * M * (cols + M), bytes_accessed=6 * amount * cols, transcendentals=0
        ),
    )(tiles, *flat, row_tab, *[wave[2] for wave in waves], *[wave[3] for wave in waves])
    return outs[: len(chunks)], outs[len(chunks) :]


def place_kernel(*refs, chunks, rows):
    sources = refs[: 2 * len(chunks)]
    out, sems = refs[-2:]
    half_at = lax.rem(lax.axis_index("wl"), 2)
    copies = []
    for k, (at, amount) in enumerate(chunks):
        for side in range(2):
            where = half_at if side == 0 else 1 - half_at
            target = out.at[pl.ds(pl.multiple_of(where * rows + at, amount), amount), :]
            copies.append(pltpu.make_async_copy(sources[2 * k + side], target, sems.at[k, side]))
    for copy in copies:
        copy.start()
    for copy in copies:
        copy.wait()


def place(done, chunks, rows, into=None):
    flat = [part for pair in done for part in pair]
    cols = flat[0].shape[1]
    operands = flat + ([into] if into is not None else [])

    def kernel(*refs):
        place_kernel(*refs, chunks=chunks, rows=rows)

    hbm = pl.BlockSpec(memory_space=pl.ANY)
    return pl.pallas_call(
        kernel,
        in_specs=[hbm] * len(operands),
        out_specs=hbm,
        out_shape=jax.ShapeDtypeStruct((2 * rows, cols), BF16),
        scratch_shapes=[pltpu.SemaphoreType.DMA((len(chunks), 2))],
        input_output_aliases={len(flat): 0} if into is not None else {},
        compiler_params=pltpu.CompilerParams(vmem_limit_bytes=1 << 20),
        cost_estimate=pl.CostEstimate(flops=0, bytes_accessed=4 * cols * sum(n for _, n in chunks), transcendentals=0),
    )(*operands)


EXCHANGED = (2, 1, 1)
REPEATED = (2, 2)


def all_steps(cotangent, incident, tiles, charge, wl_index):
    rows, cols = cotangent.shape[2:]
    n_row = lax.axis_size("row")
    n_col = lax.axis_size("col")
    tile_size = rows // tiles.shape[0]
    half = rows // 2
    core = lax.axis_index("wl") % 2
    unit = half // 8
    chunks = []
    at = 0
    for size in EXCHANGED + REPEATED:
        chunks.append((at, size * unit))
        at += size * unit
    n_first = len(EXCHANGED)
    split = chunks[n_first][0]

    def rows_for(which):
        return lax.dynamic_slice_in_dim(incident[0], which * half + split, half - split, 0)

    inc_straight = swap(rows_for(core), "wl", 2)
    inc_core = swap(incident, "wl", 1)
    groups = slot_groups(n_row, n_col)
    parts, col_own = forward(wl_index, charge, tiles, cotangent, n_row, n_col, groups)
    mine = reduce_blocks(parts, groups, n_row)
    inc_cross = swap(rows_for(1 - core), "wl", 3)
    col_core = swap(col_own, "wl", 1)
    indices = jnp.concatenate([wl_index, swap(wl_index, "wl", 2)])
    indices = jnp.concatenate([indices, swap(indices, "wl", 1)])
    row_tab = row_tables(indices, half, n_row, n_col, rows)
    col_straight = col_table(indices[1:2], cols, n_col)
    col_cross = swap(col_straight, "wl", 1)

    here = gather_row(mine, n_row)
    if n_row > 4:
        here = [jnp.concatenate(here, axis=0)]
    joined = jnp.concatenate(here, axis=0)
    pieces, pieces_core = [joined], [swap(joined, "wl", 1)]
    for ky in range(1, n_col):
        for piece in here:
            pieces.append(swap(piece, "col", ky))
            pieces_core.append(swap(pieces[-1], "wl", 1))

    far = swap(mine, "wl", 2)
    far = jnp.concatenate(gather_row(far, n_row), axis=0)
    far = jnp.concatenate([far] + [swap(far, "col", ky) for ky in range(1, n_col)], axis=0)
    far_core = swap(far, "wl", 1)

    own = (aligned(pieces), 0, col_own, incident, None)
    mate = (aligned(pieces_core), 2, col_core, inc_core, None)
    first, matrices = backward(tiles, [own, mate], row_tab, chunks[:1], tile_size, half)
    if len(matrices) == 2:
        own = ([matrices[0]],) + own[1:]
        mate = ([matrices[1]],) + mate[1:]
    second, _ = backward(tiles, [own, mate], row_tab, chunks[1:n_first], tile_size, half)
    straight = ([far], 1, col_straight, inc_straight, split)
    cross = ([far_core], 3, col_cross, inc_cross, split)
    both, _ = backward(tiles, [own, mate, straight, cross], row_tab, chunks[n_first:], tile_size, half)
    done = []
    for pair in list(first) + list(second):
        total = add_up([pair, swap(pair, "wl", 2)]).astype(BF16)
        done.append((total, swap(total, "wl", 1)))
    ready = [(part, swap(part, "wl", 1)) for part in both]
    result = place(ready, chunks[n_first:], half)
    result = place(done[:-1], chunks[: n_first - 1], half, result)
    return place(done[-1:], chunks[n_first - 1 : n_first], half, result)


def solution(mesh):
    return jax.shard_map(
        all_steps,
        mesh=mesh,
        in_specs=(
            P("wl", None, "row", "col"),
            P("wl", "row", "col"),
            P("row", "col"),
            P("wl"),
            P("wl"),
        ),
        out_specs=P("row", "col"),
        check_vma=False,
    )
```

```python
import math

import jax
import jax.numpy as jnp
from jax import lax
from jax.experimental import pallas as pl
from jax.experimental.pallas import tpu as pltpu
from jax.sharding import PartitionSpec as P


M = 512
HALF = M // 2
F32 = jnp.float32
BF16 = jnp.bfloat16


def iota(shape, axis):
    return lax.broadcasted_iota(jnp.int32, shape, axis).astype(F32)


def unit_phasor(product, period):
    turns = jnp.floor(product / period + 0.5)
    rest = product - turns * period
    quarter = jnp.floor(4.0 * rest / period + 0.5)
    theta = (4.0 * rest - quarter * period) / period * (0.5 * math.pi)
    sq = theta * theta
    sin_p = theta * (
        1.0 + sq * (-1.0 / 6.0 + sq * (1.0 / 120.0 + sq * (-1.0 / 5040.0 + sq / 362880.0)))
    )
    cos_p = 1.0 + sq * (
        -0.5 + sq * (1.0 / 24.0 + sq * (-1.0 / 720.0 + sq * (1.0 / 40320.0 - sq / 3628800.0)))
    )
    size = jnp.abs(quarter)
    odd = size == 1.0
    flip = jnp.where(size == 2.0, -1.0, 1.0)
    side = jnp.where(quarter < 0.0, -1.0, 1.0)
    cosine = jnp.where(odd, -side * sin_p, flip * cos_p)
    sine = jnp.where(odd, side * cos_p, flip * sin_p)
    return cosine, sine


def turn(first, second):
    c1, s1 = first
    c2, s2 = second
    return c1 * c2 - s1 * s2, s1 * c2 + c1 * s2


def quarter_period(index_value):
    return ((index_value + 32) * (M // 4)).astype(F32)


def table_focal_lanes(write, period, first, extent, amount, fine_ref, lanes=None, lane_count=HALF):
    block = 256
    focal = 2.0 * iota((16, lane_count), 1) + 1.0 if lanes is None else lanes
    step = iota((16, lane_count), 0)
    fine = unit_phasor(2.0 * step * focal, jnp.full((16, lane_count), period, F32))
    mid = unit_phasor(32.0 * step * focal, jnp.full((16, lane_count), period, F32))
    for b in range(16):
        re, im = turn((mid[0][b : b + 1], mid[1][b : b + 1]), fine)
        fine_ref[0, 16 * b : 16 * b + 16, :] = re
        fine_ref[1, 16 * b : 16 * b + 16, :] = im
    count = amount // block
    start = (2 * first - extent + 1).astype(F32)
    top = -(-count // 8) * 8
    focal_top = 2.0 * iota((top, lane_count), 1) + 1.0 if lanes is None else jnp.broadcast_to(lanes[:1], (top, lane_count))
    coarse = unit_phasor(
        (start + 2.0 * block * iota((top, lane_count), 0)) * focal_top,
        jnp.full((top, lane_count), period, F32),
    )
    for a in range(count):
        for part in range(0, block, 64):
            re, im = turn(
                (coarse[0][a : a + 1], coarse[1][a : a + 1]),
                (fine_ref[0, part : part + 64, :], fine_ref[1, part : part + 64, :]),
            )
            write(a * block + part, 64, re.astype(BF16), im.astype(BF16))


def table_pupil_lanes(write, period, first, extent, amount, fine_ref, focal_first, focal_count):
    count = amount // 128
    shape = (focal_count, 128)
    focal = 2.0 * (focal_first + iota(shape, 0)) + 1.0
    lane = iota(shape, 1)
    full = jnp.full(shape, period, F32)
    fine = unit_phasor(2.0 * lane * focal, full)
    fine_ref[0, :focal_count, :128] = fine[0]
    fine_ref[1, :focal_count, :128] = fine[1]
    start = (2 * first - extent + 1).astype(F32)
    coarse = unit_phasor((start + 256.0 * lane) * focal, full)
    fine_ref[0, :focal_count, 128:] = coarse[0]
    fine_ref[1, :focal_count, 128:] = coarse[1]
    for a in range(count):
        for part in range(0, focal_count, 64):
            rows = slice(part, min(part + 64, focal_count))
            re, im = turn(
                (fine_ref[0, rows, 128 + a : 129 + a], fine_ref[1, rows, 128 + a : 129 + a]),
                (fine_ref[0, rows, :128], fine_ref[1, rows, :128]),
            )
            write(part, a * 128, re.astype(BF16), im.astype(BF16))


def live_row(tiles_ref, tile_row, cells):
    tile_cols = tiles_ref.shape[1]
    width = cells // tile_cols
    parts = [
        jnp.full((1, width), jnp.where(tiles_ref[tile_row, j] == 1, 1.0, 0.0), F32)
        for j in range(tile_cols)
    ]
    return jnp.concatenate(parts, axis=1)


def forward_kernel(index_ref, charge_ref, tiles_ref, cot_ref, *refs, rows, cols, n_row, groups):
    outs, col_tab = refs[:-7], refs[-7]
    row_tab, inner, fine_ref, t_ref, held, sems = refs[-6:]
    block = min(256, rows)
    extent = rows * n_row
    row_at = lax.axis_index("row")
    col_at = lax.axis_index("col")
    tile_size = rows // tiles_ref.shape[0]
    copies = []
    for step in range(rows // block):
        span = pl.ds(step * block, block)
        copies.append(pltpu.make_async_copy(cot_ref.at[0, :, span, :], held.at[:, span, :], sems.at[step]))
        copies[-1].start()
    period = quarter_period(index_ref[0])

    def write_col(at, amount, re, im):
        col_tab[at : at + amount, :HALF] = re
        col_tab[at : at + amount, HALF:] = im

    table_focal_lanes(write_col, period, col_at * cols, extent, cols, fine_ref)

    def write_row(part, at, re, im):
        row_tab[part : part + 64, at : at + 128] = re
        row_tab[HALF + part : HALF + part + 64, at : at + 128] = im

    table_pupil_lanes(write_row, period, row_at * rows, extent, rows, fine_ref, 0.0, HALF)

    for step in range(rows // block):
        copies[step].wait()
        halves = []
        for part in range(2):
            for at in range(step * block, (step + 1) * block, tile_size):
                mask = live_row(tiles_ref, at // tile_size, cols).astype(BF16)
                halves.append(held[part, at : at + tile_size, :] * mask)
        prod = jnp.dot(jnp.concatenate(halves, axis=0), col_tab[...], preferred_element_type=F32)
        at = step * block
        inner[at : at + block, :M] = prod[:block].astype(BF16)
        inner[at : at + block, M:] = prod[block:].astype(BF16)

    charge = charge_ref[0]
    even = jnp.where(charge % 2 == 0, 1.0, 0.0).astype(F32)
    odd = 1.0 - even
    scale = 4.0 / (extent * M)
    chunk = 128
    shape = (chunk, HALF)
    for ub in range(HALF // chunk):
        both = jnp.concatenate(
            [row_tab[ub * chunk : (ub + 1) * chunk, :], row_tab[HALF + ub * chunk : HALF + (ub + 1) * chunk, :]],
            axis=0,
        )
        q = jnp.dot(both, inner[...], preferred_element_type=F32)
        q_c, q_s = q[:chunk], q[chunk:]
        u = 2.0 * (iota(shape, 0) + float(ub * chunk)) + 1.0
        v = 2.0 * iota(shape, 1) + 1.0
        inv = 1.0 / jnp.sqrt(u * u + v * v)
        power = (u * inv, v * inv)
        total = (jnp.full(shape, scale, F32), jnp.zeros(shape, F32))
        for bit in range(4):
            taken = (charge >> bit) % 2 == 1
            multiplied = turn(total, power)
            total = tuple(jnp.where(taken, new, old) for new, old in zip(multiplied, total))
            power = turn(power, power)
        c, s = total
        ce, se, co, so = c * even, s * even, c * odd, s * odd
        ca, cb, cc, cd = (q_c[:, k * HALF : (k + 1) * HALF] for k in range(4))
        sa, sb, sc, sd = (q_s[:, k * HALF : (k + 1) * HALF] for k in range(4))
        t_ee = ce * ca - se * sd + so * cb - co * sc
        t_eo = ce * cb + se * sc - so * ca - co * sd
        t_oe = ce * sa + se * cd + co * cc + so * sb
        t_oo = ce * sb - se * cc + co * cd - so * sa
        per = t_ref.shape[1]
        span = min(per, chunk)
        for j in range(chunk // span):
            rows_j = slice(j * span, (j + 1) * span)
            for first, left, right in (
                (ub * chunk + j * span, t_ee, t_eo),
                (HALF + ub * chunk + j * span, t_oe, t_oo),
            ):
                to = slice(first % per, first % per + span)
                t_ref[first // per, to, :HALF] = left[rows_j]
                t_ref[first // per, to, HALF:] = right[rows_j]
    for out, (ky, slots) in zip(outs, groups):
        for k, kz in enumerate(slots):
            source = (col_at ^ ky) * n_row + (row_at ^ kz)
            out[k] = t_ref[source].astype(BF16)


def forward(index, charge, tiles, cotangent, n_row, n_col, groups):
    rows, cols = cotangent.shape[2:]
    block = min(256, rows)
    per = M // (n_row * n_col)
    out_shape = [jax.ShapeDtypeStruct((len(slots), per, M), BF16) for _, slots in groups]
    out_shape.append(jax.ShapeDtypeStruct((cols, M), BF16))

    def kernel(*refs):
        forward_kernel(*refs, rows=rows, cols=cols, n_row=n_row, groups=groups)

    smem = pl.BlockSpec(memory_space=pltpu.SMEM)
    outs = pl.pallas_call(
        kernel,
        in_specs=[smem, smem, smem, pl.BlockSpec(memory_space=pltpu.HBM)],
        out_specs=[pl.BlockSpec(memory_space=pltpu.VMEM)] * len(out_shape),
        out_shape=out_shape,
        scratch_shapes=[
            pltpu.VMEM((M, rows), BF16),
            pltpu.VMEM((rows, 2 * M), BF16),
            pltpu.VMEM((2, HALF, HALF), F32),
            pltpu.VMEM((n_row * n_col, per, M), F32),
            pltpu.VMEM((2, rows, cols), BF16),
            pltpu.SemaphoreType.DMA((rows // block,)),
        ],
        compiler_params=pltpu.CompilerParams(vmem_limit_bytes=55 << 20),
        cost_estimate=pl.CostEstimate(
            flops=2 * rows * 2 * M * (cols + M), bytes_accessed=4 * rows * cols, transcendentals=0
        ),
        name="forward",
    )(index, charge, tiles, cotangent)
    return outs[:-1], outs[-1]


def swap(value, axis, bits):
    size = lax.axis_size(axis)
    return lax.ppermute(value, axis, [(i, i ^ bits) for i in range(size)])


def add_up(parts):
    total = parts[0].astype(F32)
    for part in parts[1:]:
        total = total + part.astype(F32)
    return total


def hop_order(n_row):
    return sorted(range(1, n_row), key=lambda k: -(k & -k))


def slot_groups(n_row, n_col):
    order = hop_order(n_row) + [0]
    if n_row <= 4:
        parts = [[kz] for kz in order]
    else:
        parts = [order[: n_row // 2], order[n_row // 2 :]]
    return [(ky, tuple(slots)) for slots in parts for ky in range(n_col)]


def reduce_blocks(parts, groups, n_row):
    reduced = {}
    for own, (ky, slots) in zip(parts, groups):
        if ky:
            continue
        terms = [own]
        for other, (step, other_slots) in zip(parts, groups):
            if step and other_slots == slots:
                terms.append(swap(other, "col", step))
        total = add_up(terms).astype(BF16)
        for k, kz in enumerate(slots):
            reduced[kz] = total[k]
    moved = [swap(reduced[kz], "row", kz) for kz in hop_order(n_row)]
    return add_up([reduced[0]] + moved).astype(BF16)


def gather_row(mine, n_row):
    found = {0: mine}
    for kz in hop_order(n_row):
        found[kz] = swap(mine, "row", kz)
    return [found[kz] for kz in range(n_row)]


def aligned(pieces):
    if any(piece.shape[0] % 16 for piece in pieces):
        return [jnp.concatenate(pieces, axis=0)]
    return pieces


def row_table_kernel(index_ref, row_tab, fine_ref, *, rows, n_row, n_col, full_rows, waves):
    extent = full_rows * n_row
    row_at = lax.axis_index("row")
    col_at = lax.axis_index("col")
    half_at = lax.rem(lax.axis_index("wl"), 2)
    per = M // (n_row * n_col)
    lane = lax.broadcasted_iota(jnp.int32, (16, M), 1)
    block = lane // per
    owner = ((block // n_row) ^ col_at) * n_row + ((block % n_row) ^ row_at)
    place = owner * per + lane % per
    is_sin = place >= HALF
    focal = 2.0 * jnp.where(is_sin, place - HALF, place).astype(F32) + 1.0
    for w in range(waves):
        period = quarter_period(index_ref[w])
        for side in range(2):
            lanes = slice(side * HALF, (side + 1) * HALF)
            sine = is_sin[:1, lanes]

            def write_row(at, amount, re, im, w=w, lanes=lanes, sine=sine):
                row_tab[w, at : at + amount, lanes] = jnp.where(
                    sine, im.astype(F32), re.astype(F32)
                ).astype(BF16)

            table_focal_lanes(
                write_row,
                period,
                row_at * full_rows + half_at * rows,
                extent,
                row_tab.shape[1],
                fine_ref,
                lanes=focal[:, lanes],
            )


def row_tables(indices, rows, n_row, n_col, full_rows):
    waves = indices.shape[0]
    own_rows = max(rows, 256)

    def kernel(*refs):
        row_table_kernel(*refs, rows=rows, n_row=n_row, n_col=n_col, full_rows=full_rows, waves=waves)

    return pl.pallas_call(
        kernel,
        in_specs=[pl.BlockSpec(memory_space=pltpu.SMEM)],
        out_specs=pl.BlockSpec(memory_space=pltpu.VMEM),
        out_shape=jax.ShapeDtypeStruct((waves, own_rows, M), BF16),
        scratch_shapes=[pltpu.VMEM((2, HALF, HALF), F32)],
        compiler_params=pltpu.CompilerParams(vmem_limit_bytes=16 << 20),
        cost_estimate=pl.CostEstimate(flops=40 * M * own_rows, bytes_accessed=4 * M * own_rows, transcendentals=0),
        name="row_tables",
    )(indices)


def col_table(index, cols, n_col):
    def kernel(index_ref, col_tab, fine_ref):
        def write_col(at, amount, re, im):
            col_tab[at : at + amount, :HALF] = re
            col_tab[at : at + amount, HALF:] = im

        table_focal_lanes(
            write_col,
            quarter_period(index_ref[0]),
            lax.axis_index("col") * cols,
            cols * n_col,
            cols,
            fine_ref,
        )

    return pl.pallas_call(
        kernel,
        in_specs=[pl.BlockSpec(memory_space=pltpu.SMEM)],
        out_specs=pl.BlockSpec(memory_space=pltpu.VMEM),
        out_shape=jax.ShapeDtypeStruct((cols, M), BF16),
        scratch_shapes=[pltpu.VMEM((2, HALF, HALF), F32)],
        compiler_params=pltpu.CompilerParams(vmem_limit_bytes=16 << 20),
        cost_estimate=pl.CostEstimate(flops=20 * M * cols, bytes_accessed=4 * M * cols, transcendentals=0),
        name="col_table",
    )(index)


def backward_kernel(tiles_ref, *refs, counts, wave_ids, part_first, chunks, tile_size, rows):
    waves = len(counts)
    total_pieces = sum(counts)
    sources, refs = refs[:total_pieces], refs[total_pieces:]
    n_tables = 1 + max(table for table, _ in wave_ids)
    row_tabs, refs = refs[:n_tables], refs[n_tables:]
    col_tabs, refs = refs[:waves], refs[waves:]
    incidents, refs = refs[:waves], refs[waves:]
    outs, refs = refs[: len(chunks)], refs[len(chunks) :]
    matrices, (held, sems) = list(refs[:-2]), refs[-2:]
    half_at = lax.rem(lax.axis_index("wl"), 2)
    first = chunks[0][0]
    copies = []
    for k, (at, amount) in enumerate(chunks):
        for w in range(waves):
            if part_first[w] is None:
                span = pl.ds(pl.multiple_of(half_at * rows + at, amount), amount)
                source = incidents[w].at[0, span, :]
            else:
                source = incidents[w].at[pl.ds(at - part_first[w], amount), :]
            copies.append(
                pltpu.make_async_copy(source, held.at[w, pl.ds(at - first, amount), :], sems.at[k, w])
            )
            copies[-1].start()
    ready = []
    for w in range(waves):
        pieces, sources = sources[: counts[w]], sources[counts[w] :]
        if counts[w] == 1:
            ready.append(pieces[0])
            continue
        target = matrices.pop(0)
        at = 0
        for piece in pieces:
            target[at : at + piece.shape[0], :] = piece[...]
            at += piece.shape[0]
        ready.append(target)
    cols = outs[0].shape[1]
    wide = min(512, cols)
    amount = sum(n for _, n in chunks)
    back_y = [
        jnp.dot(
            row_tabs[table][which, first : first + amount, :], ready[w][...], preferred_element_type=F32
        ).astype(BF16)
        for w, (table, which) in enumerate(wave_ids)
    ]
    for copy in copies:
        copy.wait()
    for part in range(0, cols, wide):
        span = slice(part, part + wide)
        total = None
        for w in range(waves):
            back = lax.dot_general(
                back_y[w], col_tabs[w][span, :], (((1,), (1,)), ((), ())), preferred_element_type=F32
            )
            term = back * held[w, :, span].astype(F32)
            total = term if total is None else total + term
        for out, (at, size) in zip(outs, chunks):
            for h in range(0, size, tile_size):
                high = min(h + tile_size, size)
                mask = live_row(tiles_ref, (half_at * rows + at + h) // tile_size, cols)[:, span]
                out[h:high, span] = (total[at - first + h : at - first + high] * mask).astype(BF16)


def backward(tiles, waves, chunks, tile_size, rows):
    cols = tiles.shape[1] * tile_size
    flat = [piece for wave in waves for piece in wave[0]]
    amount = sum(n for _, n in chunks)
    counts = [len(wave[0]) for wave in waves]
    emit = sum(count > 1 for count in counts)
    tables = []
    for wave in waves:
        if not any(wave[1] is table for table in tables):
            tables.append(wave[1])
    wave_ids = [([wave[1] is table for table in tables].index(True), wave[2]) for wave in waves]

    def kernel(*refs):
        backward_kernel(
            *refs,
            counts=counts,
            wave_ids=wave_ids,
            part_first=[wave[5] for wave in waves],
            chunks=chunks,
            tile_size=tile_size,
            rows=rows,
        )

    vmem = pl.BlockSpec(memory_space=pltpu.VMEM)
    hbm = pl.BlockSpec(memory_space=pl.ANY)
    out_shape = [jax.ShapeDtypeStruct((n, cols), BF16) for _, n in chunks]
    out_shape += [jax.ShapeDtypeStruct((M, M), BF16)] * emit
    outs = pl.pallas_call(
        kernel,
        in_specs=[pl.BlockSpec(memory_space=pltpu.SMEM)]
        + [vmem] * (len(flat) + len(tables) + len(waves))
        + [hbm] * len(waves),
        out_specs=[vmem] * len(out_shape),
        out_shape=out_shape,
        scratch_shapes=[
            pltpu.VMEM((len(waves), amount, cols), BF16),
            pltpu.SemaphoreType.DMA((len(chunks), len(waves))),
        ],
        compiler_params=pltpu.CompilerParams(vmem_limit_bytes=24 << 20),
        cost_estimate=pl.CostEstimate(
            flops=2 * len(waves) * amount * M * (cols + M), bytes_accessed=6 * amount * cols, transcendentals=0
        ),
    )(tiles, *flat, *tables, *[wave[3] for wave in waves], *[wave[4] for wave in waves])
    return outs[: len(chunks)], outs[len(chunks) :]


def place_kernel(*refs, chunks, rows):
    sources = refs[: 2 * len(chunks)]
    out, sems = refs[-2:]
    half_at = lax.rem(lax.axis_index("wl"), 2)
    copies = []
    for k, (at, amount) in enumerate(chunks):
        for side in range(2):
            where = half_at if side == 0 else 1 - half_at
            target = out.at[pl.ds(pl.multiple_of(where * rows + at, amount), amount), :]
            copies.append(pltpu.make_async_copy(sources[2 * k + side], target, sems.at[k, side]))
    for copy in copies:
        copy.start()
    for copy in copies:
        copy.wait()


def place(done, chunks, rows, into=None):
    flat = [part for pair in done for part in pair]
    cols = flat[0].shape[1]
    operands = flat + ([into] if into is not None else [])

    def kernel(*refs):
        place_kernel(*refs, chunks=chunks, rows=rows)

    hbm = pl.BlockSpec(memory_space=pl.ANY)
    return pl.pallas_call(
        kernel,
        in_specs=[hbm] * len(operands),
        out_specs=hbm,
        out_shape=jax.ShapeDtypeStruct((2 * rows, cols), BF16),
        scratch_shapes=[pltpu.SemaphoreType.DMA((len(chunks), 2))],
        input_output_aliases={len(flat): 0} if into is not None else {},
        compiler_params=pltpu.CompilerParams(vmem_limit_bytes=1 << 20),
        cost_estimate=pl.CostEstimate(flops=0, bytes_accessed=4 * cols * sum(n for _, n in chunks), transcendentals=0),
    )(*operands)


def slices(incident, rows, begin):
    amount, cols = rows - begin, incident.shape[2]

    def kernel(source, own, other, sems):
        half_at = lax.rem(lax.axis_index("wl"), 2)
        copies = []
        for k, (out, where) in enumerate(((own, half_at), (other, 1 - half_at))):
            span = pl.ds(pl.multiple_of(where * rows + begin, amount), amount)
            copies.append(pltpu.make_async_copy(source.at[0, span, :], out, sems.at[k]))
            copies[-1].start()
        for copy in copies:
            copy.wait()

    return pl.pallas_call(
        kernel,
        in_specs=[pl.BlockSpec(memory_space=pl.ANY)],
        out_specs=[pl.BlockSpec(memory_space=pltpu.VMEM)] * 2,
        out_shape=[jax.ShapeDtypeStruct((amount, cols), BF16)] * 2,
        scratch_shapes=[pltpu.SemaphoreType.DMA((2,))],
        compiler_params=pltpu.CompilerParams(vmem_limit_bytes=58 << 20),
        cost_estimate=pl.CostEstimate(flops=0, bytes_accessed=8 * amount * cols, transcendentals=0),
        name="slices",
    )(incident)


EXCHANGED = (2, 1, 1)
REPEATED = (2, 2)


def all_steps(cotangent, incident, tiles, charge, wl_index):
    rows, cols = cotangent.shape[2:]
    n_row = lax.axis_size("row")
    n_col = lax.axis_size("col")
    tile_size = rows // tiles.shape[0]
    half = rows // 2
    unit = half // 8
    chunks = []
    at = 0
    for size in EXCHANGED + REPEATED:
        chunks.append((at, size * unit))
        at += size * unit
    n_first = len(EXCHANGED)
    split = chunks[n_first][0]

    slice_own, slice_other = slices(incident, half, split)
    inc_straight = swap(slice_own, "wl", 2)
    groups = slot_groups(n_row, n_col)
    parts, col_own = forward(wl_index, charge, tiles, cotangent, n_row, n_col, groups)
    mine = reduce_blocks(parts, groups, n_row)
    inc_core = swap(incident, "wl", 1)
    inc_cross = swap(slice_other, "wl", 3)
    col_core = swap(col_own, "wl", 1)
    near = jnp.concatenate([wl_index, swap(wl_index, "wl", 1)])
    far = swap(wl_index, "wl", 2)
    far_core = swap(far, "wl", 1)
    row_near = row_tables(near, half, n_row, n_col, rows)
    row_far = row_tables(jnp.concatenate([far, far_core]), half, n_row, n_col, rows)
    col_straight = col_table(far, cols, n_col)
    col_cross = swap(col_straight, "wl", 1)

    here = gather_row(mine, n_row)
    if n_row > 4:
        here = [jnp.concatenate(here, axis=0)]
    joined = jnp.concatenate(here, axis=0)
    pieces, pieces_core = [joined], [swap(joined, "wl", 1)]
    for ky in range(1, n_col):
        for piece in here:
            pieces.append(swap(piece, "col", ky))
            pieces_core.append(swap(pieces[-1], "wl", 1))

    straight = [swap(joined, "wl", 2)]
    straight += [swap(straight[0], "col", ky) for ky in range(1, n_col)]
    cross = [swap(piece, "wl", 1) for piece in straight]

    own = (aligned(pieces), row_near, 0, col_own, incident, None)
    mate = (aligned(pieces_core), row_near, 1, col_core, inc_core, None)
    first, matrices = backward(tiles, [own, mate], chunks[:1], tile_size, half)
    if len(matrices) == 2:
        own = ([matrices[0]],) + own[1:]
        mate = ([matrices[1]],) + mate[1:]
    second, _ = backward(tiles, [own, mate], chunks[1:n_first], tile_size, half)
    straight = (aligned(straight), row_far, 0, col_straight, inc_straight, split)
    cross = (aligned(cross), row_far, 1, col_cross, inc_cross, split)
    both, _ = backward(tiles, [own, mate, straight, cross], chunks[n_first:], tile_size, half)
    done = []
    for pair in list(first) + list(second):
        total = add_up([pair, swap(pair, "wl", 2)]).astype(BF16)
        done.append((total, swap(total, "wl", 1)))
    ready = [(part, swap(part, "wl", 1)) for part in both]
    result = place(ready, chunks[n_first:], half)
    result = place(done[:-1], chunks[: n_first - 1], half, result)
    return place(done[-1:], chunks[n_first - 1 : n_first], half, result)


def solution(mesh):
    return jax.shard_map(
        all_steps,
        mesh=mesh,
        in_specs=(
            P("wl", None, "row", "col"),
            P("wl", "row", "col"),
            P("row", "col"),
            P("wl"),
            P("wl"),
        ),
        out_specs=P("row", "col"),
        check_vma=False,
    )
```

```python
import math

import jax
import jax.numpy as jnp
from jax import lax
from jax.experimental import pallas as pl
from jax.experimental.pallas import tpu as pltpu
from jax.sharding import PartitionSpec as P


M = 512
HALF = M // 2
F32 = jnp.float32
BF16 = jnp.bfloat16


def iota(shape, axis):
    return lax.broadcasted_iota(jnp.int32, shape, axis).astype(F32)


def unit_phasor(product, period):
    turns = jnp.floor(product / period + 0.5)
    rest = product - turns * period
    quarter = jnp.floor(4.0 * rest / period + 0.5)
    theta = (4.0 * rest - quarter * period) / period * (0.5 * math.pi)
    sq = theta * theta
    sin_p = theta * (
        1.0 + sq * (-1.0 / 6.0 + sq * (1.0 / 120.0 + sq * (-1.0 / 5040.0 + sq / 362880.0)))
    )
    cos_p = 1.0 + sq * (
        -0.5 + sq * (1.0 / 24.0 + sq * (-1.0 / 720.0 + sq * (1.0 / 40320.0 - sq / 3628800.0)))
    )
    size = jnp.abs(quarter)
    odd = size == 1.0
    flip = jnp.where(size == 2.0, -1.0, 1.0)
    side = jnp.where(quarter < 0.0, -1.0, 1.0)
    cosine = jnp.where(odd, -side * sin_p, flip * cos_p)
    sine = jnp.where(odd, side * cos_p, flip * sin_p)
    return cosine, sine


def turn(first, second):
    c1, s1 = first
    c2, s2 = second
    return c1 * c2 - s1 * s2, s1 * c2 + c1 * s2


def quarter_period(index_value):
    return ((index_value + 32) * (M // 4)).astype(F32)


def table_focal_lanes(write, period, first, extent, amount, fine_ref, lanes=None, lane_count=HALF):
    block = 256
    focal = 2.0 * iota((16, lane_count), 1) + 1.0 if lanes is None else lanes
    step = iota((16, lane_count), 0)
    fine = unit_phasor(2.0 * step * focal, jnp.full((16, lane_count), period, F32))
    mid = unit_phasor(32.0 * step * focal, jnp.full((16, lane_count), period, F32))
    for b in range(16):
        re, im = turn((mid[0][b : b + 1], mid[1][b : b + 1]), fine)
        fine_ref[0, 16 * b : 16 * b + 16, :] = re
        fine_ref[1, 16 * b : 16 * b + 16, :] = im
    count = amount // block
    start = (2 * first - extent + 1).astype(F32)
    top = -(-count // 8) * 8
    focal_top = 2.0 * iota((top, lane_count), 1) + 1.0 if lanes is None else jnp.broadcast_to(lanes[:1], (top, lane_count))
    coarse = unit_phasor(
        (start + 2.0 * block * iota((top, lane_count), 0)) * focal_top,
        jnp.full((top, lane_count), period, F32),
    )
    for a in range(count):
        for part in range(0, block, 64):
            re, im = turn(
                (coarse[0][a : a + 1], coarse[1][a : a + 1]),
                (fine_ref[0, part : part + 64, :], fine_ref[1, part : part + 64, :]),
            )
            write(a * block + part, 64, re.astype(BF16), im.astype(BF16))


def table_pupil_lanes(write, period, first, extent, amount, fine_ref, focal_first, focal_count):
    count = amount // 128
    shape = (focal_count, 128)
    focal = 2.0 * (focal_first + iota(shape, 0)) + 1.0
    lane = iota(shape, 1)
    full = jnp.full(shape, period, F32)
    fine = unit_phasor(2.0 * lane * focal, full)
    fine_ref[0, :focal_count, :128] = fine[0]
    fine_ref[1, :focal_count, :128] = fine[1]
    start = (2 * first - extent + 1).astype(F32)
    coarse = unit_phasor((start + 256.0 * lane) * focal, full)
    fine_ref[0, :focal_count, 128:] = coarse[0]
    fine_ref[1, :focal_count, 128:] = coarse[1]
    for a in range(count):
        for part in range(0, focal_count, 64):
            rows = slice(part, min(part + 64, focal_count))
            re, im = turn(
                (fine_ref[0, rows, 128 + a : 129 + a], fine_ref[1, rows, 128 + a : 129 + a]),
                (fine_ref[0, rows, :128], fine_ref[1, rows, :128]),
            )
            write(part, a * 128, re.astype(BF16), im.astype(BF16))


def live_row(tiles_ref, tile_row, cells):
    tile_cols = tiles_ref.shape[1]
    width = cells // tile_cols
    parts = [
        jnp.full((1, width), jnp.where(tiles_ref[tile_row, j] == 1, 1.0, 0.0), F32)
        for j in range(tile_cols)
    ]
    return jnp.concatenate(parts, axis=1)


def slice_rows(source, target, sem, which, begin):
    span = pl.ds(pl.multiple_of(which * (source.shape[1] // 2) + begin, target.shape[0]), target.shape[0])
    return pltpu.make_async_copy(source.at[0, span, :], target, sem)


def forward_kernel(index_ref, charge_ref, tiles_ref, cot_ref, inc_ref, *refs, rows, cols, n_row, groups, begin):
    outs, (col_tab, slice_ref) = refs[:-8], refs[-8:-6]
    row_tab, inner, fine_ref, t_ref, held, sems = refs[-6:]
    block = min(256, rows)
    extent = rows * n_row
    row_at = lax.axis_index("row")
    col_at = lax.axis_index("col")
    tile_size = rows // tiles_ref.shape[0]
    copies = []
    for step in range(rows // block):
        span = pl.ds(step * block, block)
        copies.append(pltpu.make_async_copy(cot_ref.at[0, :, span, :], held.at[:, span, :], sems.at[step]))
        copies[-1].start()
    half_at = lax.rem(lax.axis_index("wl"), 2)
    slice_copy = slice_rows(inc_ref, slice_ref, sems.at[rows // block], 1 - half_at, begin)
    slice_copy.start()
    period = quarter_period(index_ref[0])

    def write_col(at, amount, re, im):
        col_tab[at : at + amount, :HALF] = re
        col_tab[at : at + amount, HALF:] = im

    table_focal_lanes(write_col, period, col_at * cols, extent, cols, fine_ref)

    def write_row(part, at, re, im):
        row_tab[part : part + 64, at : at + 128] = re
        row_tab[HALF + part : HALF + part + 64, at : at + 128] = im

    table_pupil_lanes(write_row, period, row_at * rows, extent, rows, fine_ref, 0.0, HALF)

    for step in range(rows // block):
        copies[step].wait()
        halves = []
        for part in range(2):
            for at in range(step * block, (step + 1) * block, tile_size):
                mask = live_row(tiles_ref, at // tile_size, cols).astype(BF16)
                halves.append(held[part, at : at + tile_size, :] * mask)
        prod = jnp.dot(jnp.concatenate(halves, axis=0), col_tab[...], preferred_element_type=F32)
        at = step * block
        inner[at : at + block, :M] = prod[:block].astype(BF16)
        inner[at : at + block, M:] = prod[block:].astype(BF16)

    charge = charge_ref[0]
    even = jnp.where(charge % 2 == 0, 1.0, 0.0).astype(F32)
    odd = 1.0 - even
    scale = 4.0 / (extent * M)
    chunk = 128
    shape = (chunk, HALF)
    for ub in range(HALF // chunk):
        both = jnp.concatenate(
            [row_tab[ub * chunk : (ub + 1) * chunk, :], row_tab[HALF + ub * chunk : HALF + (ub + 1) * chunk, :]],
            axis=0,
        )
        q = jnp.dot(both, inner[...], preferred_element_type=F32)
        q_c, q_s = q[:chunk], q[chunk:]
        u = 2.0 * (iota(shape, 0) + float(ub * chunk)) + 1.0
        v = 2.0 * iota(shape, 1) + 1.0
        inv = 1.0 / jnp.sqrt(u * u + v * v)
        power = (u * inv, v * inv)
        total = (jnp.full(shape, scale, F32), jnp.zeros(shape, F32))
        for bit in range(4):
            taken = (charge >> bit) % 2 == 1
            multiplied = turn(total, power)
            total = tuple(jnp.where(taken, new, old) for new, old in zip(multiplied, total))
            power = turn(power, power)
        c, s = total
        ce, se, co, so = c * even, s * even, c * odd, s * odd
        ca, cb, cc, cd = (q_c[:, k * HALF : (k + 1) * HALF] for k in range(4))
        sa, sb, sc, sd = (q_s[:, k * HALF : (k + 1) * HALF] for k in range(4))
        t_ee = ce * ca - se * sd + so * cb - co * sc
        t_eo = ce * cb + se * sc - so * ca - co * sd
        t_oe = ce * sa + se * cd + co * cc + so * sb
        t_oo = ce * sb - se * cc + co * cd - so * sa
        per = t_ref.shape[1]
        span = min(per, chunk)
        for j in range(chunk // span):
            rows_j = slice(j * span, (j + 1) * span)
            for first, left, right in (
                (ub * chunk + j * span, t_ee, t_eo),
                (HALF + ub * chunk + j * span, t_oe, t_oo),
            ):
                to = slice(first % per, first % per + span)
                t_ref[first // per, to, :HALF] = left[rows_j]
                t_ref[first // per, to, HALF:] = right[rows_j]
    for out, (ky, slots) in zip(outs, groups):
        for k, kz in enumerate(slots):
            source = (col_at ^ ky) * n_row + (row_at ^ kz)
            out[k] = t_ref[source].astype(BF16)
    slice_copy.wait()


def in_hbm(value):
    return pltpu.with_memory_space_constraint(value, pltpu.HBM)


def forward(index, charge, tiles, cotangent, incident, begin, n_row, n_col, groups):
    rows, cols = cotangent.shape[2:]
    block = min(256, rows)
    per = M // (n_row * n_col)
    out_shape = [jax.ShapeDtypeStruct((len(slots), per, M), BF16) for _, slots in groups]
    out_shape.append(jax.ShapeDtypeStruct((cols, M), BF16))
    out_shape.append(jax.ShapeDtypeStruct((rows // 2 - begin, cols), BF16))

    def kernel(*refs):
        forward_kernel(*refs, rows=rows, cols=cols, n_row=n_row, groups=groups, begin=begin)

    smem = pl.BlockSpec(memory_space=pltpu.SMEM)
    outs = pl.pallas_call(
        kernel,
        in_specs=[smem, smem, smem] + [pl.BlockSpec(memory_space=pltpu.HBM)] * 2,
        out_specs=[pl.BlockSpec(memory_space=pltpu.VMEM)] * len(out_shape),
        out_shape=out_shape,
        scratch_shapes=[
            pltpu.VMEM((M, rows), BF16),
            pltpu.VMEM((rows, 2 * M), BF16),
            pltpu.VMEM((2, HALF, HALF), F32),
            pltpu.VMEM((n_row * n_col, per, M), F32),
            pltpu.VMEM((2, rows, cols), BF16),
            pltpu.SemaphoreType.DMA((rows // block + 1,)),
        ],
        compiler_params=pltpu.CompilerParams(vmem_limit_bytes=36 << 20),
        cost_estimate=pl.CostEstimate(
            flops=2 * rows * 2 * M * (cols + M), bytes_accessed=4 * rows * cols, transcendentals=0
        ),
        name="forward",
    )(index, charge, tiles, in_hbm(cotangent), in_hbm(incident))
    return outs[:-2], outs[-2], outs[-1]


def swap(value, axis, bits):
    size = lax.axis_size(axis)
    return lax.ppermute(value, axis, [(i, i ^ bits) for i in range(size)])


def add_up(parts):
    total = parts[0].astype(F32)
    for part in parts[1:]:
        total = total + part.astype(F32)
    return total


def hop_order(n_row):
    return sorted(range(1, n_row), key=lambda k: -(k & -k))


def slot_groups(n_row, n_col):
    order = hop_order(n_row) + [0]
    if n_row <= 4:
        parts = [[kz] for kz in order]
    else:
        parts = [order[: n_row // 2], order[n_row // 2 :]]
    return [(ky, tuple(slots)) for slots in parts for ky in range(n_col)]


def reduce_blocks(parts, groups, n_row):
    reduced = {}
    for own, (ky, slots) in zip(parts, groups):
        if ky:
            continue
        terms = [own]
        for other, (step, other_slots) in zip(parts, groups):
            if step and other_slots == slots:
                terms.append(swap(other, "col", step))
        total = add_up(terms).astype(BF16)
        for k, kz in enumerate(slots):
            reduced[kz] = total[k]
    moved = [swap(reduced[kz], "row", kz) for kz in hop_order(n_row)]
    return add_up([reduced[0]] + moved).astype(BF16)


def gather_row(mine, n_row):
    found = {0: mine}
    for kz in hop_order(n_row):
        found[kz] = swap(mine, "row", kz)
    return [found[kz] for kz in range(n_row)]


def aligned(pieces):
    if any(piece.shape[0] % 16 for piece in pieces):
        return [jnp.concatenate(pieces, axis=0)]
    return pieces


def row_table_kernel(index_ref, row_tab, fine_ref, *, rows, n_row, n_col, full_rows, waves):
    extent = full_rows * n_row
    row_at = lax.axis_index("row")
    col_at = lax.axis_index("col")
    half_at = lax.rem(lax.axis_index("wl"), 2)
    per = M // (n_row * n_col)
    lane = lax.broadcasted_iota(jnp.int32, (16, M), 1)
    block = lane // per
    owner = ((block // n_row) ^ col_at) * n_row + ((block % n_row) ^ row_at)
    place = owner * per + lane % per
    is_sin = place >= HALF
    focal = 2.0 * jnp.where(is_sin, place - HALF, place).astype(F32) + 1.0
    for w in range(waves):
        period = quarter_period(index_ref[w])
        for side in range(2):
            lanes = slice(side * HALF, (side + 1) * HALF)
            sine = is_sin[:1, lanes]

            def write_row(at, amount, re, im, w=w, lanes=lanes, sine=sine):
                row_tab[w, at : at + amount, lanes] = jnp.where(
                    sine, im.astype(F32), re.astype(F32)
                ).astype(BF16)

            table_focal_lanes(
                write_row,
                period,
                row_at * full_rows + half_at * rows,
                extent,
                row_tab.shape[1],
                fine_ref,
                lanes=focal[:, lanes],
            )


def row_tables(indices, rows, n_row, n_col, full_rows):
    waves = indices.shape[0]
    own_rows = max(rows, 256)

    def kernel(*refs):
        row_table_kernel(*refs, rows=rows, n_row=n_row, n_col=n_col, full_rows=full_rows, waves=waves)

    return pl.pallas_call(
        kernel,
        in_specs=[pl.BlockSpec(memory_space=pltpu.SMEM)],
        out_specs=pl.BlockSpec(memory_space=pltpu.VMEM),
        out_shape=jax.ShapeDtypeStruct((waves, own_rows, M), BF16),
        scratch_shapes=[pltpu.VMEM((2, HALF, HALF), F32)],
        compiler_params=pltpu.CompilerParams(vmem_limit_bytes=16 << 20),
        cost_estimate=pl.CostEstimate(flops=40 * M * own_rows, bytes_accessed=4 * M * own_rows, transcendentals=0),
        name="row_tables",
    )(indices)


def col_table(index, cols, n_col):
    def kernel(index_ref, col_tab, fine_ref):
        def write_col(at, amount, re, im):
            col_tab[at : at + amount, :HALF] = re
            col_tab[at : at + amount, HALF:] = im

        table_focal_lanes(
            write_col,
            quarter_period(index_ref[0]),
            lax.axis_index("col") * cols,
            cols * n_col,
            cols,
            fine_ref,
        )

    return pl.pallas_call(
        kernel,
        in_specs=[pl.BlockSpec(memory_space=pltpu.SMEM)],
        out_specs=pl.BlockSpec(memory_space=pltpu.VMEM),
        out_shape=jax.ShapeDtypeStruct((cols, M), BF16),
        scratch_shapes=[pltpu.VMEM((2, HALF, HALF), F32)],
        compiler_params=pltpu.CompilerParams(vmem_limit_bytes=16 << 20),
        cost_estimate=pl.CostEstimate(flops=20 * M * cols, bytes_accessed=4 * M * cols, transcendentals=0),
        name="col_table",
    )(index)


def backward_kernel(tiles_ref, *refs, counts, wave_ids, part_first, chunks, tile_size, rows):
    waves = len(counts)
    total_pieces = sum(counts)
    sources, refs = refs[:total_pieces], refs[total_pieces:]
    n_tables = 1 + max(table for table, _ in wave_ids)
    row_tabs, refs = refs[:n_tables], refs[n_tables:]
    col_tabs, refs = refs[:waves], refs[waves:]
    incidents, refs = refs[:waves], refs[waves:]
    outs, refs = refs[: len(chunks)], refs[len(chunks) :]
    matrices, (held, sems) = list(refs[:-2]), refs[-2:]
    half_at = lax.rem(lax.axis_index("wl"), 2)
    first = chunks[0][0]
    copies = []
    for k, (at, amount) in enumerate(chunks):
        for w in range(waves):
            if part_first[w] is None:
                span = pl.ds(pl.multiple_of(half_at * rows + at, amount), amount)
                source = incidents[w].at[0, span, :]
            else:
                source = incidents[w].at[pl.ds(at - part_first[w], amount), :]
            copies.append(
                pltpu.make_async_copy(source, held.at[w, pl.ds(at - first, amount), :], sems.at[k, w])
            )
            copies[-1].start()
    ready = []
    for w in range(waves):
        pieces, sources = sources[: counts[w]], sources[counts[w] :]
        if counts[w] == 1:
            ready.append(pieces[0])
            continue
        target = matrices.pop(0)
        at = 0
        for piece in pieces:
            target[at : at + piece.shape[0], :] = piece[...]
            at += piece.shape[0]
        ready.append(target)
    cols = outs[0].shape[1]
    wide = min(512, cols)
    amount = sum(n for _, n in chunks)
    back_y = [
        jnp.dot(
            row_tabs[table][which, first : first + amount, :], ready[w][...], preferred_element_type=F32
        ).astype(BF16)
        for w, (table, which) in enumerate(wave_ids)
    ]
    for copy in copies:
        copy.wait()
    for part in range(0, cols, wide):
        span = slice(part, part + wide)
        total = None
        for w in range(waves):
            back = lax.dot_general(
                back_y[w], col_tabs[w][span, :], (((1,), (1,)), ((), ())), preferred_element_type=F32
            )
            term = back * held[w, :, span].astype(F32)
            total = term if total is None else total + term
        for out, (at, size) in zip(outs, chunks):
            for h in range(0, size, tile_size):
                high = min(h + tile_size, size)
                mask = live_row(tiles_ref, (half_at * rows + at + h) // tile_size, cols)[:, span]
                out[h:high, span] = (total[at - first + h : at - first + high] * mask).astype(BF16)


def backward(tiles, waves, chunks, tile_size, rows):
    cols = tiles.shape[1] * tile_size
    flat = [piece for wave in waves for piece in wave[0]]
    amount = sum(n for _, n in chunks)
    counts = [len(wave[0]) for wave in waves]
    emit = sum(count > 1 for count in counts)
    tables = []
    for wave in waves:
        if not any(wave[1] is table for table in tables):
            tables.append(wave[1])
    wave_ids = [([wave[1] is table for table in tables].index(True), wave[2]) for wave in waves]

    def kernel(*refs):
        backward_kernel(
            *refs,
            counts=counts,
            wave_ids=wave_ids,
            part_first=[wave[5] for wave in waves],
            chunks=chunks,
            tile_size=tile_size,
            rows=rows,
        )

    vmem = pl.BlockSpec(memory_space=pltpu.VMEM)
    hbm = pl.BlockSpec(memory_space=pl.ANY)
    out_shape = [jax.ShapeDtypeStruct((n, cols), BF16) for _, n in chunks]
    out_shape += [jax.ShapeDtypeStruct((M, M), BF16)] * emit
    outs = pl.pallas_call(
        kernel,
        in_specs=[pl.BlockSpec(memory_space=pltpu.SMEM)]
        + [vmem] * (len(flat) + len(tables) + len(waves))
        + [hbm] * len(waves),
        out_specs=[vmem] * len(out_shape),
        out_shape=out_shape,
        scratch_shapes=[
            pltpu.VMEM((len(waves), amount, cols), BF16),
            pltpu.SemaphoreType.DMA((len(chunks), len(waves))),
        ],
        compiler_params=pltpu.CompilerParams(vmem_limit_bytes=24 << 20),
        cost_estimate=pl.CostEstimate(
            flops=2 * len(waves) * amount * M * (cols + M), bytes_accessed=6 * amount * cols, transcendentals=0
        ),
    )(tiles, *flat, *tables, *[wave[3] for wave in waves], *[wave[4] for wave in waves])
    return outs[: len(chunks)], outs[len(chunks) :]


def place_kernel(*refs, chunks, rows):
    sources = refs[: 2 * len(chunks)]
    out, sems = refs[-2:]
    half_at = lax.rem(lax.axis_index("wl"), 2)
    copies = []
    for k, (at, amount) in enumerate(chunks):
        for side in range(2):
            where = half_at if side == 0 else 1 - half_at
            target = out.at[pl.ds(pl.multiple_of(where * rows + at, amount), amount), :]
            copies.append(pltpu.make_async_copy(sources[2 * k + side], target, sems.at[k, side]))
    for copy in copies:
        copy.start()
    for copy in copies:
        copy.wait()


def place(done, chunks, rows, into=None):
    flat = [part for pair in done for part in pair]
    cols = flat[0].shape[1]
    operands = flat + ([into] if into is not None else [])

    def kernel(*refs):
        place_kernel(*refs, chunks=chunks, rows=rows)

    hbm = pl.BlockSpec(memory_space=pl.ANY)
    return pl.pallas_call(
        kernel,
        in_specs=[hbm] * len(operands),
        out_specs=hbm,
        out_shape=jax.ShapeDtypeStruct((2 * rows, cols), BF16),
        scratch_shapes=[pltpu.SemaphoreType.DMA((len(chunks), 2))],
        input_output_aliases={len(flat): 0} if into is not None else {},
        compiler_params=pltpu.CompilerParams(vmem_limit_bytes=1 << 20),
        cost_estimate=pl.CostEstimate(flops=0, bytes_accessed=4 * cols * sum(n for _, n in chunks), transcendentals=0),
    )(*operands)


def own_slice(incident, begin):
    amount, cols = incident.shape[1] // 2 - begin, incident.shape[2]

    def kernel(source, out, sem):
        copy = slice_rows(source, out, sem, lax.rem(lax.axis_index("wl"), 2), begin)
        copy.start()
        copy.wait()

    return pl.pallas_call(
        kernel,
        in_specs=[pl.BlockSpec(memory_space=pltpu.HBM)],
        out_specs=pl.BlockSpec(memory_space=pltpu.VMEM),
        out_shape=jax.ShapeDtypeStruct((amount, cols), BF16),
        scratch_shapes=[pltpu.SemaphoreType.DMA],
        compiler_params=pltpu.CompilerParams(vmem_limit_bytes=4 << 20),
        cost_estimate=pl.CostEstimate(flops=0, bytes_accessed=4 * amount * cols, transcendentals=0),
        name="own_slice",
    )(in_hbm(incident))


EXCHANGED = (2, 1, 1)
REPEATED = (2, 2)


def all_steps(cotangent, incident, tiles, charge, wl_index):
    rows, cols = cotangent.shape[2:]
    n_row = lax.axis_size("row")
    n_col = lax.axis_size("col")
    tile_size = rows // tiles.shape[0]
    half = rows // 2
    unit = half // 8
    chunks = []
    at = 0
    for size in EXCHANGED + REPEATED:
        chunks.append((at, size * unit))
        at += size * unit
    n_first = len(EXCHANGED)
    split = chunks[n_first][0]

    inc_straight = swap(own_slice(incident, split), "wl", 2)
    groups = slot_groups(n_row, n_col)
    parts, col_own, slice_other = forward(
        wl_index, charge, tiles, cotangent, incident, split, n_row, n_col, groups
    )
    mine = reduce_blocks(parts, groups, n_row)
    inc_core = swap(incident, "wl", 1)
    inc_cross = swap(slice_other, "wl", 3)
    col_core = swap(col_own, "wl", 1)
    near = jnp.concatenate([wl_index, swap(wl_index, "wl", 1)])
    far = swap(wl_index, "wl", 2)
    far_core = swap(far, "wl", 1)
    row_near = row_tables(near, half, n_row, n_col, rows)
    row_far = row_tables(jnp.concatenate([far, far_core]), half, n_row, n_col, rows)
    col_straight = col_table(far, cols, n_col)
    col_cross = swap(col_straight, "wl", 1)

    here = gather_row(mine, n_row)
    if n_row > 4:
        here = [jnp.concatenate(here, axis=0)]
    joined = jnp.concatenate(here, axis=0)
    pieces, pieces_core = [joined], [swap(joined, "wl", 1)]
    for ky in range(1, n_col):
        for piece in here:
            pieces.append(swap(piece, "col", ky))
            pieces_core.append(swap(pieces[-1], "wl", 1))

    straight = [swap(joined, "wl", 2)]
    straight += [swap(straight[0], "col", ky) for ky in range(1, n_col)]
    cross = [swap(piece, "wl", 1) for piece in straight]

    own = (aligned(pieces), row_near, 0, col_own, incident, None)
    mate = (aligned(pieces_core), row_near, 1, col_core, inc_core, None)
    first, matrices = backward(tiles, [own, mate], chunks[:1], tile_size, half)
    if len(matrices) == 2:
        own = ([matrices[0]],) + own[1:]
        mate = ([matrices[1]],) + mate[1:]
    second, _ = backward(tiles, [own, mate], chunks[1:n_first], tile_size, half)
    straight = (aligned(straight), row_far, 0, col_straight, inc_straight, split)
    cross = (aligned(cross), row_far, 1, col_cross, inc_cross, split)
    both, _ = backward(tiles, [own, mate, straight, cross], chunks[n_first:], tile_size, half)
    done = []
    for pair in list(first) + list(second):
        total = add_up([pair, swap(pair, "wl", 2)]).astype(BF16)
        done.append((total, swap(total, "wl", 1)))
    ready = [(part, swap(part, "wl", 1)) for part in both]
    result = place(ready, chunks[n_first:], half)
    result = place(done[:-1], chunks[: n_first - 1], half, result)
    return place(done[-1:], chunks[n_first - 1 : n_first], half, result)


def solution(mesh):
    return jax.shard_map(
        all_steps,
        mesh=mesh,
        in_specs=(
            P("wl", None, "row", "col"),
            P("wl", "row", "col"),
            P("row", "col"),
            P("wl"),
            P("wl"),
        ),
        out_specs=P("row", "col"),
        check_vma=False,
    )
```

```python
import math

import jax
import jax.numpy as jnp
from jax import lax
from jax.experimental import pallas as pl
from jax.experimental.pallas import tpu as pltpu
from jax.sharding import PartitionSpec as P


M = 512
HALF = M // 2
F32 = jnp.float32
BF16 = jnp.bfloat16


def iota(shape, axis):
    return lax.broadcasted_iota(jnp.int32, shape, axis).astype(F32)


def unit_phasor(product, period):
    turns = jnp.floor(product / period + 0.5)
    rest = product - turns * period
    quarter = jnp.floor(4.0 * rest / period + 0.5)
    theta = (4.0 * rest - quarter * period) / period * (0.5 * math.pi)
    sq = theta * theta
    sin_p = theta * (
        1.0 + sq * (-1.0 / 6.0 + sq * (1.0 / 120.0 + sq * (-1.0 / 5040.0 + sq / 362880.0)))
    )
    cos_p = 1.0 + sq * (
        -0.5 + sq * (1.0 / 24.0 + sq * (-1.0 / 720.0 + sq * (1.0 / 40320.0 - sq / 3628800.0)))
    )
    size = jnp.abs(quarter)
    odd = size == 1.0
    flip = jnp.where(size == 2.0, -1.0, 1.0)
    side = jnp.where(quarter < 0.0, -1.0, 1.0)
    cosine = jnp.where(odd, -side * sin_p, flip * cos_p)
    sine = jnp.where(odd, side * cos_p, flip * sin_p)
    return cosine, sine


def turn(first, second):
    c1, s1 = first
    c2, s2 = second
    return c1 * c2 - s1 * s2, s1 * c2 + c1 * s2


def quarter_period(index_value):
    return ((index_value + 32) * (M // 4)).astype(F32)


def table_focal_lanes(write, period, first, extent, amount, fine_ref, lanes=None, lane_count=HALF):
    block = 256
    focal = 2.0 * iota((16, lane_count), 1) + 1.0 if lanes is None else lanes
    step = iota((16, lane_count), 0)
    fine = unit_phasor(2.0 * step * focal, jnp.broadcast_to(period, (16, lane_count)))
    mid = unit_phasor(32.0 * step * focal, jnp.broadcast_to(period, (16, lane_count)))
    for b in range(16):
        re, im = turn((mid[0][b : b + 1], mid[1][b : b + 1]), fine)
        fine_ref[0, 16 * b : 16 * b + 16, :] = re
        fine_ref[1, 16 * b : 16 * b + 16, :] = im
    count = amount // block
    start = (2 * first - extent + 1).astype(F32)
    top = -(-count // 8) * 8
    focal_top = 2.0 * iota((top, lane_count), 1) + 1.0 if lanes is None else jnp.broadcast_to(lanes[:1], (top, lane_count))
    coarse = unit_phasor(
        (start + 2.0 * block * iota((top, lane_count), 0)) * focal_top,
        jnp.broadcast_to(period, (top, lane_count)),
    )
    for a in range(count):
        for part in range(0, block, 64):
            re, im = turn(
                (coarse[0][a : a + 1], coarse[1][a : a + 1]),
                (fine_ref[0, part : part + 64, :], fine_ref[1, part : part + 64, :]),
            )
            write(a * block + part, 64, re.astype(BF16), im.astype(BF16))


def table_pupil_lanes(write, period, first, extent, amount, fine_ref, focal_first, focal_count):
    count = amount // 128
    shape = (focal_count, 128)
    focal = 2.0 * (focal_first + iota(shape, 0)) + 1.0
    lane = iota(shape, 1)
    full = jnp.broadcast_to(period, shape)
    fine = unit_phasor(2.0 * lane * focal, full)
    fine_ref[0, :focal_count, :128] = fine[0]
    fine_ref[1, :focal_count, :128] = fine[1]
    start = (2 * first - extent + 1).astype(F32)
    coarse = unit_phasor((start + 256.0 * lane) * focal, full)
    fine_ref[0, :focal_count, 128:] = coarse[0]
    fine_ref[1, :focal_count, 128:] = coarse[1]
    for a in range(count):
        for part in range(0, focal_count, 64):
            rows = slice(part, min(part + 64, focal_count))
            re, im = turn(
                (fine_ref[0, rows, 128 + a : 129 + a], fine_ref[1, rows, 128 + a : 129 + a]),
                (fine_ref[0, rows, :128], fine_ref[1, rows, :128]),
            )
            write(part, a * 128, re.astype(BF16), im.astype(BF16))


def live_row(tiles_ref, tile_row, cells):
    tile_cols = tiles_ref.shape[1]
    width = cells // tile_cols
    parts = [
        jnp.full((1, width), jnp.where(tiles_ref[tile_row, j] == 1, 1.0, 0.0), F32)
        for j in range(tile_cols)
    ]
    return jnp.concatenate(parts, axis=1)


def slice_rows(source, target, sem, which, begin):
    span = pl.ds(pl.multiple_of(which * (source.shape[1] // 2) + begin, 16), target.shape[0])
    return pltpu.make_async_copy(source.at[0, span, :], target, sem)


def forward_kernel(index_ref, charge_ref, tiles_ref, cot_ref, inc_ref, *refs, rows, cols, n_row, groups, begin):
    outs, (col_tab, slice_ref) = refs[:-8], refs[-8:-6]
    row_tab, inner, fine_ref, t_ref, held, sems = refs[-6:]
    block = min(256, rows)
    extent = rows * n_row
    row_at = lax.axis_index("row")
    col_at = lax.axis_index("col")
    tile_size = rows // tiles_ref.shape[0]
    copies = []
    for step in range(rows // block):
        span = pl.ds(step * block, block)
        copies.append(pltpu.make_async_copy(cot_ref.at[0, :, span, :], held.at[:, span, :], sems.at[step]))
        copies[-1].start()
    half_at = lax.rem(lax.axis_index("wl"), 2)
    slice_copy = slice_rows(inc_ref, slice_ref, sems.at[rows // block], 1 - half_at, begin)
    slice_copy.start()
    period = quarter_period(index_ref[...])

    def write_col(at, amount, re, im):
        col_tab[at : at + amount, :HALF] = re
        col_tab[at : at + amount, HALF:] = im

    table_focal_lanes(write_col, period, col_at * cols, extent, cols, fine_ref)

    def write_row(part, at, re, im):
        row_tab[part : part + 64, at : at + 128] = re
        row_tab[HALF + part : HALF + part + 64, at : at + 128] = im

    table_pupil_lanes(write_row, period, row_at * rows, extent, rows, fine_ref, 0.0, HALF)

    for step in range(rows // block):
        copies[step].wait()
        halves = []
        for part in range(2):
            for at in range(step * block, (step + 1) * block, tile_size):
                mask = live_row(tiles_ref, at // tile_size, cols).astype(BF16)
                halves.append(held[part, at : at + tile_size, :] * mask)
        prod = jnp.dot(jnp.concatenate(halves, axis=0), col_tab[...], preferred_element_type=F32)
        at = step * block
        inner[at : at + block, :M] = prod[:block].astype(BF16)
        inner[at : at + block, M:] = prod[block:].astype(BF16)

    charge = charge_ref[...]
    even = jnp.where(charge % 2 == 0, 1.0, 0.0).astype(F32)
    odd = 1.0 - even
    scale = 4.0 / (extent * M)
    chunk = 128
    shape = (chunk, HALF)
    for ub in range(HALF // chunk):
        both = jnp.concatenate(
            [row_tab[ub * chunk : (ub + 1) * chunk, :], row_tab[HALF + ub * chunk : HALF + (ub + 1) * chunk, :]],
            axis=0,
        )
        q = jnp.dot(both, inner[...], preferred_element_type=F32)
        q_c, q_s = q[:chunk], q[chunk:]
        u = 2.0 * (iota(shape, 0) + float(ub * chunk)) + 1.0
        v = 2.0 * iota(shape, 1) + 1.0
        inv = 1.0 / jnp.sqrt(u * u + v * v)
        power = (u * inv, v * inv)
        total = (jnp.full(shape, scale, F32), jnp.zeros(shape, F32))
        for bit in range(4):
            taken = (charge >> bit) % 2 == 1
            multiplied = turn(total, power)
            total = tuple(jnp.where(taken, new, old) for new, old in zip(multiplied, total))
            power = turn(power, power)
        c, s = total
        ce, se, co, so = c * even, s * even, c * odd, s * odd
        ca, cb, cc, cd = (q_c[:, k * HALF : (k + 1) * HALF] for k in range(4))
        sa, sb, sc, sd = (q_s[:, k * HALF : (k + 1) * HALF] for k in range(4))
        t_ee = ce * ca - se * sd + so * cb - co * sc
        t_eo = ce * cb + se * sc - so * ca - co * sd
        t_oe = ce * sa + se * cd + co * cc + so * sb
        t_oo = ce * sb - se * cc + co * cd - so * sa
        per = t_ref.shape[1]
        span = min(per, chunk)
        for j in range(chunk // span):
            rows_j = slice(j * span, (j + 1) * span)
            for first, left, right in (
                (ub * chunk + j * span, t_ee, t_eo),
                (HALF + ub * chunk + j * span, t_oe, t_oo),
            ):
                to = slice(first % per, first % per + span)
                t_ref[first // per, to, :HALF] = left[rows_j]
                t_ref[first // per, to, HALF:] = right[rows_j]
    for out, (ky, slots) in zip(outs, groups):
        for k, kz in enumerate(slots):
            source = (col_at ^ ky) * n_row + (row_at ^ kz)
            out[k] = t_ref[source].astype(BF16)
    slice_copy.wait()


def in_hbm(value):
    return pltpu.with_memory_space_constraint(value, pltpu.HBM)


def forward(index, charge, tiles, cotangent, incident, begin, n_row, n_col, groups):
    rows, cols = cotangent.shape[2:]
    block = min(256, rows)
    per = M // (n_row * n_col)
    out_shape = [jax.ShapeDtypeStruct((len(slots), per, M), BF16) for _, slots in groups]
    out_shape.append(jax.ShapeDtypeStruct((cols, M), BF16))
    out_shape.append(jax.ShapeDtypeStruct((rows // 2 - begin, cols), BF16))

    def kernel(*refs):
        forward_kernel(*refs, rows=rows, cols=cols, n_row=n_row, groups=groups, begin=begin)

    vmem = pl.BlockSpec(memory_space=pltpu.VMEM)
    outs = pl.pallas_call(
        kernel,
        in_specs=[vmem, vmem, pl.BlockSpec(memory_space=pltpu.SMEM)] + [pl.BlockSpec(memory_space=pltpu.HBM)] * 2,
        out_specs=[pl.BlockSpec(memory_space=pltpu.VMEM)] * len(out_shape),
        out_shape=out_shape,
        scratch_shapes=[
            pltpu.VMEM((M, rows), BF16),
            pltpu.VMEM((rows, 2 * M), BF16),
            pltpu.VMEM((2, HALF, HALF), F32),
            pltpu.VMEM((n_row * n_col, per, M), F32),
            pltpu.VMEM((2, rows, cols), BF16),
            pltpu.SemaphoreType.DMA((rows // block + 1,)),
        ],
        compiler_params=pltpu.CompilerParams(vmem_limit_bytes=36 << 20),
        cost_estimate=pl.CostEstimate(
            flops=2 * rows * 2 * M * (cols + M), bytes_accessed=4 * rows * cols, transcendentals=0
        ),
        name="forward",
    )(index.reshape(1, 1), charge.reshape(1, 1), tiles, in_hbm(cotangent), in_hbm(incident))
    return outs[:-2], outs[-2], outs[-1]


def swap(value, axis, bits):
    size = lax.axis_size(axis)
    return lax.ppermute(value, axis, [(i, i ^ bits) for i in range(size)])


def add_up(parts):
    total = parts[0].astype(F32)
    for part in parts[1:]:
        total = total + part.astype(F32)
    return total


def hop_order(n_row):
    return sorted(range(1, n_row), key=lambda k: -(k & -k))


def slot_groups(n_row, n_col):
    order = hop_order(n_row) + [0]
    if n_row <= 4:
        parts = [[kz] for kz in order]
    else:
        parts = [order[: n_row // 2], order[n_row // 2 :]]
    return [(ky, tuple(slots)) for slots in parts for ky in range(n_col)]


def reduce_blocks(parts, groups, n_row):
    reduced = {}
    for own, (ky, slots) in zip(parts, groups):
        if ky:
            continue
        terms = [own]
        for other, (step, other_slots) in zip(parts, groups):
            if step and other_slots == slots:
                terms.append(swap(other, "col", step))
        total = add_up(terms).astype(BF16)
        for k, kz in enumerate(slots):
            reduced[kz] = total[k]
    moved = [swap(reduced[kz], "row", kz) for kz in hop_order(n_row)]
    return add_up([reduced[0]] + moved).astype(BF16)


def gather_row(mine, n_row):
    found = {0: mine}
    for kz in hop_order(n_row):
        found[kz] = swap(mine, "row", kz)
    return [found[kz] for kz in range(n_row)]


def aligned(pieces):
    if any(piece.shape[0] % 16 for piece in pieces):
        return [jnp.concatenate(pieces, axis=0)]
    return pieces


def row_table_kernel(index_ref, row_tab, fine_ref, *, rows, n_row, n_col, full_rows, waves):
    extent = full_rows * n_row
    row_at = lax.axis_index("row")
    col_at = lax.axis_index("col")
    half_at = lax.rem(lax.axis_index("wl"), 2)
    per = M // (n_row * n_col)
    lane = lax.broadcasted_iota(jnp.int32, (16, M), 1)
    block = lane // per
    owner = ((block // n_row) ^ col_at) * n_row + ((block % n_row) ^ row_at)
    place = owner * per + lane % per
    is_sin = place >= HALF
    focal = 2.0 * jnp.where(is_sin, place - HALF, place).astype(F32) + 1.0
    for w in range(waves):
        period = quarter_period(index_ref[w])
        for side in range(2):
            lanes = slice(side * HALF, (side + 1) * HALF)
            sine = is_sin[:1, lanes]

            def write_row(at, amount, re, im, w=w, lanes=lanes, sine=sine):
                row_tab[w, at : at + amount, lanes] = jnp.where(
                    sine, im.astype(F32), re.astype(F32)
                ).astype(BF16)

            table_focal_lanes(
                write_row,
                period,
                row_at * full_rows + half_at * rows,
                extent,
                row_tab.shape[1],
                fine_ref,
                lanes=focal[:, lanes],
            )


def row_tables(indices, rows, n_row, n_col, full_rows):
    waves = indices.shape[0]
    own_rows = max(rows, 256)

    def kernel(*refs):
        row_table_kernel(*refs, rows=rows, n_row=n_row, n_col=n_col, full_rows=full_rows, waves=waves)

    return pl.pallas_call(
        kernel,
        in_specs=[pl.BlockSpec(memory_space=pltpu.SMEM)],
        out_specs=pl.BlockSpec(memory_space=pltpu.VMEM),
        out_shape=jax.ShapeDtypeStruct((waves, own_rows, M), BF16),
        scratch_shapes=[pltpu.VMEM((2, HALF, HALF), F32)],
        compiler_params=pltpu.CompilerParams(vmem_limit_bytes=16 << 20),
        cost_estimate=pl.CostEstimate(flops=40 * M * own_rows, bytes_accessed=4 * M * own_rows, transcendentals=0),
        name="row_tables",
    )(indices)


def col_table(index, cols, n_col):
    def kernel(index_ref, col_tab, fine_ref):
        def write_col(at, amount, re, im):
            col_tab[at : at + amount, :HALF] = re
            col_tab[at : at + amount, HALF:] = im

        table_focal_lanes(
            write_col,
            quarter_period(index_ref[0]),
            lax.axis_index("col") * cols,
            cols * n_col,
            cols,
            fine_ref,
        )

    return pl.pallas_call(
        kernel,
        in_specs=[pl.BlockSpec(memory_space=pltpu.SMEM)],
        out_specs=pl.BlockSpec(memory_space=pltpu.VMEM),
        out_shape=jax.ShapeDtypeStruct((cols, M), BF16),
        scratch_shapes=[pltpu.VMEM((2, HALF, HALF), F32)],
        compiler_params=pltpu.CompilerParams(vmem_limit_bytes=16 << 20),
        cost_estimate=pl.CostEstimate(flops=20 * M * cols, bytes_accessed=4 * M * cols, transcendentals=0),
        name="col_table",
    )(index)


def backward_kernel(tiles_ref, *refs, counts, wave_ids, part_first, chunks, tile_size, rows, emit):
    waves = len(counts)
    total_pieces = sum(counts)
    sources, refs = refs[:total_pieces], refs[total_pieces:]
    n_tables = 1 + max(table for table, _ in wave_ids)
    row_tabs, refs = refs[:n_tables], refs[n_tables:]
    col_tabs, refs = refs[:waves], refs[waves:]
    incidents, refs = refs[:waves], refs[waves:]
    outs, refs = refs[: len(chunks)], refs[len(chunks) :]
    held, sems = refs[emit : emit + 2]
    matrices = list(refs[:emit] + refs[emit + 2 :])
    half_at = lax.rem(lax.axis_index("wl"), 2)
    first = chunks[0][0]
    copies = []
    for k, (at, amount) in enumerate(chunks):
        for w in range(waves):
            if part_first[w] is None:
                span = pl.ds(pl.multiple_of(half_at * rows + at, 16), amount)
                source = incidents[w].at[0, span, :]
            else:
                source = incidents[w].at[pl.ds(at - part_first[w], amount), :]
            copies.append(
                pltpu.make_async_copy(source, held.at[w, pl.ds(at - first, amount), :], sems.at[k, w])
            )
            copies[-1].start()
    ready = []
    for w in range(waves):
        pieces, sources = sources[: counts[w]], sources[counts[w] :]
        if counts[w] == 1:
            ready.append(pieces[0])
            continue
        target = matrices.pop(0)
        at = 0
        for piece in pieces:
            target[at : at + piece.shape[0], :] = piece[...]
            at += piece.shape[0]
        ready.append(target)
    cols = outs[0].shape[1]
    wide = min(512, cols)
    amount = sum(n for _, n in chunks)
    back_y = [
        jnp.dot(
            row_tabs[table][which, first : first + amount, :], ready[w][...], preferred_element_type=F32
        ).astype(BF16)
        for w, (table, which) in enumerate(wave_ids)
    ]
    for copy in copies:
        copy.wait()
    for part in range(0, cols, wide):
        span = slice(part, part + wide)
        total = None
        for w in range(waves):
            back = lax.dot_general(
                back_y[w], col_tabs[w][span, :], (((1,), (1,)), ((), ())), preferred_element_type=F32
            )
            term = back * held[w, :, span].astype(F32)
            total = term if total is None else total + term
        for out, (at, size) in zip(outs, chunks):
            borders = [at] + list(range((at // tile_size + 1) * tile_size, at + size, tile_size)) + [at + size]
            for low, high in zip(borders, borders[1:]):
                mask = live_row(tiles_ref, half_at * (rows // tile_size) + low // tile_size, cols)[:, span]
                out[low - at : high - at, span] = (total[low - first : high - first] * mask).astype(BF16)


def backward(tiles, waves, chunks, tile_size, rows, keep=False):
    cols = tiles.shape[1] * tile_size
    flat = [piece for wave in waves for piece in wave[0]]
    amount = sum(n for _, n in chunks)
    counts = [len(wave[0]) for wave in waves]
    built = sum(count > 1 for count in counts)
    emit = built if keep else 0
    tables = []
    for wave in waves:
        if not any(wave[1] is table for table in tables):
            tables.append(wave[1])
    wave_ids = [([wave[1] is table for table in tables].index(True), wave[2]) for wave in waves]

    def kernel(*refs):
        backward_kernel(
            *refs,
            counts=counts,
            wave_ids=wave_ids,
            part_first=[wave[5] for wave in waves],
            chunks=chunks,
            tile_size=tile_size,
            rows=rows,
            emit=emit,
        )

    vmem = pl.BlockSpec(memory_space=pltpu.VMEM)
    hbm = pl.BlockSpec(memory_space=pl.ANY)
    out_shape = [jax.ShapeDtypeStruct((n, cols), BF16) for _, n in chunks]
    out_shape += [jax.ShapeDtypeStruct((M, M), BF16)] * emit
    outs = pl.pallas_call(
        kernel,
        in_specs=[pl.BlockSpec(memory_space=pltpu.SMEM)]
        + [vmem] * (len(flat) + len(tables) + len(waves))
        + [hbm] * len(waves),
        out_specs=[vmem] * len(out_shape),
        out_shape=out_shape,
        scratch_shapes=[
            pltpu.VMEM((len(waves), amount, cols), BF16),
            pltpu.SemaphoreType.DMA((len(chunks), len(waves))),
        ]
        + [pltpu.VMEM((M, M), BF16)] * (built - emit),
        compiler_params=pltpu.CompilerParams(vmem_limit_bytes=24 << 20),
        cost_estimate=pl.CostEstimate(
            flops=2 * len(waves) * amount * M * (cols + M), bytes_accessed=6 * amount * cols, transcendentals=0
        ),
    )(tiles, *flat, *tables, *[wave[3] for wave in waves], *[wave[4] for wave in waves])
    return outs[: len(chunks)], outs[len(chunks) :]


def place_kernel(*refs, chunks, rows):
    sources = refs[: 2 * len(chunks)]
    out, sems = refs[-2:]
    half_at = lax.rem(lax.axis_index("wl"), 2)
    copies = []
    for k, (at, amount) in enumerate(chunks):
        for side in range(2):
            where = half_at if side == 0 else 1 - half_at
            target = out.at[pl.ds(pl.multiple_of(where * rows + at, 16), amount), :]
            copies.append(pltpu.make_async_copy(sources[2 * k + side], target, sems.at[k, side]))
    for copy in copies:
        copy.start()
    for copy in copies:
        copy.wait()


def place(done, chunks, rows, into=None):
    flat = [part for pair in done for part in pair]
    cols = flat[0].shape[1]
    operands = flat + ([into] if into is not None else [])

    def kernel(*refs):
        place_kernel(*refs, chunks=chunks, rows=rows)

    hbm = pl.BlockSpec(memory_space=pl.ANY)
    return pl.pallas_call(
        kernel,
        in_specs=[hbm] * len(operands),
        out_specs=hbm,
        out_shape=jax.ShapeDtypeStruct((2 * rows, cols), BF16),
        scratch_shapes=[pltpu.SemaphoreType.DMA((len(chunks), 2))],
        input_output_aliases={len(flat): 0} if into is not None else {},
        compiler_params=pltpu.CompilerParams(vmem_limit_bytes=1 << 20),
        cost_estimate=pl.CostEstimate(flops=0, bytes_accessed=4 * cols * sum(n for _, n in chunks), transcendentals=0),
    )(*operands)


def own_slice(incident, begin):
    amount, cols = incident.shape[1] // 2 - begin, incident.shape[2]

    def kernel(source, out, sem):
        copy = slice_rows(source, out, sem, lax.rem(lax.axis_index("wl"), 2), begin)
        copy.start()
        copy.wait()

    return pl.pallas_call(
        kernel,
        in_specs=[pl.BlockSpec(memory_space=pltpu.HBM)],
        out_specs=pl.BlockSpec(memory_space=pltpu.VMEM),
        out_shape=jax.ShapeDtypeStruct((amount, cols), BF16),
        scratch_shapes=[pltpu.SemaphoreType.DMA],
        compiler_params=pltpu.CompilerParams(vmem_limit_bytes=4 << 20),
        cost_estimate=pl.CostEstimate(flops=0, bytes_accessed=4 * amount * cols, transcendentals=0),
        name="own_slice",
    )(in_hbm(incident))


BOUNDS = (0, 4, 7, 9, 13, 16)
EXCHANGED = 3


def all_steps(cotangent, incident, tiles, charge, wl_index):
    rows, cols = cotangent.shape[2:]
    n_row = lax.axis_size("row")
    n_col = lax.axis_size("col")
    tile_size = rows // tiles.shape[0]
    half = rows // 2
    bounds = [half * bound // 16 // 16 * 16 for bound in BOUNDS]
    chunks = [(low, high - low) for low, high in zip(bounds, bounds[1:])]
    n_first = EXCHANGED
    split = chunks[n_first][0]

    inc_straight = swap(own_slice(incident, split), "wl", 2)
    groups = slot_groups(n_row, n_col)
    parts, col_own, slice_other = forward(
        wl_index, charge, tiles, cotangent, incident, split, n_row, n_col, groups
    )
    mine = reduce_blocks(parts, groups, n_row)
    inc_core = swap(incident, "wl", 1)
    inc_cross = swap(slice_other, "wl", 3)
    col_core = swap(col_own, "wl", 1)
    near = jnp.concatenate([wl_index, swap(wl_index, "wl", 1)])
    far = swap(wl_index, "wl", 2)
    far_core = swap(far, "wl", 1)
    row_near = row_tables(near, half, n_row, n_col, rows)
    row_far = row_tables(jnp.concatenate([far, far_core]), half, n_row, n_col, rows)
    col_straight = col_table(far, cols, n_col)
    col_cross = swap(col_straight, "wl", 1)

    here = gather_row(mine, n_row)
    if n_row > 4:
        here = [jnp.concatenate(here, axis=0)]
    joined = jnp.concatenate(here, axis=0)
    pieces, pieces_core = [joined], [swap(joined, "wl", 1)]
    for ky in range(1, n_col):
        for piece in here:
            pieces.append(swap(piece, "col", ky))
            pieces_core.append(swap(pieces[-1], "wl", 1))

    straight = [swap(joined, "wl", 2)]
    straight += [swap(straight[0], "col", ky) for ky in range(1, n_col)]
    cross = [swap(piece, "wl", 1) for piece in straight]

    own = (aligned(pieces), row_near, 0, col_own, incident, None)
    mate = (aligned(pieces_core), row_near, 1, col_core, inc_core, None)
    first, matrices = backward(tiles, [own, mate], chunks[:1], tile_size, half, keep=True)
    if len(matrices) == 2:
        own = ([matrices[0]],) + own[1:]
        mate = ([matrices[1]],) + mate[1:]
    second, _ = backward(tiles, [own, mate], chunks[1:n_first], tile_size, half)
    straight = (aligned(straight), row_far, 0, col_straight, inc_straight, split)
    cross = (aligned(cross), row_far, 1, col_cross, inc_cross, split)
    both, _ = backward(tiles, [own, mate, straight, cross], chunks[n_first:], tile_size, half)
    done = []
    for pair in list(first) + list(second):
        total = add_up([pair, swap(pair, "wl", 2)]).astype(BF16)
        done.append((total, swap(total, "wl", 1)))
    ready = [(part, swap(part, "wl", 1)) for part in both]
    result = place(ready, chunks[n_first:], half)
    result = place(done[:-1], chunks[: n_first - 1], half, result)
    return place(done[-1:], chunks[n_first - 1 : n_first], half, result)


def solution(mesh):
    return jax.shard_map(
        all_steps,
        mesh=mesh,
        in_specs=(
            P("wl", None, "row", "col"),
            P("wl", "row", "col"),
            P("row", "col"),
            P("wl"),
            P("wl"),
        ),
        out_specs=P("row", "col"),
        check_vma=False,
    )
```

```python
import math

import jax
import jax.numpy as jnp
from jax import lax
from jax.experimental import pallas as pl
from jax.experimental.pallas import tpu as pltpu
from jax.sharding import PartitionSpec as P


M = 512
HALF = M // 2
F32 = jnp.float32
BF16 = jnp.bfloat16


def iota(shape, axis):
    return lax.broadcasted_iota(jnp.int32, shape, axis).astype(F32)


def unit_phasor(product, period):
    turns = jnp.floor(product / period + 0.5)
    rest = product - turns * period
    quarter = jnp.floor(4.0 * rest / period + 0.5)
    theta = (4.0 * rest - quarter * period) / period * (0.5 * math.pi)
    sq = theta * theta
    sin_p = theta * (
        1.0 + sq * (-1.0 / 6.0 + sq * (1.0 / 120.0 + sq * (-1.0 / 5040.0 + sq / 362880.0)))
    )
    cos_p = 1.0 + sq * (
        -0.5 + sq * (1.0 / 24.0 + sq * (-1.0 / 720.0 + sq * (1.0 / 40320.0 - sq / 3628800.0)))
    )
    size = jnp.abs(quarter)
    odd = size == 1.0
    flip = jnp.where(size == 2.0, -1.0, 1.0)
    side = jnp.where(quarter < 0.0, -1.0, 1.0)
    cosine = jnp.where(odd, -side * sin_p, flip * cos_p)
    sine = jnp.where(odd, side * cos_p, flip * sin_p)
    return cosine, sine


def turn(first, second):
    c1, s1 = first
    c2, s2 = second
    return c1 * c2 - s1 * s2, s1 * c2 + c1 * s2


def quarter_period(index_value):
    return ((index_value + 32) * (M // 4)).astype(F32)


def table_focal_lanes(write, period, first, extent, amount, fine_ref, lanes=None, lane_count=HALF):
    block = 256
    focal = 2.0 * iota((16, lane_count), 1) + 1.0 if lanes is None else lanes
    step = iota((16, lane_count), 0)
    fine = unit_phasor(2.0 * step * focal, jnp.broadcast_to(period, (16, lane_count)))
    mid = unit_phasor(32.0 * step * focal, jnp.broadcast_to(period, (16, lane_count)))
    for b in range(16):
        re, im = turn((mid[0][b : b + 1], mid[1][b : b + 1]), fine)
        fine_ref[0, 16 * b : 16 * b + 16, :] = re
        fine_ref[1, 16 * b : 16 * b + 16, :] = im
    count = amount // block
    start = (2 * first - extent + 1).astype(F32)
    top = -(-count // 8) * 8
    focal_top = 2.0 * iota((top, lane_count), 1) + 1.0 if lanes is None else jnp.broadcast_to(lanes[:1], (top, lane_count))
    coarse = unit_phasor(
        (start + 2.0 * block * iota((top, lane_count), 0)) * focal_top,
        jnp.broadcast_to(period, (top, lane_count)),
    )
    for a in range(count):
        for part in range(0, block, 64):
            re, im = turn(
                (coarse[0][a : a + 1], coarse[1][a : a + 1]),
                (fine_ref[0, part : part + 64, :], fine_ref[1, part : part + 64, :]),
            )
            write(a * block + part, 64, re.astype(BF16), im.astype(BF16))


def table_pupil_lanes(write, period, first, extent, amount, fine_ref, focal_first, focal_count):
    count = amount // 128
    shape = (focal_count, 128)
    focal = 2.0 * (focal_first + iota(shape, 0)) + 1.0
    lane = iota(shape, 1)
    full = jnp.broadcast_to(period, shape)
    fine = unit_phasor(2.0 * lane * focal, full)
    fine_ref[0, :focal_count, :128] = fine[0]
    fine_ref[1, :focal_count, :128] = fine[1]
    start = (2 * first - extent + 1).astype(F32)
    coarse = unit_phasor((start + 256.0 * lane) * focal, full)
    fine_ref[0, :focal_count, 128:] = coarse[0]
    fine_ref[1, :focal_count, 128:] = coarse[1]
    for a in range(count):
        for part in range(0, focal_count, 64):
            rows = slice(part, min(part + 64, focal_count))
            re, im = turn(
                (fine_ref[0, rows, 128 + a : 129 + a], fine_ref[1, rows, 128 + a : 129 + a]),
                (fine_ref[0, rows, :128], fine_ref[1, rows, :128]),
            )
            write(part, a * 128, re.astype(BF16), im.astype(BF16))


def live_row(tiles_ref, tile_row, cells):
    tile_cols = tiles_ref.shape[1]
    width = cells // tile_cols
    parts = [
        jnp.full((1, width), jnp.where(tiles_ref[tile_row, j] == 1, 1.0, 0.0), F32)
        for j in range(tile_cols)
    ]
    return jnp.concatenate(parts, axis=1)


def slice_rows(source, target, sem, which, begin):
    span = pl.ds(pl.multiple_of(which * (source.shape[1] // 2) + begin, 16), target.shape[0])
    return pltpu.make_async_copy(source.at[0, span, :], target, sem)


def forward_kernel(index_ref, charge_ref, tiles_ref, cot_ref, inc_ref, *refs, rows, cols, n_row, groups, begin):
    outs, (col_tab, slice_ref) = refs[:-8], refs[-8:-6]
    row_tab, inner, fine_ref, t_ref, held, sems = refs[-6:]
    block = min(256, rows)
    extent = rows * n_row
    row_at = lax.axis_index("row")
    col_at = lax.axis_index("col")
    tile_size = rows // tiles_ref.shape[0]
    copies = []
    for step in range(rows // block):
        span = pl.ds(step * block, block)
        copies.append(pltpu.make_async_copy(cot_ref.at[0, :, span, :], held.at[:, span, :], sems.at[step]))
        copies[-1].start()
    half_at = lax.rem(lax.axis_index("wl"), 2)
    slice_copy = slice_rows(inc_ref, slice_ref, sems.at[rows // block], 1 - half_at, begin)
    slice_copy.start()
    period = quarter_period(index_ref[0])

    def write_col(at, amount, re, im):
        col_tab[at : at + amount, :HALF] = re
        col_tab[at : at + amount, HALF:] = im

    table_focal_lanes(write_col, period, col_at * cols, extent, cols, fine_ref)

    def write_row(part, at, re, im):
        row_tab[part : part + 64, at : at + 128] = re
        row_tab[HALF + part : HALF + part + 64, at : at + 128] = im

    table_pupil_lanes(write_row, period, row_at * rows, extent, rows, fine_ref, 0.0, HALF)

    for step in range(rows // block):
        copies[step].wait()
        halves = []
        for part in range(2):
            for at in range(step * block, (step + 1) * block, tile_size):
                mask = live_row(tiles_ref, at // tile_size, cols).astype(BF16)
                halves.append(held[part, at : at + tile_size, :] * mask)
        prod = jnp.dot(jnp.concatenate(halves, axis=0), col_tab[...], preferred_element_type=F32)
        at = step * block
        inner[at : at + block, :M] = prod[:block].astype(BF16)
        inner[at : at + block, M:] = prod[block:].astype(BF16)

    charge = charge_ref[0]
    even = jnp.where(charge % 2 == 0, 1.0, 0.0).astype(F32)
    odd = 1.0 - even
    scale = 4.0 / (extent * M)
    chunk = 128
    shape = (chunk, HALF)
    for ub in range(HALF // chunk):
        both = jnp.concatenate(
            [row_tab[ub * chunk : (ub + 1) * chunk, :], row_tab[HALF + ub * chunk : HALF + (ub + 1) * chunk, :]],
            axis=0,
        )
        q = jnp.dot(both, inner[...], preferred_element_type=F32)
        q_c, q_s = q[:chunk], q[chunk:]
        u = 2.0 * (iota(shape, 0) + float(ub * chunk)) + 1.0
        v = 2.0 * iota(shape, 1) + 1.0
        inv = 1.0 / jnp.sqrt(u * u + v * v)
        power = (u * inv, v * inv)
        total = (jnp.full(shape, scale, F32), jnp.zeros(shape, F32))
        for bit in range(4):
            taken = (charge >> bit) % 2 == 1
            multiplied = turn(total, power)
            total = tuple(jnp.where(taken, new, old) for new, old in zip(multiplied, total))
            power = turn(power, power)
        c, s = total
        ce, se, co, so = c * even, s * even, c * odd, s * odd
        ca, cb, cc, cd = (q_c[:, k * HALF : (k + 1) * HALF] for k in range(4))
        sa, sb, sc, sd = (q_s[:, k * HALF : (k + 1) * HALF] for k in range(4))
        t_ee = ce * ca - se * sd + so * cb - co * sc
        t_eo = ce * cb + se * sc - so * ca - co * sd
        t_oe = ce * sa + se * cd + co * cc + so * sb
        t_oo = ce * sb - se * cc + co * cd - so * sa
        per = t_ref.shape[1]
        span = min(per, chunk)
        for j in range(chunk // span):
            rows_j = slice(j * span, (j + 1) * span)
            for first, left, right in (
                (ub * chunk + j * span, t_ee, t_eo),
                (HALF + ub * chunk + j * span, t_oe, t_oo),
            ):
                to = slice(first % per, first % per + span)
                t_ref[first // per, to, :HALF] = left[rows_j]
                t_ref[first // per, to, HALF:] = right[rows_j]
    for out, (ky, slots) in zip(outs, groups):
        for k, kz in enumerate(slots):
            source = (col_at ^ ky) * n_row + (row_at ^ kz)
            out[k] = t_ref[source].astype(BF16)
    slice_copy.wait()


def in_hbm(value):
    return pltpu.with_memory_space_constraint(value, pltpu.HBM)


def forward(index, charge, tiles, cotangent, incident, begin, n_row, n_col, groups):
    rows, cols = cotangent.shape[2:]
    block = min(256, rows)
    per = M // (n_row * n_col)
    out_shape = [jax.ShapeDtypeStruct((len(slots), per, M), BF16) for _, slots in groups]
    out_shape.append(jax.ShapeDtypeStruct((cols, M), BF16))
    out_shape.append(jax.ShapeDtypeStruct((rows // 2 - begin, cols), BF16))

    def kernel(*refs):
        forward_kernel(*refs, rows=rows, cols=cols, n_row=n_row, groups=groups, begin=begin)

    hbm, smem = pl.BlockSpec(memory_space=pltpu.HBM), pl.BlockSpec(memory_space=pltpu.SMEM)
    outs = pl.pallas_call(
        kernel,
        in_specs=[smem, smem, smem, hbm, hbm],
        out_specs=[pl.BlockSpec(memory_space=pltpu.VMEM)] * len(out_shape),
        out_shape=out_shape,
        scratch_shapes=[
            pltpu.VMEM((M, rows), BF16),
            pltpu.VMEM((rows, 2 * M), BF16),
            pltpu.VMEM((2, HALF, HALF), F32),
            pltpu.VMEM((n_row * n_col, per, M), F32),
            pltpu.VMEM((2, rows, cols), BF16),
            pltpu.SemaphoreType.DMA((rows // block + 1,)),
        ],
        compiler_params=pltpu.CompilerParams(vmem_limit_bytes=36 << 20),
        cost_estimate=pl.CostEstimate(
            flops=2 * rows * 2 * M * (cols + M), bytes_accessed=4 * rows * cols, transcendentals=0
        ),
        name="forward",
    )(index, charge, tiles, in_hbm(cotangent), in_hbm(incident))
    return outs[:-2], outs[-2], outs[-1]


def swap(value, axis, bits):
    size = lax.axis_size(axis)
    return lax.ppermute(value, axis, [(i, i ^ bits) for i in range(size)])


def add_up(parts):
    total = parts[0].astype(F32)
    for part in parts[1:]:
        total = total + part.astype(F32)
    return total


def hop_order(n_row):
    return sorted(range(1, n_row), key=lambda k: -(k & -k))


def slot_groups(n_row, n_col):
    order = hop_order(n_row) + [0]
    if n_row <= 4:
        parts = [order[:1], order[1:]]
    else:
        parts = [order[: n_row // 2], order[n_row // 2 :]]
    return [(ky, tuple(slots)) for slots in parts for ky in range(n_col)]


def reduce_blocks(parts, groups, n_row):
    reduced = {}
    for own, (ky, slots) in zip(parts, groups):
        if ky:
            continue
        terms = [own]
        for other, (step, other_slots) in zip(parts, groups):
            if step and other_slots == slots:
                terms.append(swap(other, "col", step))
        total = add_up(terms).astype(BF16)
        for k, kz in enumerate(slots):
            reduced[kz] = total[k]
    moved = [swap(reduced[kz], "row", kz) for kz in hop_order(n_row)]
    return add_up([reduced[0]] + moved).astype(BF16)


def gather_row(mine, n_row):
    found = {0: mine}
    for kz in hop_order(n_row):
        found[kz] = swap(mine, "row", kz)
    return [found[kz] for kz in range(n_row)]


def aligned(pieces):
    if any(piece.shape[0] % 16 for piece in pieces):
        return [jnp.concatenate(pieces, axis=0)]
    return pieces


def row_table_kernel(index_ref, row_tab, fine_ref, *, rows, n_row, n_col, full_rows, waves):
    extent = full_rows * n_row
    row_at = lax.axis_index("row")
    col_at = lax.axis_index("col")
    half_at = lax.rem(lax.axis_index("wl"), 2)
    per = M // (n_row * n_col)
    lane = lax.broadcasted_iota(jnp.int32, (16, M), 1)
    block = lane // per
    owner = ((block // n_row) ^ col_at) * n_row + ((block % n_row) ^ row_at)
    place = owner * per + lane % per
    is_sin = place >= HALF
    focal = 2.0 * jnp.where(is_sin, place - HALF, place).astype(F32) + 1.0
    for w in range(waves):
        period = quarter_period(index_ref[w])
        for side in range(2):
            lanes = slice(side * HALF, (side + 1) * HALF)
            sine = is_sin[:1, lanes]

            def write_row(at, amount, re, im, w=w, lanes=lanes, sine=sine):
                row_tab[w, at : at + amount, lanes] = jnp.where(
                    sine, im.astype(F32), re.astype(F32)
                ).astype(BF16)

            table_focal_lanes(
                write_row,
                period,
                row_at * full_rows + half_at * rows,
                extent,
                row_tab.shape[1],
                fine_ref,
                lanes=focal[:, lanes],
            )


def row_tables(indices, rows, n_row, n_col, full_rows):
    waves = indices.shape[0]
    own_rows = max(rows, 256)

    def kernel(*refs):
        row_table_kernel(*refs, rows=rows, n_row=n_row, n_col=n_col, full_rows=full_rows, waves=waves)

    return pl.pallas_call(
        kernel,
        in_specs=[pl.BlockSpec(memory_space=pltpu.SMEM)],
        out_specs=pl.BlockSpec(memory_space=pltpu.VMEM),
        out_shape=jax.ShapeDtypeStruct((waves, own_rows, M), BF16),
        scratch_shapes=[pltpu.VMEM((2, HALF, HALF), F32)],
        compiler_params=pltpu.CompilerParams(vmem_limit_bytes=16 << 20),
        cost_estimate=pl.CostEstimate(flops=40 * M * own_rows, bytes_accessed=4 * M * own_rows, transcendentals=0),
        name="row_tables",
    )(indices)


def col_table(index, cols, n_col):
    def kernel(index_ref, col_tab, fine_ref):
        def write_col(at, amount, re, im):
            col_tab[at : at + amount, :HALF] = re
            col_tab[at : at + amount, HALF:] = im

        table_focal_lanes(
            write_col,
            quarter_period(index_ref[0]),
            lax.axis_index("col") * cols,
            cols * n_col,
            cols,
            fine_ref,
        )

    return pl.pallas_call(
        kernel,
        in_specs=[pl.BlockSpec(memory_space=pltpu.SMEM)],
        out_specs=pl.BlockSpec(memory_space=pltpu.VMEM),
        out_shape=jax.ShapeDtypeStruct((cols, M), BF16),
        scratch_shapes=[pltpu.VMEM((2, HALF, HALF), F32)],
        compiler_params=pltpu.CompilerParams(vmem_limit_bytes=16 << 20),
        cost_estimate=pl.CostEstimate(flops=20 * M * cols, bytes_accessed=4 * M * cols, transcendentals=0),
        name="col_table",
    )(index)


def backward_kernel(tiles_ref, *refs, counts, wave_ids, part_first, chunks, tile_size, rows, emit):
    waves = len(counts)
    total_pieces = sum(counts)
    sources, refs = refs[:total_pieces], refs[total_pieces:]
    n_tables = 1 + max(table for table, _ in wave_ids)
    row_tabs, refs = refs[:n_tables], refs[n_tables:]
    col_tabs, refs = refs[:waves], refs[waves:]
    incidents, refs = refs[:waves], refs[waves:]
    outs, refs = refs[: len(chunks)], refs[len(chunks) :]
    held, sems = refs[emit : emit + 2]
    matrices = list(refs[:emit] + refs[emit + 2 :])
    half_at = lax.rem(lax.axis_index("wl"), 2)
    first = chunks[0][0]
    copies = []
    for k, (at, amount) in enumerate(chunks):
        for w in range(waves):
            if part_first[w] is None:
                span = pl.ds(pl.multiple_of(half_at * rows + at, 16), amount)
                source = incidents[w].at[0, span, :]
            else:
                source = incidents[w].at[pl.ds(at - part_first[w], amount), :]
            copies.append(
                pltpu.make_async_copy(source, held.at[w, pl.ds(at - first, amount), :], sems.at[k, w])
            )
            copies[-1].start()
    ready = []
    for w in range(waves):
        pieces, sources = sources[: counts[w]], sources[counts[w] :]
        if counts[w] == 1:
            ready.append(pieces[0])
            continue
        target = matrices.pop(0)
        at = 0
        for piece in pieces:
            target[at : at + piece.shape[0], :] = piece[...]
            at += piece.shape[0]
        ready.append(target)
    cols = outs[0].shape[1]
    wide = min(512, cols)
    amount = sum(n for _, n in chunks)
    back_y = [
        jnp.dot(
            row_tabs[table][which, first : first + amount, :], ready[w][...], preferred_element_type=F32
        ).astype(BF16)
        for w, (table, which) in enumerate(wave_ids)
    ]
    for copy in copies:
        copy.wait()
    for part in range(0, cols, wide):
        span = slice(part, part + wide)
        total = None
        for w in range(waves):
            back = lax.dot_general(
                back_y[w], col_tabs[w][span, :], (((1,), (1,)), ((), ())), preferred_element_type=F32
            )
            term = back * held[w, :, span].astype(F32)
            total = term if total is None else total + term
        for out, (at, size) in zip(outs, chunks):
            borders = [at] + list(range((at // tile_size + 1) * tile_size, at + size, tile_size)) + [at + size]
            for low, high in zip(borders, borders[1:]):
                mask = live_row(tiles_ref, half_at * (rows // tile_size) + low // tile_size, cols)[:, span]
                out[low - at : high - at, span] = (total[low - first : high - first] * mask).astype(BF16)


def backward(tiles, waves, chunks, tile_size, rows, keep=False):
    cols = tiles.shape[1] * tile_size
    flat = [piece for wave in waves for piece in wave[0]]
    amount = sum(n for _, n in chunks)
    counts = [len(wave[0]) for wave in waves]
    built = sum(count > 1 for count in counts)
    emit = built if keep else 0
    tables = []
    for wave in waves:
        if not any(wave[1] is table for table in tables):
            tables.append(wave[1])
    wave_ids = [([wave[1] is table for table in tables].index(True), wave[2]) for wave in waves]

    def kernel(*refs):
        backward_kernel(
            *refs,
            counts=counts,
            wave_ids=wave_ids,
            part_first=[wave[5] for wave in waves],
            chunks=chunks,
            tile_size=tile_size,
            rows=rows,
            emit=emit,
        )

    vmem = pl.BlockSpec(memory_space=pltpu.VMEM)
    hbm = pl.BlockSpec(memory_space=pl.ANY)
    out_shape = [jax.ShapeDtypeStruct((n, cols), BF16) for _, n in chunks]
    out_shape += [jax.ShapeDtypeStruct((M, M), BF16)] * emit
    outs = pl.pallas_call(
        kernel,
        in_specs=[pl.BlockSpec(memory_space=pltpu.SMEM)]
        + [vmem] * (len(flat) + len(tables) + len(waves))
        + [hbm] * len(waves),
        out_specs=[vmem] * len(out_shape),
        out_shape=out_shape,
        scratch_shapes=[
            pltpu.VMEM((len(waves), amount, cols), BF16),
            pltpu.SemaphoreType.DMA((len(chunks), len(waves))),
        ]
        + [pltpu.VMEM((M, M), BF16)] * (built - emit),
        compiler_params=pltpu.CompilerParams(vmem_limit_bytes=24 << 20),
        cost_estimate=pl.CostEstimate(
            flops=2 * len(waves) * amount * M * (cols + M), bytes_accessed=6 * amount * cols, transcendentals=0
        ),
    )(tiles, *flat, *tables, *[wave[3] for wave in waves], *[wave[4] for wave in waves])
    return outs[: len(chunks)], outs[len(chunks) :]


def place_kernel(*refs, chunks, rows):
    sources = refs[: 2 * len(chunks)]
    out, sems = refs[-2:]
    half_at = lax.rem(lax.axis_index("wl"), 2)
    copies = []
    for k, (at, amount) in enumerate(chunks):
        for side in range(2):
            where = half_at if side == 0 else 1 - half_at
            target = out.at[pl.ds(pl.multiple_of(where * rows + at, 16), amount), :]
            copies.append(pltpu.make_async_copy(sources[2 * k + side], target, sems.at[k, side]))
    for copy in copies:
        copy.start()
    for copy in copies:
        copy.wait()


def place(done, chunks, rows, into=None):
    flat = [part for pair in done for part in pair]
    cols = flat[0].shape[1]
    operands = flat + ([into] if into is not None else [])

    def kernel(*refs):
        place_kernel(*refs, chunks=chunks, rows=rows)

    hbm = pl.BlockSpec(memory_space=pl.ANY)
    return pl.pallas_call(
        kernel,
        in_specs=[hbm] * len(operands),
        out_specs=hbm,
        out_shape=jax.ShapeDtypeStruct((2 * rows, cols), BF16),
        scratch_shapes=[pltpu.SemaphoreType.DMA((len(chunks), 2))],
        input_output_aliases={len(flat): 0} if into is not None else {},
        compiler_params=pltpu.CompilerParams(vmem_limit_bytes=1 << 20),
        cost_estimate=pl.CostEstimate(flops=0, bytes_accessed=4 * cols * sum(n for _, n in chunks), transcendentals=0),
    )(*operands)


def own_slice(incident, begin):
    amount, cols = incident.shape[1] // 2 - begin, incident.shape[2]

    def kernel(source, out, sem):
        copy = slice_rows(source, out, sem, lax.rem(lax.axis_index("wl"), 2), begin)
        copy.start()
        copy.wait()

    return pl.pallas_call(
        kernel,
        in_specs=[pl.BlockSpec(memory_space=pltpu.HBM)],
        out_specs=pl.BlockSpec(memory_space=pltpu.VMEM),
        out_shape=jax.ShapeDtypeStruct((amount, cols), BF16),
        scratch_shapes=[pltpu.SemaphoreType.DMA],
        compiler_params=pltpu.CompilerParams(vmem_limit_bytes=4 << 20),
        cost_estimate=pl.CostEstimate(flops=0, bytes_accessed=4 * amount * cols, transcendentals=0),
        name="own_slice",
    )(in_hbm(incident))


BOUNDS = (0, 4, 7, 9, 13, 16)
EXCHANGED = 3


def all_steps(cotangent, incident, tiles, charge, wl_index):
    rows, cols = cotangent.shape[2:]
    n_row = lax.axis_size("row")
    n_col = lax.axis_size("col")
    tile_size = rows // tiles.shape[0]
    half = rows // 2
    bounds = [half * bound // 16 // 16 * 16 for bound in BOUNDS]
    chunks = [(low, high - low) for low, high in zip(bounds, bounds[1:])]
    n_first = EXCHANGED
    split = chunks[n_first][0]

    inc_straight = swap(own_slice(incident, split), "wl", 2)
    groups = slot_groups(n_row, n_col)
    parts, col_own, slice_other = forward(
        wl_index, charge, tiles, cotangent, incident, split, n_row, n_col, groups
    )
    mine = reduce_blocks(parts, groups, n_row)
    inc_core = swap(incident, "wl", 1)
    inc_cross = swap(slice_other, "wl", 3)
    col_core = swap(col_own, "wl", 1)
    near = jnp.concatenate([wl_index, swap(wl_index, "wl", 1)])
    far = swap(wl_index, "wl", 2)
    far_core = swap(far, "wl", 1)
    row_near = row_tables(near, half, n_row, n_col, rows)
    row_far = row_tables(jnp.concatenate([far, far_core]), half, n_row, n_col, rows)
    col_straight = col_table(far, cols, n_col)
    col_cross = swap(col_straight, "wl", 1)

    here = gather_row(mine, n_row)
    if n_row > 4:
        here = [jnp.concatenate(here, axis=0)]
    joined = jnp.concatenate(here, axis=0)
    pieces, pieces_core = [joined], [swap(joined, "wl", 1)]
    for ky in range(1, n_col):
        for piece in here:
            pieces.append(swap(piece, "col", ky))
            pieces_core.append(swap(pieces[-1], "wl", 1))

    straight = [swap(joined, "wl", 2)]
    straight += [swap(straight[0], "col", ky) for ky in range(1, n_col)]
    cross = [swap(piece, "wl", 1) for piece in straight]

    own = (aligned(pieces), row_near, 0, col_own, incident, None)
    mate = (aligned(pieces_core), row_near, 1, col_core, inc_core, None)
    first, matrices = backward(tiles, [own, mate], chunks[:1], tile_size, half, keep=True)
    if len(matrices) == 2:
        own = ([matrices[0]],) + own[1:]
        mate = ([matrices[1]],) + mate[1:]
    second, _ = backward(tiles, [own, mate], chunks[1:n_first], tile_size, half)
    straight = (aligned(straight), row_far, 0, col_straight, inc_straight, split)
    cross = (aligned(cross), row_far, 1, col_cross, inc_cross, split)
    both, _ = backward(tiles, [own, mate, straight, cross], chunks[n_first:], tile_size, half)
    done = []
    for pair in list(first) + list(second):
        total = add_up([pair, swap(pair, "wl", 2)]).astype(BF16)
        done.append((total, swap(total, "wl", 1)))
    ready = [(part, swap(part, "wl", 1)) for part in both]
    result = place(ready, chunks[n_first:], half)
    result = place(done[:-1], chunks[: n_first - 1], half, result)
    return place(done[-1:], chunks[n_first - 1 : n_first], half, result)


def solution(mesh):
    return jax.shard_map(
        all_steps,
        mesh=mesh,
        in_specs=(
            P("wl", None, "row", "col"),
            P("wl", "row", "col"),
            P("row", "col"),
            P("wl"),
            P("wl"),
        ),
        out_specs=P("row", "col"),
        check_vma=False,
    )
```

```python
import math

import jax
import jax.numpy as jnp
from jax import lax
from jax.experimental import pallas as pl
from jax.experimental.pallas import tpu as pltpu
from jax.sharding import PartitionSpec as P


M = 512
HALF = M // 2
F32 = jnp.float32
BF16 = jnp.bfloat16


def iota(shape, axis):
    return lax.broadcasted_iota(jnp.int32, shape, axis).astype(F32)


def unit_phasor(product, period):
    turns = jnp.floor(product / period + 0.5)
    rest = product - turns * period
    quarter = jnp.floor(4.0 * rest / period + 0.5)
    theta = (4.0 * rest - quarter * period) / period * (0.5 * math.pi)
    sq = theta * theta
    sin_p = theta * (
        1.0 + sq * (-1.0 / 6.0 + sq * (1.0 / 120.0 + sq * (-1.0 / 5040.0 + sq / 362880.0)))
    )
    cos_p = 1.0 + sq * (
        -0.5 + sq * (1.0 / 24.0 + sq * (-1.0 / 720.0 + sq * (1.0 / 40320.0 - sq / 3628800.0)))
    )
    size = jnp.abs(quarter)
    odd = size == 1.0
    flip = jnp.where(size == 2.0, -1.0, 1.0)
    side = jnp.where(quarter < 0.0, -1.0, 1.0)
    cosine = jnp.where(odd, -side * sin_p, flip * cos_p)
    sine = jnp.where(odd, side * cos_p, flip * sin_p)
    return cosine, sine


def turn(first, second):
    c1, s1 = first
    c2, s2 = second
    return c1 * c2 - s1 * s2, s1 * c2 + c1 * s2


def quarter_period(index_value):
    return ((index_value + 32) * (M // 4)).astype(F32)


def table_focal_lanes(write, period, first, extent, amount, fine_ref, lanes=None, lane_count=HALF):
    block = 256
    focal = 2.0 * iota((16, lane_count), 1) + 1.0 if lanes is None else lanes
    step = iota((16, lane_count), 0)
    fine = unit_phasor(2.0 * step * focal, jnp.broadcast_to(period, (16, lane_count)))
    mid = unit_phasor(32.0 * step * focal, jnp.broadcast_to(period, (16, lane_count)))
    for b in range(16):
        re, im = turn((mid[0][b : b + 1], mid[1][b : b + 1]), fine)
        fine_ref[0, 16 * b : 16 * b + 16, :] = re
        fine_ref[1, 16 * b : 16 * b + 16, :] = im
    count = amount // block
    start = (2 * first - extent + 1).astype(F32)
    top = -(-count // 8) * 8
    focal_top = 2.0 * iota((top, lane_count), 1) + 1.0 if lanes is None else jnp.broadcast_to(lanes[:1], (top, lane_count))
    coarse = unit_phasor(
        (start + 2.0 * block * iota((top, lane_count), 0)) * focal_top,
        jnp.broadcast_to(period, (top, lane_count)),
    )
    for a in range(count):
        for part in range(0, block, 64):
            re, im = turn(
                (coarse[0][a : a + 1], coarse[1][a : a + 1]),
                (fine_ref[0, part : part + 64, :], fine_ref[1, part : part + 64, :]),
            )
            write(a * block + part, 64, re.astype(BF16), im.astype(BF16))


def table_pupil_lanes(write, period, first, extent, amount, fine_ref, focal_first, focal_count):
    count = amount // 128
    shape = (focal_count, 128)
    focal = 2.0 * (focal_first + iota(shape, 0)) + 1.0
    lane = iota(shape, 1)
    full = jnp.broadcast_to(period, shape)
    fine = unit_phasor(2.0 * lane * focal, full)
    fine_ref[0, :focal_count, :128] = fine[0]
    fine_ref[1, :focal_count, :128] = fine[1]
    start = (2 * first - extent + 1).astype(F32)
    coarse = unit_phasor((start + 256.0 * lane) * focal, full)
    fine_ref[0, :focal_count, 128:] = coarse[0]
    fine_ref[1, :focal_count, 128:] = coarse[1]
    for a in range(count):
        for part in range(0, focal_count, 64):
            rows = slice(part, min(part + 64, focal_count))
            re, im = turn(
                (fine_ref[0, rows, 128 + a : 129 + a], fine_ref[1, rows, 128 + a : 129 + a]),
                (fine_ref[0, rows, :128], fine_ref[1, rows, :128]),
            )
            write(part, a * 128, re.astype(BF16), im.astype(BF16))


def live_row(tiles_ref, tile_row, cells):
    tile_cols = tiles_ref.shape[1]
    width = cells // tile_cols
    parts = [
        jnp.full((1, width), jnp.where(tiles_ref[tile_row, j] == 1, 1.0, 0.0), F32)
        for j in range(tile_cols)
    ]
    return jnp.concatenate(parts, axis=1)


def slice_rows(source, target, sem, which, begin):
    span = pl.ds(pl.multiple_of(which * (source.shape[1] // 2) + begin, 16), target.shape[0])
    return pltpu.make_async_copy(source.at[0, span, :], target, sem)


def forward_kernel(index_ref, charge_ref, tiles_ref, cot_ref, inc_ref, *refs, rows, cols, n_row, groups, begin):
    outs, (col_tab, slice_ref) = refs[:-8], refs[-8:-6]
    row_tab, inner, fine_ref, t_ref, held, sems = refs[-6:]
    block = min(256, rows)
    extent = rows * n_row
    row_at = lax.axis_index("row")
    col_at = lax.axis_index("col")
    tile_size = rows // tiles_ref.shape[0]
    copies = []
    for step in range(rows // block):
        span = pl.ds(step * block, block)
        copies.append(pltpu.make_async_copy(cot_ref.at[0, :, span, :], held.at[:, span, :], sems.at[step]))
        copies[-1].start()
    half_at = lax.rem(lax.axis_index("wl"), 2)
    slice_copy = slice_rows(inc_ref, slice_ref, sems.at[rows // block], 1 - half_at, begin)
    slice_copy.start()
    period = quarter_period(index_ref[0])

    def write_col(at, amount, re, im):
        col_tab[at : at + amount, :HALF] = re
        col_tab[at : at + amount, HALF:] = im

    table_focal_lanes(write_col, period, col_at * cols, extent, cols, fine_ref)

    def write_row(part, at, re, im):
        row_tab[part : part + 64, at : at + 128] = re
        row_tab[HALF + part : HALF + part + 64, at : at + 128] = im

    table_pupil_lanes(write_row, period, row_at * rows, extent, rows, fine_ref, 0.0, HALF)

    for step in range(rows // block):
        copies[step].wait()
        halves = []
        for part in range(2):
            for at in range(step * block, (step + 1) * block, tile_size):
                mask = live_row(tiles_ref, at // tile_size, cols).astype(BF16)
                halves.append(held[part, at : at + tile_size, :] * mask)
        prod = jnp.dot(jnp.concatenate(halves, axis=0), col_tab[...], preferred_element_type=F32)
        at = step * block
        inner[at : at + block, :M] = prod[:block].astype(BF16)
        inner[at : at + block, M:] = prod[block:].astype(BF16)

    charge = charge_ref[0]
    even = jnp.where(charge % 2 == 0, 1.0, 0.0).astype(F32)
    odd = 1.0 - even
    scale = 4.0 / (extent * M)
    chunk = 128
    shape = (chunk, HALF)
    for ub in range(HALF // chunk):
        both = jnp.concatenate(
            [row_tab[ub * chunk : (ub + 1) * chunk, :], row_tab[HALF + ub * chunk : HALF + (ub + 1) * chunk, :]],
            axis=0,
        )
        q = jnp.dot(both, inner[...], preferred_element_type=F32)
        q_c, q_s = q[:chunk], q[chunk:]
        u = 2.0 * (iota(shape, 0) + float(ub * chunk)) + 1.0
        v = 2.0 * iota(shape, 1) + 1.0
        inv = 1.0 / jnp.sqrt(u * u + v * v)
        power = (u * inv, v * inv)
        total = (jnp.full(shape, scale, F32), jnp.zeros(shape, F32))
        for bit in range(4):
            taken = (charge >> bit) % 2 == 1
            multiplied = turn(total, power)
            total = tuple(jnp.where(taken, new, old) for new, old in zip(multiplied, total))
            power = turn(power, power)
        c, s = total
        ce, se, co, so = c * even, s * even, c * odd, s * odd
        ca, cb, cc, cd = (q_c[:, k * HALF : (k + 1) * HALF] for k in range(4))
        sa, sb, sc, sd = (q_s[:, k * HALF : (k + 1) * HALF] for k in range(4))
        t_ee = ce * ca - se * sd + so * cb - co * sc
        t_eo = ce * cb + se * sc - so * ca - co * sd
        t_oe = ce * sa + se * cd + co * cc + so * sb
        t_oo = ce * sb - se * cc + co * cd - so * sa
        per = t_ref.shape[1]
        span = min(per, chunk)
        for j in range(chunk // span):
            rows_j = slice(j * span, (j + 1) * span)
            for first, left, right in (
                (ub * chunk + j * span, t_ee, t_eo),
                (HALF + ub * chunk + j * span, t_oe, t_oo),
            ):
                to = slice(first % per, first % per + span)
                t_ref[first // per, to, :HALF] = left[rows_j]
                t_ref[first // per, to, HALF:] = right[rows_j]
    for out, (ky, slots) in zip(outs, groups):
        for k, kz in enumerate(slots):
            source = (col_at ^ ky) * n_row + (row_at ^ kz)
            out[k] = t_ref[source].astype(BF16)
    slice_copy.wait()


def in_hbm(value):
    return pltpu.with_memory_space_constraint(value, pltpu.HBM)


def forward(index, charge, tiles, cotangent, incident, begin, n_row, n_col, groups):
    rows, cols = cotangent.shape[2:]
    block = min(256, rows)
    per = M // (n_row * n_col)
    out_shape = [jax.ShapeDtypeStruct((len(slots), per, M), BF16) for _, slots in groups]
    out_shape.append(jax.ShapeDtypeStruct((cols, M), BF16))
    out_shape.append(jax.ShapeDtypeStruct((rows // 2 - begin, cols), BF16))

    def kernel(*refs):
        forward_kernel(*refs, rows=rows, cols=cols, n_row=n_row, groups=groups, begin=begin)

    hbm, smem = pl.BlockSpec(memory_space=pltpu.HBM), pl.BlockSpec(memory_space=pltpu.SMEM)
    outs = pl.pallas_call(
        kernel,
        in_specs=[smem, smem, smem, hbm, hbm],
        out_specs=[pl.BlockSpec(memory_space=pltpu.VMEM)] * len(out_shape),
        out_shape=out_shape,
        scratch_shapes=[
            pltpu.VMEM((M, rows), BF16),
            pltpu.VMEM((rows, 2 * M), BF16),
            pltpu.VMEM((2, HALF, HALF), F32),
            pltpu.VMEM((n_row * n_col, per, M), F32),
            pltpu.VMEM((2, rows, cols), BF16),
            pltpu.SemaphoreType.DMA((rows // block + 1,)),
        ],
        compiler_params=pltpu.CompilerParams(vmem_limit_bytes=36 << 20),
        cost_estimate=pl.CostEstimate(
            flops=2 * rows * 2 * M * (cols + M), bytes_accessed=4 * rows * cols, transcendentals=0
        ),
        name="forward",
    )(index, charge, tiles, in_hbm(cotangent), in_hbm(incident))
    return outs[:-2], outs[-2], outs[-1]


def swap(value, axis, bits):
    size = lax.axis_size(axis)
    return lax.ppermute(value, axis, [(i, i ^ bits) for i in range(size)])


def add_up(parts):
    total = parts[0].astype(F32)
    for part in parts[1:]:
        total = total + part.astype(F32)
    return total


def hop_order(n_row):
    return list(range(n_row - 1, 0, -1))


def slot_groups(n_row, n_col):
    order = hop_order(n_row) + [0]
    if n_row <= 4:
        parts = [order[:1], order[1:]]
    else:
        parts = [order[: n_row // 2], order[n_row // 2 :]]
    return [(ky, tuple(slots)) for slots in parts for ky in range(n_col)]


def reduce_blocks(parts, groups, n_row):
    reduced = {}
    for own, (ky, slots) in zip(parts, groups):
        if ky:
            continue
        terms = [own]
        for other, (step, other_slots) in zip(parts, groups):
            if step and other_slots == slots:
                terms.append(swap(other, "col", step))
        total = add_up(terms).astype(BF16)
        for k, kz in enumerate(slots):
            reduced[kz] = total[k]
    moved = [swap(reduced[kz], "row", kz) for kz in hop_order(n_row)]
    return add_up([reduced[0]] + moved).astype(BF16)


def gather_row(mine, n_row):
    return [mine] + [swap(mine, "row", kz) for kz in hop_order(n_row)]


def aligned(pieces):
    if any(piece.shape[0] % 16 for piece in pieces):
        return [jnp.concatenate(pieces, axis=0)]
    return pieces


def row_table_kernel(index_ref, row_tab, fine_ref, *, rows, n_row, n_col, full_rows, waves):
    extent = full_rows * n_row
    row_at = lax.axis_index("row")
    col_at = lax.axis_index("col")
    half_at = lax.rem(lax.axis_index("wl"), 2)
    per = M // (n_row * n_col)
    lane = lax.broadcasted_iota(jnp.int32, (16, M), 1)
    block = lane // per
    hops = (n_row - block % n_row) % n_row
    owner = ((block // n_row) ^ col_at) * n_row + (hops ^ row_at)
    place = owner * per + lane % per
    is_sin = place >= HALF
    focal = 2.0 * jnp.where(is_sin, place - HALF, place).astype(F32) + 1.0
    for w in range(waves):
        period = quarter_period(index_ref[w])
        for side in range(2):
            lanes = slice(side * HALF, (side + 1) * HALF)
            sine = is_sin[:1, lanes]

            def write_row(at, amount, re, im, w=w, lanes=lanes, sine=sine):
                row_tab[w, at : at + amount, lanes] = jnp.where(
                    sine, im.astype(F32), re.astype(F32)
                ).astype(BF16)

            table_focal_lanes(
                write_row,
                period,
                row_at * full_rows + half_at * rows,
                extent,
                row_tab.shape[1],
                fine_ref,
                lanes=focal[:, lanes],
            )


def row_tables(indices, rows, n_row, n_col, full_rows):
    waves = indices.shape[0]
    own_rows = max(rows, 256)

    def kernel(*refs):
        row_table_kernel(*refs, rows=rows, n_row=n_row, n_col=n_col, full_rows=full_rows, waves=waves)

    return pl.pallas_call(
        kernel,
        in_specs=[pl.BlockSpec(memory_space=pltpu.SMEM)],
        out_specs=pl.BlockSpec(memory_space=pltpu.VMEM),
        out_shape=jax.ShapeDtypeStruct((waves, own_rows, M), BF16),
        scratch_shapes=[pltpu.VMEM((2, HALF, HALF), F32)],
        compiler_params=pltpu.CompilerParams(vmem_limit_bytes=16 << 20),
        cost_estimate=pl.CostEstimate(flops=40 * M * own_rows, bytes_accessed=4 * M * own_rows, transcendentals=0),
        name="row_tables",
    )(indices)


def col_table(index, cols, n_col):
    def kernel(index_ref, col_tab, fine_ref):
        def write_col(at, amount, re, im):
            col_tab[at : at + amount, :HALF] = re
            col_tab[at : at + amount, HALF:] = im

        table_focal_lanes(
            write_col,
            quarter_period(index_ref[0]),
            lax.axis_index("col") * cols,
            cols * n_col,
            cols,
            fine_ref,
        )

    return pl.pallas_call(
        kernel,
        in_specs=[pl.BlockSpec(memory_space=pltpu.SMEM)],
        out_specs=pl.BlockSpec(memory_space=pltpu.VMEM),
        out_shape=jax.ShapeDtypeStruct((cols, M), BF16),
        scratch_shapes=[pltpu.VMEM((2, HALF, HALF), F32)],
        compiler_params=pltpu.CompilerParams(vmem_limit_bytes=16 << 20),
        cost_estimate=pl.CostEstimate(flops=20 * M * cols, bytes_accessed=4 * M * cols, transcendentals=0),
        name="col_table",
    )(index)


def backward_kernel(tiles_ref, *refs, counts, wave_ids, part_first, chunks, tile_size, rows, emit):
    waves = len(counts)
    total_pieces = sum(counts)
    sources, refs = refs[:total_pieces], refs[total_pieces:]
    n_tables = 1 + max(table for table, _ in wave_ids)
    row_tabs, refs = refs[:n_tables], refs[n_tables:]
    col_tabs, refs = refs[:waves], refs[waves:]
    incidents, refs = refs[:waves], refs[waves:]
    outs, refs = refs[: len(chunks)], refs[len(chunks) :]
    held, sems = refs[emit : emit + 2]
    matrices = list(refs[:emit] + refs[emit + 2 :])
    half_at = lax.rem(lax.axis_index("wl"), 2)
    first = chunks[0][0]
    copies = []
    for k, (at, amount) in enumerate(chunks):
        for w in range(waves):
            if part_first[w] is None:
                span = pl.ds(pl.multiple_of(half_at * rows + at, 16), amount)
                source = incidents[w].at[0, span, :]
            else:
                source = incidents[w].at[pl.ds(at - part_first[w], amount), :]
            copies.append(
                pltpu.make_async_copy(source, held.at[w, pl.ds(at - first, amount), :], sems.at[k, w])
            )
            copies[-1].start()
    ready = []
    for w in range(waves):
        pieces, sources = sources[: counts[w]], sources[counts[w] :]
        if counts[w] == 1:
            ready.append(pieces[0])
            continue
        target = matrices.pop(0)
        at = 0
        for piece in pieces:
            target[at : at + piece.shape[0], :] = piece[...]
            at += piece.shape[0]
        ready.append(target)
    cols = outs[0].shape[1]
    wide = min(512, cols)
    amount = sum(n for _, n in chunks)
    back_y = [
        jnp.dot(
            row_tabs[table][which, first : first + amount, :], ready[w][...], preferred_element_type=F32
        ).astype(BF16)
        for w, (table, which) in enumerate(wave_ids)
    ]
    for copy in copies:
        copy.wait()
    for part in range(0, cols, wide):
        span = slice(part, part + wide)
        total = None
        for w in range(waves):
            back = lax.dot_general(
                back_y[w], col_tabs[w][span, :], (((1,), (1,)), ((), ())), preferred_element_type=F32
            )
            term = back * held[w, :, span].astype(F32)
            total = term if total is None else total + term
        for out, (at, size) in zip(outs, chunks):
            borders = [at] + list(range((at // tile_size + 1) * tile_size, at + size, tile_size)) + [at + size]
            for low, high in zip(borders, borders[1:]):
                mask = live_row(tiles_ref, half_at * (rows // tile_size) + low // tile_size, cols)[:, span]
                out[low - at : high - at, span] = (total[low - first : high - first] * mask).astype(BF16)


def backward(tiles, waves, chunks, tile_size, rows, keep=False):
    cols = tiles.shape[1] * tile_size
    flat = [piece for wave in waves for piece in wave[0]]
    amount = sum(n for _, n in chunks)
    counts = [len(wave[0]) for wave in waves]
    built = sum(count > 1 for count in counts)
    emit = built if keep else 0
    tables = []
    for wave in waves:
        if not any(wave[1] is table for table in tables):
            tables.append(wave[1])
    wave_ids = [([wave[1] is table for table in tables].index(True), wave[2]) for wave in waves]

    def kernel(*refs):
        backward_kernel(
            *refs,
            counts=counts,
            wave_ids=wave_ids,
            part_first=[wave[5] for wave in waves],
            chunks=chunks,
            tile_size=tile_size,
            rows=rows,
            emit=emit,
        )

    vmem = pl.BlockSpec(memory_space=pltpu.VMEM)
    hbm = pl.BlockSpec(memory_space=pl.ANY)
    out_shape = [jax.ShapeDtypeStruct((n, cols), BF16) for _, n in chunks]
    out_shape += [jax.ShapeDtypeStruct((M, M), BF16)] * emit
    outs = pl.pallas_call(
        kernel,
        in_specs=[pl.BlockSpec(memory_space=pltpu.SMEM)]
        + [vmem] * (len(flat) + len(tables) + len(waves))
        + [hbm] * len(waves),
        out_specs=[vmem] * len(out_shape),
        out_shape=out_shape,
        scratch_shapes=[
            pltpu.VMEM((len(waves), amount, cols), BF16),
            pltpu.SemaphoreType.DMA((len(chunks), len(waves))),
        ]
        + [pltpu.VMEM((M, M), BF16)] * (built - emit),
        compiler_params=pltpu.CompilerParams(vmem_limit_bytes=24 << 20),
        cost_estimate=pl.CostEstimate(
            flops=2 * len(waves) * amount * M * (cols + M), bytes_accessed=6 * amount * cols, transcendentals=0
        ),
    )(tiles, *flat, *tables, *[wave[3] for wave in waves], *[wave[4] for wave in waves])
    return outs[: len(chunks)], outs[len(chunks) :]


def place_kernel(*refs, chunks, rows):
    sources = refs[: 2 * len(chunks)]
    out, sems = refs[-2:]
    half_at = lax.rem(lax.axis_index("wl"), 2)
    copies = []
    for k, (at, amount) in enumerate(chunks):
        for side in range(2):
            where = half_at if side == 0 else 1 - half_at
            target = out.at[pl.ds(pl.multiple_of(where * rows + at, 16), amount), :]
            copies.append(pltpu.make_async_copy(sources[2 * k + side], target, sems.at[k, side]))
    for copy in copies:
        copy.start()
    for copy in copies:
        copy.wait()


def place(done, chunks, rows, into=None):
    flat = [part for pair in done for part in pair]
    cols = flat[0].shape[1]
    operands = flat + ([into] if into is not None else [])

    def kernel(*refs):
        place_kernel(*refs, chunks=chunks, rows=rows)

    hbm = pl.BlockSpec(memory_space=pl.ANY)
    return pl.pallas_call(
        kernel,
        in_specs=[hbm] * len(operands),
        out_specs=hbm,
        out_shape=jax.ShapeDtypeStruct((2 * rows, cols), BF16),
        scratch_shapes=[pltpu.SemaphoreType.DMA((len(chunks), 2))],
        input_output_aliases={len(flat): 0} if into is not None else {},
        compiler_params=pltpu.CompilerParams(vmem_limit_bytes=1 << 20),
        cost_estimate=pl.CostEstimate(flops=0, bytes_accessed=4 * cols * sum(n for _, n in chunks), transcendentals=0),
    )(*operands)


def own_slice(incident, begin):
    amount, cols = incident.shape[1] // 2 - begin, incident.shape[2]

    def kernel(source, out, sem):
        copy = slice_rows(source, out, sem, lax.rem(lax.axis_index("wl"), 2), begin)
        copy.start()
        copy.wait()

    return pl.pallas_call(
        kernel,
        in_specs=[pl.BlockSpec(memory_space=pltpu.HBM)],
        out_specs=pl.BlockSpec(memory_space=pltpu.VMEM),
        out_shape=jax.ShapeDtypeStruct((amount, cols), BF16),
        scratch_shapes=[pltpu.SemaphoreType.DMA],
        compiler_params=pltpu.CompilerParams(vmem_limit_bytes=4 << 20),
        cost_estimate=pl.CostEstimate(flops=0, bytes_accessed=4 * amount * cols, transcendentals=0),
        name="own_slice",
    )(in_hbm(incident))


BOUNDS = (0, 4, 7, 9, 13, 16)
EXCHANGED = 3


def all_steps(cotangent, incident, tiles, charge, wl_index):
    rows, cols = cotangent.shape[2:]
    n_row = lax.axis_size("row")
    n_col = lax.axis_size("col")
    tile_size = rows // tiles.shape[0]
    half = rows // 2
    bounds = [half * bound // 16 // 16 * 16 for bound in BOUNDS]
    chunks = [(low, high - low) for low, high in zip(bounds, bounds[1:])]
    n_first = EXCHANGED
    split = chunks[n_first][0]

    inc_straight = swap(own_slice(incident, split), "wl", 2)
    groups = slot_groups(n_row, n_col)
    parts, col_own, slice_other = forward(
        wl_index, charge, tiles, cotangent, incident, split, n_row, n_col, groups
    )
    mine = reduce_blocks(parts, groups, n_row)
    inc_core = swap(incident, "wl", 1)
    inc_cross = swap(slice_other, "wl", 3)
    col_core = swap(col_own, "wl", 1)
    near = jnp.concatenate([wl_index, swap(wl_index, "wl", 1)])
    far = swap(wl_index, "wl", 2)
    far_core = swap(far, "wl", 1)
    row_near = row_tables(near, half, n_row, n_col, rows)
    row_far = row_tables(jnp.concatenate([far, far_core]), half, n_row, n_col, rows)
    col_straight = col_table(far, cols, n_col)
    col_cross = swap(col_straight, "wl", 1)

    here = gather_row(mine, n_row)
    joined = jnp.concatenate(here, axis=0)
    if n_row > 4:
        here = [joined]
    elif n_row > 2:
        here = here[:2] + [jnp.concatenate(here[2:], axis=0)]
    pieces, pieces_core = [joined], [swap(joined, "wl", 1)]
    for ky in range(1, n_col):
        for piece in here:
            pieces.append(swap(piece, "col", ky))
            pieces_core.append(swap(pieces[-1], "wl", 1))

    straight = [swap(joined, "wl", 2)]
    straight += [swap(straight[0], "col", ky) for ky in range(1, n_col)]
    cross = [swap(piece, "wl", 1) for piece in straight]

    own = (aligned(pieces), row_near, 0, col_own, incident, None)
    mate = (aligned(pieces_core), row_near, 1, col_core, inc_core, None)
    first, matrices = backward(tiles, [own, mate], chunks[:1], tile_size, half, keep=True)
    if len(matrices) == 2:
        own = ([matrices[0]],) + own[1:]
        mate = ([matrices[1]],) + mate[1:]
    second, _ = backward(tiles, [own, mate], chunks[1:n_first], tile_size, half)
    straight = (aligned(straight), row_far, 0, col_straight, inc_straight, split)
    cross = (aligned(cross), row_far, 1, col_cross, inc_cross, split)
    both, _ = backward(tiles, [own, mate, straight, cross], chunks[n_first:], tile_size, half)
    done = []
    for pair in list(first) + list(second):
        total = add_up([pair, swap(pair, "wl", 2)]).astype(BF16)
        done.append((total, swap(total, "wl", 1)))
    ready = [(part, swap(part, "wl", 1)) for part in both]
    result = place(ready, chunks[n_first:], half)
    result = place(done[:-1], chunks[: n_first - 1], half, result)
    return place(done[-1:], chunks[n_first - 1 : n_first], half, result)


def solution(mesh):
    return jax.shard_map(
        all_steps,
        mesh=mesh,
        in_specs=(
            P("wl", None, "row", "col"),
            P("wl", "row", "col"),
            P("row", "col"),
            P("wl"),
            P("wl"),
        ),
        out_specs=P("row", "col"),
        check_vma=False,
    )
```

```python
import math

import jax
import jax.numpy as jnp
from jax import lax
from jax.experimental import pallas as pl
from jax.experimental.pallas import tpu as pltpu
from jax.sharding import PartitionSpec as P


M = 512
HALF = M // 2
F32 = jnp.float32
BF16 = jnp.bfloat16


def iota(shape, axis):
    return lax.broadcasted_iota(jnp.int32, shape, axis).astype(F32)


def unit_phasor(product, period):
    turns = jnp.floor(product / period + 0.5)
    rest = product - turns * period
    quarter = jnp.floor(4.0 * rest / period + 0.5)
    theta = (4.0 * rest - quarter * period) / period * (0.5 * math.pi)
    sq = theta * theta
    sin_p = theta * (
        1.0 + sq * (-1.0 / 6.0 + sq * (1.0 / 120.0 + sq * (-1.0 / 5040.0 + sq / 362880.0)))
    )
    cos_p = 1.0 + sq * (
        -0.5 + sq * (1.0 / 24.0 + sq * (-1.0 / 720.0 + sq * (1.0 / 40320.0 - sq / 3628800.0)))
    )
    size = jnp.abs(quarter)
    odd = size == 1.0
    flip = jnp.where(size == 2.0, -1.0, 1.0)
    side = jnp.where(quarter < 0.0, -1.0, 1.0)
    cosine = jnp.where(odd, -side * sin_p, flip * cos_p)
    sine = jnp.where(odd, side * cos_p, flip * sin_p)
    return cosine, sine


def turn(first, second):
    c1, s1 = first
    c2, s2 = second
    return c1 * c2 - s1 * s2, s1 * c2 + c1 * s2


def quarter_period(index_value):
    return ((index_value + 32) * (M // 4)).astype(F32)


def table_focal_lanes(write, period, first, extent, amount, fine_ref, lanes=None, lane_count=HALF):
    block = 256
    focal = 2.0 * iota((16, lane_count), 1) + 1.0 if lanes is None else lanes
    step = iota((16, lane_count), 0)
    fine = unit_phasor(2.0 * step * focal, jnp.broadcast_to(period, (16, lane_count)))
    mid = unit_phasor(32.0 * step * focal, jnp.broadcast_to(period, (16, lane_count)))
    for b in range(16):
        re, im = turn((mid[0][b : b + 1], mid[1][b : b + 1]), fine)
        fine_ref[0, 16 * b : 16 * b + 16, :] = re
        fine_ref[1, 16 * b : 16 * b + 16, :] = im
    count = amount // block
    start = (2 * first - extent + 1).astype(F32)
    top = -(-count // 8) * 8
    focal_top = 2.0 * iota((top, lane_count), 1) + 1.0 if lanes is None else jnp.broadcast_to(lanes[:1], (top, lane_count))
    coarse = unit_phasor(
        (start + 2.0 * block * iota((top, lane_count), 0)) * focal_top,
        jnp.broadcast_to(period, (top, lane_count)),
    )
    for a in range(count):
        for part in range(0, block, 64):
            re, im = turn(
                (coarse[0][a : a + 1], coarse[1][a : a + 1]),
                (fine_ref[0, part : part + 64, :], fine_ref[1, part : part + 64, :]),
            )
            write(a * block + part, 64, re.astype(BF16), im.astype(BF16))


def table_pupil_lanes(write, period, first, extent, amount, fine_ref, focal_first, focal_count):
    count = amount // 128
    shape = (focal_count, 128)
    focal = 2.0 * (focal_first + iota(shape, 0)) + 1.0
    lane = iota(shape, 1)
    full = jnp.broadcast_to(period, shape)
    fine = unit_phasor(2.0 * lane * focal, full)
    fine_ref[0, :focal_count, :128] = fine[0]
    fine_ref[1, :focal_count, :128] = fine[1]
    start = (2 * first - extent + 1).astype(F32)
    coarse = unit_phasor((start + 256.0 * lane) * focal, full)
    fine_ref[0, :focal_count, 128:] = coarse[0]
    fine_ref[1, :focal_count, 128:] = coarse[1]
    for a in range(count):
        for part in range(0, focal_count, 64):
            rows = slice(part, min(part + 64, focal_count))
            re, im = turn(
                (fine_ref[0, rows, 128 + a : 129 + a], fine_ref[1, rows, 128 + a : 129 + a]),
                (fine_ref[0, rows, :128], fine_ref[1, rows, :128]),
            )
            write(part, a * 128, re.astype(BF16), im.astype(BF16))


def live_row(tiles_ref, tile_row, cells):
    tile_cols = tiles_ref.shape[1]
    width = cells // tile_cols
    parts = [
        jnp.full((1, width), jnp.where(tiles_ref[tile_row, j] == 1, 1.0, 0.0), F32)
        for j in range(tile_cols)
    ]
    return jnp.concatenate(parts, axis=1)


def slice_rows(source, target, sem, which, begin):
    span = pl.ds(pl.multiple_of(which * (source.shape[1] // 2) + begin, 16), target.shape[0])
    return pltpu.make_async_copy(source.at[0, span, :], target, sem)


def forward_kernel(index_ref, charge_ref, tiles_ref, cot_ref, inc_ref, *refs, rows, cols, n_row, groups, begin):
    outs, (col_tab, slice_ref) = refs[:-7], refs[-7:-5]
    row_tab, inner, fine_ref, t_ref, sem = refs[-5:]
    block = min(256, rows)
    extent = rows * n_row
    row_at = lax.axis_index("row")
    col_at = lax.axis_index("col")
    tile_size = rows // tiles_ref.shape[0]
    half_at = lax.rem(lax.axis_index("wl"), 2)
    slice_copy = slice_rows(inc_ref, slice_ref, sem, 1 - half_at, begin)
    slice_copy.start()
    period = quarter_period(index_ref[0])

    def write_col(at, amount, re, im):
        col_tab[at : at + amount, :HALF] = re
        col_tab[at : at + amount, HALF:] = im

    table_focal_lanes(write_col, period, col_at * cols, extent, cols, fine_ref)

    def write_row(part, at, re, im):
        row_tab[part : part + 64, at : at + 128] = re
        row_tab[HALF + part : HALF + part + 64, at : at + 128] = im

    table_pupil_lanes(write_row, period, row_at * rows, extent, rows, fine_ref, 0.0, HALF)

    for step in range(rows // block):
        halves = []
        for part in range(2):
            for at in range(step * block, (step + 1) * block, tile_size):
                mask = live_row(tiles_ref, at // tile_size, cols).astype(BF16)
                halves.append(cot_ref[0, part, at : at + tile_size, :] * mask)
        prod = jnp.dot(jnp.concatenate(halves, axis=0), col_tab[...], preferred_element_type=F32)
        at = step * block
        inner[at : at + block, :M] = prod[:block].astype(BF16)
        inner[at : at + block, M:] = prod[block:].astype(BF16)

    charge = charge_ref[0]
    even = jnp.where(charge % 2 == 0, 1.0, 0.0).astype(F32)
    odd = 1.0 - even
    scale = 4.0 / (extent * M)
    chunk = 128
    shape = (chunk, HALF)
    for ub in range(HALF // chunk):
        both = jnp.concatenate(
            [row_tab[ub * chunk : (ub + 1) * chunk, :], row_tab[HALF + ub * chunk : HALF + (ub + 1) * chunk, :]],
            axis=0,
        )
        q = jnp.dot(both, inner[...], preferred_element_type=F32)
        q_c, q_s = q[:chunk], q[chunk:]
        u = 2.0 * (iota(shape, 0) + float(ub * chunk)) + 1.0
        v = 2.0 * iota(shape, 1) + 1.0
        inv = 1.0 / jnp.sqrt(u * u + v * v)
        power = (u * inv, v * inv)
        total = (jnp.full(shape, scale, F32), jnp.zeros(shape, F32))
        for bit in range(4):
            taken = (charge >> bit) % 2 == 1
            multiplied = turn(total, power)
            total = tuple(jnp.where(taken, new, old) for new, old in zip(multiplied, total))
            power = turn(power, power)
        c, s = total
        ce, se, co, so = c * even, s * even, c * odd, s * odd
        ca, cb, cc, cd = (q_c[:, k * HALF : (k + 1) * HALF] for k in range(4))
        sa, sb, sc, sd = (q_s[:, k * HALF : (k + 1) * HALF] for k in range(4))
        t_ee = ce * ca - se * sd + so * cb - co * sc
        t_eo = ce * cb + se * sc - so * ca - co * sd
        t_oe = ce * sa + se * cd + co * cc + so * sb
        t_oo = ce * sb - se * cc + co * cd - so * sa
        per = t_ref.shape[1]
        span = min(per, chunk)
        for j in range(chunk // span):
            rows_j = slice(j * span, (j + 1) * span)
            for first, left, right in (
                (ub * chunk + j * span, t_ee, t_eo),
                (HALF + ub * chunk + j * span, t_oe, t_oo),
            ):
                to = slice(first % per, first % per + span)
                t_ref[first // per, to, :HALF] = left[rows_j]
                t_ref[first // per, to, HALF:] = right[rows_j]
    for out, (ky, slots) in zip(outs, groups):
        for k, kz in enumerate(slots):
            source = (col_at ^ ky) * n_row + (row_at ^ kz)
            out[k] = t_ref[source].astype(BF16)
    slice_copy.wait()


def in_hbm(value):
    return pltpu.with_memory_space_constraint(value, pltpu.HBM)


def forward(index, charge, tiles, cotangent, incident, begin, n_row, n_col, groups):
    rows, cols = cotangent.shape[2:]
    per = M // (n_row * n_col)
    out_shape = [jax.ShapeDtypeStruct((len(slots), per, M), BF16) for _, slots in groups]
    out_shape.append(jax.ShapeDtypeStruct((cols, M), BF16))
    out_shape.append(jax.ShapeDtypeStruct((rows // 2 - begin, cols), BF16))

    def kernel(*refs):
        forward_kernel(*refs, rows=rows, cols=cols, n_row=n_row, groups=groups, begin=begin)

    hbm, smem = pl.BlockSpec(memory_space=pltpu.HBM), pl.BlockSpec(memory_space=pltpu.SMEM)
    outs = pl.pallas_call(
        kernel,
        in_specs=[smem, smem, smem, pl.BlockSpec(memory_space=pltpu.VMEM), hbm],
        out_specs=[pl.BlockSpec(memory_space=pltpu.VMEM)] * len(out_shape),
        out_shape=out_shape,
        scratch_shapes=[
            pltpu.VMEM((M, rows), BF16),
            pltpu.VMEM((rows, 2 * M), BF16),
            pltpu.VMEM((2, HALF, HALF), F32),
            pltpu.VMEM((n_row * n_col, per, M), F32),
            pltpu.SemaphoreType.DMA,
        ],
        compiler_params=pltpu.CompilerParams(vmem_limit_bytes=36 << 20),
        cost_estimate=pl.CostEstimate(
            flops=2 * rows * 2 * M * (cols + M), bytes_accessed=4 * rows * cols, transcendentals=0
        ),
        name="forward",
    )(index, charge, tiles, cotangent, in_hbm(incident))
    return outs[:-2], outs[-2], outs[-1]


def swap(value, axis, bits):
    size = lax.axis_size(axis)
    return lax.ppermute(value, axis, [(i, i ^ bits) for i in range(size)])


def add_up(parts):
    total = parts[0].astype(F32)
    for part in parts[1:]:
        total = total + part.astype(F32)
    return total


def hop_order(n_row):
    return sorted(range(1, n_row), key=lambda k: -(k & -k))


def slot_groups(n_row, n_col):
    order = hop_order(n_row) + [0]
    if n_row <= 4:
        parts = [order[:1], order[1:]]
    else:
        parts = [order[: n_row // 2], order[n_row // 2 :]]
    return [(ky, tuple(slots)) for slots in parts for ky in range(n_col)]


def reduce_blocks(parts, groups, n_row):
    reduced = {}
    for own, (ky, slots) in zip(parts, groups):
        if ky:
            continue
        terms = [own]
        for other, (step, other_slots) in zip(parts, groups):
            if step and other_slots == slots:
                terms.append(swap(other, "col", step))
        total = add_up(terms).astype(BF16)
        for k, kz in enumerate(slots):
            reduced[kz] = total[k]
    moved = [swap(reduced[kz], "row", kz) for kz in hop_order(n_row)]
    return add_up([reduced[0]] + moved).astype(BF16)


def gather_row(mine, n_row):
    found = {0: mine}
    for kz in hop_order(n_row):
        found[kz] = swap(mine, "row", kz)
    return [found[kz] for kz in range(n_row)]


def aligned(pieces):
    if any(piece.shape[0] % 16 for piece in pieces):
        return [jnp.concatenate(pieces, axis=0)]
    return pieces


def row_table_kernel(index_ref, row_tab, fine_ref, *, rows, n_row, n_col, full_rows, waves):
    extent = full_rows * n_row
    row_at = lax.axis_index("row")
    col_at = lax.axis_index("col")
    half_at = lax.rem(lax.axis_index("wl"), 2)
    per = M // (n_row * n_col)
    lane = lax.broadcasted_iota(jnp.int32, (16, M), 1)
    block = lane // per
    owner = ((block // n_row) ^ col_at) * n_row + ((block % n_row) ^ row_at)
    place = owner * per + lane % per
    is_sin = place >= HALF
    focal = 2.0 * jnp.where(is_sin, place - HALF, place).astype(F32) + 1.0
    for w in range(waves):
        period = quarter_period(index_ref[w])
        for side in range(2):
            lanes = slice(side * HALF, (side + 1) * HALF)
            sine = is_sin[:1, lanes]

            def write_row(at, amount, re, im, w=w, lanes=lanes, sine=sine):
                row_tab[w, at : at + amount, lanes] = jnp.where(
                    sine, im.astype(F32), re.astype(F32)
                ).astype(BF16)

            table_focal_lanes(
                write_row,
                period,
                row_at * full_rows + half_at * rows,
                extent,
                row_tab.shape[1],
                fine_ref,
                lanes=focal[:, lanes],
            )


def row_tables(indices, rows, n_row, n_col, full_rows):
    waves = indices.shape[0]
    own_rows = max(rows, 256)

    def kernel(*refs):
        row_table_kernel(*refs, rows=rows, n_row=n_row, n_col=n_col, full_rows=full_rows, waves=waves)

    return pl.pallas_call(
        kernel,
        in_specs=[pl.BlockSpec(memory_space=pltpu.SMEM)],
        out_specs=pl.BlockSpec(memory_space=pltpu.VMEM),
        out_shape=jax.ShapeDtypeStruct((waves, own_rows, M), BF16),
        scratch_shapes=[pltpu.VMEM((2, HALF, HALF), F32)],
        compiler_params=pltpu.CompilerParams(vmem_limit_bytes=16 << 20),
        cost_estimate=pl.CostEstimate(flops=40 * M * own_rows, bytes_accessed=4 * M * own_rows, transcendentals=0),
        name="row_tables",
    )(indices)


def col_table(index, cols, n_col):
    def kernel(index_ref, col_tab, fine_ref):
        def write_col(at, amount, re, im):
            col_tab[at : at + amount, :HALF] = re
            col_tab[at : at + amount, HALF:] = im

        table_focal_lanes(
            write_col,
            quarter_period(index_ref[0]),
            lax.axis_index("col") * cols,
            cols * n_col,
            cols,
            fine_ref,
        )

    return pl.pallas_call(
        kernel,
        in_specs=[pl.BlockSpec(memory_space=pltpu.SMEM)],
        out_specs=pl.BlockSpec(memory_space=pltpu.VMEM),
        out_shape=jax.ShapeDtypeStruct((cols, M), BF16),
        scratch_shapes=[pltpu.VMEM((2, HALF, HALF), F32)],
        compiler_params=pltpu.CompilerParams(vmem_limit_bytes=16 << 20),
        cost_estimate=pl.CostEstimate(flops=20 * M * cols, bytes_accessed=4 * M * cols, transcendentals=0),
        name="col_table",
    )(index)


def backward_kernel(tiles_ref, *refs, counts, wave_ids, part_first, chunks, tile_size, rows, emit):
    waves = len(counts)
    total_pieces = sum(counts)
    sources, refs = refs[:total_pieces], refs[total_pieces:]
    n_tables = 1 + max(table for table, _ in wave_ids)
    row_tabs, refs = refs[:n_tables], refs[n_tables:]
    col_tabs, refs = refs[:waves], refs[waves:]
    incidents, refs = refs[:waves], refs[waves:]
    outs, refs = refs[: len(chunks)], refs[len(chunks) :]
    held, sems = refs[emit : emit + 2]
    matrices = list(refs[:emit] + refs[emit + 2 :])
    half_at = lax.rem(lax.axis_index("wl"), 2)
    first = chunks[0][0]
    copies = []
    for k, (at, amount) in enumerate(chunks):
        for w in range(waves):
            if part_first[w] is None:
                span = pl.ds(pl.multiple_of(half_at * rows + at, 16), amount)
                source = incidents[w].at[0, span, :]
            else:
                source = incidents[w].at[pl.ds(at - part_first[w], amount), :]
            copies.append(
                pltpu.make_async_copy(source, held.at[w, pl.ds(at - first, amount), :], sems.at[k, w])
            )
            copies[-1].start()
    ready = []
    for w in range(waves):
        pieces, sources = sources[: counts[w]], sources[counts[w] :]
        if counts[w] == 1:
            ready.append(pieces[0])
            continue
        target = matrices.pop(0)
        at = 0
        for piece in pieces:
            target[at : at + piece.shape[0], :] = piece[...]
            at += piece.shape[0]
        ready.append(target)
    cols = outs[0].shape[1]
    wide = min(512, cols)
    amount = sum(n for _, n in chunks)
    back_y = [
        jnp.dot(
            row_tabs[table][which, first : first + amount, :], ready[w][...], preferred_element_type=F32
        ).astype(BF16)
        for w, (table, which) in enumerate(wave_ids)
    ]
    for copy in copies:
        copy.wait()
    for part in range(0, cols, wide):
        span = slice(part, part + wide)
        total = None
        for w in range(waves):
            back = lax.dot_general(
                back_y[w], col_tabs[w][span, :], (((1,), (1,)), ((), ())), preferred_element_type=F32
            )
            term = back * held[w, :, span].astype(F32)
            total = term if total is None else total + term
        for out, (at, size) in zip(outs, chunks):
            borders = [at] + list(range((at // tile_size + 1) * tile_size, at + size, tile_size)) + [at + size]
            for low, high in zip(borders, borders[1:]):
                mask = live_row(tiles_ref, half_at * (rows // tile_size) + low // tile_size, cols)[:, span]
                out[low - at : high - at, span] = (total[low - first : high - first] * mask).astype(BF16)


def backward(tiles, waves, chunks, tile_size, rows, keep=False):
    cols = tiles.shape[1] * tile_size
    flat = [piece for wave in waves for piece in wave[0]]
    amount = sum(n for _, n in chunks)
    counts = [len(wave[0]) for wave in waves]
    built = sum(count > 1 for count in counts)
    emit = built if keep else 0
    tables = []
    for wave in waves:
        if not any(wave[1] is table for table in tables):
            tables.append(wave[1])
    wave_ids = [([wave[1] is table for table in tables].index(True), wave[2]) for wave in waves]

    def kernel(*refs):
        backward_kernel(
            *refs,
            counts=counts,
            wave_ids=wave_ids,
            part_first=[wave[5] for wave in waves],
            chunks=chunks,
            tile_size=tile_size,
            rows=rows,
            emit=emit,
        )

    vmem = pl.BlockSpec(memory_space=pltpu.VMEM)
    hbm = pl.BlockSpec(memory_space=pl.ANY)
    out_shape = [jax.ShapeDtypeStruct((n, cols), BF16) for _, n in chunks]
    out_shape += [jax.ShapeDtypeStruct((M, M), BF16)] * emit
    outs = pl.pallas_call(
        kernel,
        in_specs=[pl.BlockSpec(memory_space=pltpu.SMEM)]
        + [vmem] * (len(flat) + len(tables) + len(waves))
        + [hbm] * len(waves),
        out_specs=[vmem] * len(out_shape),
        out_shape=out_shape,
        scratch_shapes=[
            pltpu.VMEM((len(waves), amount, cols), BF16),
            pltpu.SemaphoreType.DMA((len(chunks), len(waves))),
        ]
        + [pltpu.VMEM((M, M), BF16)] * (built - emit),
        compiler_params=pltpu.CompilerParams(vmem_limit_bytes=24 << 20),
        cost_estimate=pl.CostEstimate(
            flops=2 * len(waves) * amount * M * (cols + M), bytes_accessed=6 * amount * cols, transcendentals=0
        ),
    )(tiles, *flat, *tables, *[wave[3] for wave in waves], *[wave[4] for wave in waves])
    return outs[: len(chunks)], outs[len(chunks) :]


def place_kernel(*refs, chunks, rows):
    sources = refs[: 2 * len(chunks)]
    out, sems = refs[-2:]
    half_at = lax.rem(lax.axis_index("wl"), 2)
    copies = []
    for k, (at, amount) in enumerate(chunks):
        for side in range(2):
            where = half_at if side == 0 else 1 - half_at
            target = out.at[pl.ds(pl.multiple_of(where * rows + at, 16), amount), :]
            copies.append(pltpu.make_async_copy(sources[2 * k + side], target, sems.at[k, side]))
    for copy in copies:
        copy.start()
    for copy in copies:
        copy.wait()


def place(done, chunks, rows, into=None):
    flat = [part for pair in done for part in pair]
    cols = flat[0].shape[1]
    operands = flat + ([into] if into is not None else [])

    def kernel(*refs):
        place_kernel(*refs, chunks=chunks, rows=rows)

    hbm = pl.BlockSpec(memory_space=pl.ANY)
    return pl.pallas_call(
        kernel,
        in_specs=[hbm] * len(operands),
        out_specs=hbm,
        out_shape=jax.ShapeDtypeStruct((2 * rows, cols), BF16),
        scratch_shapes=[pltpu.SemaphoreType.DMA((len(chunks), 2))],
        input_output_aliases={len(flat): 0} if into is not None else {},
        compiler_params=pltpu.CompilerParams(vmem_limit_bytes=1 << 20),
        cost_estimate=pl.CostEstimate(flops=0, bytes_accessed=4 * cols * sum(n for _, n in chunks), transcendentals=0),
    )(*operands)


def own_slice(incident, begin):
    amount, cols = incident.shape[1] // 2 - begin, incident.shape[2]

    def kernel(source, out, sem):
        copy = slice_rows(source, out, sem, lax.rem(lax.axis_index("wl"), 2), begin)
        copy.start()
        copy.wait()

    return pl.pallas_call(
        kernel,
        in_specs=[pl.BlockSpec(memory_space=pltpu.HBM)],
        out_specs=pl.BlockSpec(memory_space=pltpu.VMEM),
        out_shape=jax.ShapeDtypeStruct((amount, cols), BF16),
        scratch_shapes=[pltpu.SemaphoreType.DMA],
        compiler_params=pltpu.CompilerParams(vmem_limit_bytes=4 << 20),
        cost_estimate=pl.CostEstimate(flops=4 << 30, bytes_accessed=4 * amount * cols, transcendentals=0),
        name="own_slice",
    )(in_hbm(incident))


BOUNDS = (0, 4, 7, 9, 13, 16)
EXCHANGED = 3


def all_steps(cotangent, incident, tiles, charge, wl_index):
    rows, cols = cotangent.shape[2:]
    n_row = lax.axis_size("row")
    n_col = lax.axis_size("col")
    tile_size = rows // tiles.shape[0]
    half = rows // 2
    bounds = [half * bound // 16 // 16 * 16 for bound in BOUNDS]
    chunks = [(low, high - low) for low, high in zip(bounds, bounds[1:])]
    n_first = EXCHANGED
    split = chunks[n_first][0]

    inc_straight = swap(own_slice(incident, split), "wl", 2)
    groups = slot_groups(n_row, n_col)
    parts, col_own, slice_other = forward(
        wl_index, charge, tiles, cotangent, incident, split, n_row, n_col, groups
    )
    mine = reduce_blocks(parts, groups, n_row)
    inc_core = swap(incident, "wl", 1)
    inc_cross = swap(slice_other, "wl", 3)
    col_core = swap(col_own, "wl", 1)
    near = jnp.concatenate([wl_index, swap(wl_index, "wl", 1)])
    far = swap(wl_index, "wl", 2)
    far_core = swap(far, "wl", 1)
    row_near = row_tables(near, half, n_row, n_col, rows)
    row_far = row_tables(jnp.concatenate([far, far_core]), half, n_row, n_col, rows)
    col_straight = col_table(far, cols, n_col)
    col_cross = swap(col_straight, "wl", 1)

    here = gather_row(mine, n_row)
    if n_row > 4:
        here = [jnp.concatenate(here, axis=0)]
    joined = jnp.concatenate(here, axis=0)
    pieces, pieces_core = [joined], [swap(joined, "wl", 1)]
    for ky in range(1, n_col):
        for piece in here:
            pieces.append(swap(piece, "col", ky))
            pieces_core.append(swap(pieces[-1], "wl", 1))

    straight = [swap(joined, "wl", 2)]
    straight += [swap(straight[0], "col", ky) for ky in range(1, n_col)]
    cross = [swap(piece, "wl", 1) for piece in straight]

    own = (aligned(pieces), row_near, 0, col_own, incident, None)
    mate = (aligned(pieces_core), row_near, 1, col_core, inc_core, None)
    first, matrices = backward(tiles, [own, mate], chunks[:1], tile_size, half, keep=True)
    if len(matrices) == 2:
        own = ([matrices[0]],) + own[1:]
        mate = ([matrices[1]],) + mate[1:]
    second, _ = backward(tiles, [own, mate], chunks[1:n_first], tile_size, half)
    straight = (aligned(straight), row_far, 0, col_straight, inc_straight, split)
    cross = (aligned(cross), row_far, 1, col_cross, inc_cross, split)
    both, _ = backward(tiles, [own, mate, straight, cross], chunks[n_first:], tile_size, half)
    done = []
    for pair in list(first) + list(second):
        total = add_up([pair, swap(pair, "wl", 2)]).astype(BF16)
        done.append((total, swap(total, "wl", 1)))
    ready = [(part, swap(part, "wl", 1)) for part in both]
    result = place(ready, chunks[n_first:], half)
    result = place(done[:-1], chunks[: n_first - 1], half, result)
    return place(done[-1:], chunks[n_first - 1 : n_first], half, result)


def solution(mesh):
    return jax.shard_map(
        all_steps,
        mesh=mesh,
        in_specs=(
            P("wl", None, "row", "col"),
            P("wl", "row", "col"),
            P("row", "col"),
            P("wl"),
            P("wl"),
        ),
        out_specs=P("row", "col"),
        check_vma=False,
    )
```

```python
import math

import jax
import jax.numpy as jnp
from jax import lax
from jax.experimental import pallas as pl
from jax.experimental.pallas import tpu as pltpu
from jax.sharding import PartitionSpec as P


M = 512
HALF = M // 2
F32 = jnp.float32
BF16 = jnp.bfloat16


def iota(shape, axis):
    return lax.broadcasted_iota(jnp.int32, shape, axis).astype(F32)


def unit_phasor(product, period):
    turns = jnp.floor(product / period + 0.5)
    rest = product - turns * period
    quarter = jnp.floor(4.0 * rest / period + 0.5)
    theta = (4.0 * rest - quarter * period) / period * (0.5 * math.pi)
    sq = theta * theta
    sin_p = theta * (
        1.0 + sq * (-1.0 / 6.0 + sq * (1.0 / 120.0 + sq * (-1.0 / 5040.0 + sq / 362880.0)))
    )
    cos_p = 1.0 + sq * (
        -0.5 + sq * (1.0 / 24.0 + sq * (-1.0 / 720.0 + sq * (1.0 / 40320.0 - sq / 3628800.0)))
    )
    size = jnp.abs(quarter)
    odd = size == 1.0
    flip = jnp.where(size == 2.0, -1.0, 1.0)
    side = jnp.where(quarter < 0.0, -1.0, 1.0)
    cosine = jnp.where(odd, -side * sin_p, flip * cos_p)
    sine = jnp.where(odd, side * cos_p, flip * sin_p)
    return cosine, sine


def turn(first, second):
    c1, s1 = first
    c2, s2 = second
    return c1 * c2 - s1 * s2, s1 * c2 + c1 * s2


def quarter_period(index_value):
    return ((index_value + 32) * (M // 4)).astype(F32)


def table_focal_lanes(write, period, first, extent, amount, fine_ref, lanes=None, lane_count=HALF):
    block = 256
    focal = 2.0 * iota((16, lane_count), 1) + 1.0 if lanes is None else lanes
    step = iota((16, lane_count), 0)
    fine = unit_phasor(2.0 * step * focal, jnp.broadcast_to(period, (16, lane_count)))
    mid = unit_phasor(32.0 * step * focal, jnp.broadcast_to(period, (16, lane_count)))
    for b in range(16):
        re, im = turn((mid[0][b : b + 1], mid[1][b : b + 1]), fine)
        fine_ref[0, 16 * b : 16 * b + 16, :] = re
        fine_ref[1, 16 * b : 16 * b + 16, :] = im
    count = amount // block
    start = (2 * first - extent + 1).astype(F32)
    top = -(-count // 8) * 8
    focal_top = 2.0 * iota((top, lane_count), 1) + 1.0 if lanes is None else jnp.broadcast_to(lanes[:1], (top, lane_count))
    coarse = unit_phasor(
        (start + 2.0 * block * iota((top, lane_count), 0)) * focal_top,
        jnp.broadcast_to(period, (top, lane_count)),
    )
    for a in range(count):
        for part in range(0, block, 64):
            re, im = turn(
                (coarse[0][a : a + 1], coarse[1][a : a + 1]),
                (fine_ref[0, part : part + 64, :], fine_ref[1, part : part + 64, :]),
            )
            write(a * block + part, 64, re.astype(BF16), im.astype(BF16))


def table_pupil_lanes(write, period, first, extent, amount, fine_ref, focal_first, focal_count):
    count = amount // 128
    shape = (focal_count, 128)
    focal = 2.0 * (focal_first + iota(shape, 0)) + 1.0
    lane = iota(shape, 1)
    full = jnp.broadcast_to(period, shape)
    fine = unit_phasor(2.0 * lane * focal, full)
    fine_ref[0, :focal_count, :128] = fine[0]
    fine_ref[1, :focal_count, :128] = fine[1]
    start = (2 * first - extent + 1).astype(F32)
    coarse = unit_phasor((start + 256.0 * lane) * focal, full)
    fine_ref[0, :focal_count, 128:] = coarse[0]
    fine_ref[1, :focal_count, 128:] = coarse[1]
    for a in range(count):
        for part in range(0, focal_count, 64):
            rows = slice(part, min(part + 64, focal_count))
            re, im = turn(
                (fine_ref[0, rows, 128 + a : 129 + a], fine_ref[1, rows, 128 + a : 129 + a]),
                (fine_ref[0, rows, :128], fine_ref[1, rows, :128]),
            )
            write(part, a * 128, re.astype(BF16), im.astype(BF16))


def live_row(tiles_ref, tile_row, cells):
    tile_cols = tiles_ref.shape[1]
    width = cells // tile_cols
    parts = [
        jnp.full((1, width), jnp.where(tiles_ref[tile_row, j] == 1, 1.0, 0.0), F32)
        for j in range(tile_cols)
    ]
    return jnp.concatenate(parts, axis=1)


def slice_rows(source, target, sem, which, begin):
    span = pl.ds(pl.multiple_of(which * (source.shape[1] // 2) + begin, 16), target.shape[0])
    return pltpu.make_async_copy(source.at[0, span, :], target, sem)


def forward_kernel(index_ref, charge_ref, tiles_ref, cot_ref, inc_ref, *refs, rows, cols, n_row, groups, begin):
    outs, (col_tab, slice_ref) = refs[:-8], refs[-8:-6]
    row_tab, inner, fine_ref, t_ref, phase_ref, sem = refs[-6:]
    block = min(256, rows)
    extent = rows * n_row
    row_at = lax.axis_index("row")
    col_at = lax.axis_index("col")
    tile_size = rows // tiles_ref.shape[0]
    half_at = lax.rem(lax.axis_index("wl"), 2)
    slice_copy = slice_rows(inc_ref, slice_ref, sem, 1 - half_at, begin)
    slice_copy.start()
    period = quarter_period(index_ref[0])

    def write_col(at, amount, re, im):
        col_tab[at : at + amount, :HALF] = re
        col_tab[at : at + amount, HALF:] = im

    table_focal_lanes(write_col, period, col_at * cols, extent, cols, fine_ref)

    def write_row(part, at, re, im):
        row_tab[part : part + 64, at : at + 128] = re
        row_tab[HALF + part : HALF + part + 64, at : at + 128] = im

    table_pupil_lanes(write_row, period, row_at * rows, extent, rows, fine_ref, 0.0, HALF)

    charge = charge_ref[0]
    scale = 4.0 / (extent * M)
    shape = (64, HALF)
    for ub in range(HALF // 64):
        u = 2.0 * (iota(shape, 0) + float(ub * 64)) + 1.0
        v = 2.0 * iota(shape, 1) + 1.0
        inv = 1.0 / jnp.sqrt(u * u + v * v)
        power = (u * inv, v * inv)
        total = (jnp.full(shape, scale, F32), jnp.zeros(shape, F32))
        for bit in range(4):
            taken = (charge >> bit) % 2 == 1
            multiplied = turn(total, power)
            total = tuple(jnp.where(taken, new, old) for new, old in zip(multiplied, total))
            power = turn(power, power)
        phase_ref[0, ub * 64 : (ub + 1) * 64, :], phase_ref[1, ub * 64 : (ub + 1) * 64, :] = total

    for step in range(rows // block):
        halves = []
        for part in range(2):
            for at in range(step * block, (step + 1) * block, tile_size):
                mask = live_row(tiles_ref, at // tile_size, cols).astype(BF16)
                halves.append(cot_ref[0, part, at : at + tile_size, :] * mask)
        prod = jnp.dot(jnp.concatenate(halves, axis=0), col_tab[...], preferred_element_type=F32)
        at = step * block
        inner[at : at + block, :M] = prod[:block].astype(BF16)
        inner[at : at + block, M:] = prod[block:].astype(BF16)

    charge = charge_ref[0]
    even = jnp.where(charge % 2 == 0, 1.0, 0.0).astype(F32)
    odd = 1.0 - even
    scale = 4.0 / (extent * M)
    chunk = 128
    shape = (chunk, HALF)
    for ub in range(HALF // chunk):
        both = jnp.concatenate(
            [row_tab[ub * chunk : (ub + 1) * chunk, :], row_tab[HALF + ub * chunk : HALF + (ub + 1) * chunk, :]],
            axis=0,
        )
        q = jnp.dot(both, inner[...], preferred_element_type=F32)
        q_c, q_s = q[:chunk], q[chunk:]
        c, s = phase_ref[0, ub * chunk : (ub + 1) * chunk, :], phase_ref[1, ub * chunk : (ub + 1) * chunk, :]
        ce, se, co, so = c * even, s * even, c * odd, s * odd
        ca, cb, cc, cd = (q_c[:, k * HALF : (k + 1) * HALF] for k in range(4))
        sa, sb, sc, sd = (q_s[:, k * HALF : (k + 1) * HALF] for k in range(4))
        t_ee = ce * ca - se * sd + so * cb - co * sc
        t_eo = ce * cb + se * sc - so * ca - co * sd
        t_oe = ce * sa + se * cd + co * cc + so * sb
        t_oo = ce * sb - se * cc + co * cd - so * sa
        per = t_ref.shape[1]
        span = min(per, chunk)
        for j in range(chunk // span):
            rows_j = slice(j * span, (j + 1) * span)
            for first, left, right in (
                (ub * chunk + j * span, t_ee, t_eo),
                (HALF + ub * chunk + j * span, t_oe, t_oo),
            ):
                to = slice(first % per, first % per + span)
                t_ref[first // per, to, :HALF] = left[rows_j]
                t_ref[first // per, to, HALF:] = right[rows_j]
    for out, (ky, slots) in zip(outs, groups):
        for k, kz in enumerate(slots):
            source = (col_at ^ ky) * n_row + (row_at ^ kz)
            out[k] = t_ref[source].astype(BF16)
    slice_copy.wait()


def in_hbm(value):
    return pltpu.with_memory_space_constraint(value, pltpu.HBM)


def forward(index, charge, tiles, cotangent, incident, begin, n_row, n_col, groups):
    rows, cols = cotangent.shape[2:]
    per = M // (n_row * n_col)
    out_shape = [jax.ShapeDtypeStruct((len(slots), per, M), BF16) for _, slots in groups]
    out_shape.append(jax.ShapeDtypeStruct((cols, M), BF16))
    out_shape.append(jax.ShapeDtypeStruct((rows // 2 - begin, cols), BF16))

    def kernel(*refs):
        forward_kernel(*refs, rows=rows, cols=cols, n_row=n_row, groups=groups, begin=begin)

    hbm, smem = pl.BlockSpec(memory_space=pltpu.HBM), pl.BlockSpec(memory_space=pltpu.SMEM)
    outs = pl.pallas_call(
        kernel,
        in_specs=[smem, smem, smem, pl.BlockSpec(memory_space=pltpu.VMEM), hbm],
        out_specs=[pl.BlockSpec(memory_space=pltpu.VMEM)] * len(out_shape),
        out_shape=out_shape,
        scratch_shapes=[
            pltpu.VMEM((M, rows), BF16),
            pltpu.VMEM((rows, 2 * M), BF16),
            pltpu.VMEM((2, HALF, HALF), F32),
            pltpu.VMEM((n_row * n_col, per, M), F32),
            pltpu.VMEM((2, HALF, HALF), F32),
            pltpu.SemaphoreType.DMA,
        ],
        compiler_params=pltpu.CompilerParams(vmem_limit_bytes=36 << 20),
        cost_estimate=pl.CostEstimate(
            flops=2 * rows * 2 * M * (cols + M), bytes_accessed=4 * rows * cols, transcendentals=0
        ),
        name="forward",
    )(index, charge, tiles, cotangent, in_hbm(incident))
    return outs[:-2], outs[-2], outs[-1]


def swap(value, axis, bits):
    size = lax.axis_size(axis)
    return lax.ppermute(value, axis, [(i, i ^ bits) for i in range(size)])


def add_up(parts):
    total = parts[0].astype(F32)
    for part in parts[1:]:
        total = total + part.astype(F32)
    return total


def hop_order(n_row):
    return sorted(range(1, n_row), key=lambda k: -(k & -k))


def slot_groups(n_row, n_col):
    order = hop_order(n_row) + [0]
    if n_row <= 4:
        parts = [order[:1], order[1:]]
    else:
        parts = [order[: n_row // 2], order[n_row // 2 :]]
    return [(ky, tuple(slots)) for slots in parts for ky in range(n_col)]


def reduce_blocks(parts, groups, n_row):
    reduced = {}
    for own, (ky, slots) in zip(parts, groups):
        if ky:
            continue
        terms = [own]
        for other, (step, other_slots) in zip(parts, groups):
            if step and other_slots == slots:
                terms.append(swap(other, "col", step))
        total = add_up(terms).astype(BF16)
        for k, kz in enumerate(slots):
            reduced[kz] = total[k]
    moved = [swap(reduced[kz], "row", kz) for kz in hop_order(n_row)]
    return add_up([reduced[0]] + moved).astype(BF16)


def gather_row(mine, n_row):
    found = {0: mine}
    for kz in hop_order(n_row):
        found[kz] = swap(mine, "row", kz)
    return [found[kz] for kz in range(n_row)]


def aligned(pieces):
    if any(piece.shape[0] % 16 for piece in pieces):
        return [jnp.concatenate(pieces, axis=0)]
    return pieces


def row_table_kernel(index_ref, row_tab, fine_ref, *, rows, n_row, n_col, full_rows, waves):
    extent = full_rows * n_row
    row_at = lax.axis_index("row")
    col_at = lax.axis_index("col")
    half_at = lax.rem(lax.axis_index("wl"), 2)
    per = M // (n_row * n_col)
    lane = lax.broadcasted_iota(jnp.int32, (16, M), 1)
    block = lane // per
    owner = ((block // n_row) ^ col_at) * n_row + ((block % n_row) ^ row_at)
    place = owner * per + lane % per
    is_sin = place >= HALF
    focal = 2.0 * jnp.where(is_sin, place - HALF, place).astype(F32) + 1.0
    for w in range(waves):
        period = quarter_period(index_ref[w])
        for side in range(2):
            lanes = slice(side * HALF, (side + 1) * HALF)
            sine = is_sin[:1, lanes]

            def write_row(at, amount, re, im, w=w, lanes=lanes, sine=sine):
                row_tab[w, at : at + amount, lanes] = jnp.where(
                    sine, im.astype(F32), re.astype(F32)
                ).astype(BF16)

            table_focal_lanes(
                write_row,
                period,
                row_at * full_rows + half_at * rows,
                extent,
                row_tab.shape[1],
                fine_ref,
                lanes=focal[:, lanes],
            )


def row_tables(indices, rows, n_row, n_col, full_rows):
    waves = indices.shape[0]
    own_rows = max(rows, 256)

    def kernel(*refs):
        row_table_kernel(*refs, rows=rows, n_row=n_row, n_col=n_col, full_rows=full_rows, waves=waves)

    return pl.pallas_call(
        kernel,
        in_specs=[pl.BlockSpec(memory_space=pltpu.SMEM)],
        out_specs=pl.BlockSpec(memory_space=pltpu.VMEM),
        out_shape=jax.ShapeDtypeStruct((waves, own_rows, M), BF16),
        scratch_shapes=[pltpu.VMEM((2, HALF, HALF), F32)],
        compiler_params=pltpu.CompilerParams(vmem_limit_bytes=16 << 20),
        cost_estimate=pl.CostEstimate(flops=40 * M * own_rows, bytes_accessed=4 * M * own_rows, transcendentals=0),
        name="row_tables",
    )(indices)


def col_table(index, cols, n_col):
    def kernel(index_ref, col_tab, fine_ref):
        def write_col(at, amount, re, im):
            col_tab[at : at + amount, :HALF] = re
            col_tab[at : at + amount, HALF:] = im

        table_focal_lanes(
            write_col,
            quarter_period(index_ref[0]),
            lax.axis_index("col") * cols,
            cols * n_col,
            cols,
            fine_ref,
        )

    return pl.pallas_call(
        kernel,
        in_specs=[pl.BlockSpec(memory_space=pltpu.SMEM)],
        out_specs=pl.BlockSpec(memory_space=pltpu.VMEM),
        out_shape=jax.ShapeDtypeStruct((cols, M), BF16),
        scratch_shapes=[pltpu.VMEM((2, HALF, HALF), F32)],
        compiler_params=pltpu.CompilerParams(vmem_limit_bytes=16 << 20),
        cost_estimate=pl.CostEstimate(flops=20 * M * cols, bytes_accessed=4 * M * cols, transcendentals=0),
        name="col_table",
    )(index)


def backward_kernel(tiles_ref, *refs, counts, wave_ids, part_first, chunks, tile_size, rows, emit):
    waves = len(counts)
    total_pieces = sum(counts)
    sources, refs = refs[:total_pieces], refs[total_pieces:]
    n_tables = 1 + max(table for table, _ in wave_ids)
    row_tabs, refs = refs[:n_tables], refs[n_tables:]
    col_tabs, refs = refs[:waves], refs[waves:]
    incidents, refs = refs[:waves], refs[waves:]
    outs, refs = refs[: len(chunks)], refs[len(chunks) :]
    held, sems = refs[emit : emit + 2]
    matrices = list(refs[:emit] + refs[emit + 2 :])
    half_at = lax.rem(lax.axis_index("wl"), 2)
    first = chunks[0][0]
    copies = []
    for k, (at, amount) in enumerate(chunks):
        for w in range(waves):
            if part_first[w] is None:
                span = pl.ds(pl.multiple_of(half_at * rows + at, 16), amount)
                source = incidents[w].at[0, span, :]
            else:
                source = incidents[w].at[pl.ds(at - part_first[w], amount), :]
            copies.append(
                pltpu.make_async_copy(source, held.at[w, pl.ds(at - first, amount), :], sems.at[k, w])
            )
            copies[-1].start()
    ready = []
    for w in range(waves):
        pieces, sources = sources[: counts[w]], sources[counts[w] :]
        if counts[w] == 1:
            ready.append(pieces[0])
            continue
        target = matrices.pop(0)
        at = 0
        for piece in pieces:
            target[at : at + piece.shape[0], :] = piece[...]
            at += piece.shape[0]
        ready.append(target)
    cols = outs[0].shape[1]
    wide = min(512, cols)
    amount = sum(n for _, n in chunks)
    back_y = [
        jnp.dot(
            row_tabs[table][which, first : first + amount, :], ready[w][...], preferred_element_type=F32
        ).astype(BF16)
        for w, (table, which) in enumerate(wave_ids)
    ]
    for copy in copies:
        copy.wait()
    for part in range(0, cols, wide):
        span = slice(part, part + wide)
        total = None
        for w in range(waves):
            back = lax.dot_general(
                back_y[w], col_tabs[w][span, :], (((1,), (1,)), ((), ())), preferred_element_type=F32
            )
            term = back * held[w, :, span].astype(F32)
            total = term if total is None else total + term
        for out, (at, size) in zip(outs, chunks):
            borders = [at] + list(range((at // tile_size + 1) * tile_size, at + size, tile_size)) + [at + size]
            for low, high in zip(borders, borders[1:]):
                mask = live_row(tiles_ref, half_at * (rows // tile_size) + low // tile_size, cols)[:, span]
                out[low - at : high - at, span] = (total[low - first : high - first] * mask).astype(BF16)


def backward(tiles, waves, chunks, tile_size, rows, keep=False):
    cols = tiles.shape[1] * tile_size
    flat = [piece for wave in waves for piece in wave[0]]
    amount = sum(n for _, n in chunks)
    counts = [len(wave[0]) for wave in waves]
    built = sum(count > 1 for count in counts)
    emit = built if keep else 0
    tables = []
    for wave in waves:
        if not any(wave[1] is table for table in tables):
            tables.append(wave[1])
    wave_ids = [([wave[1] is table for table in tables].index(True), wave[2]) for wave in waves]

    def kernel(*refs):
        backward_kernel(
            *refs,
            counts=counts,
            wave_ids=wave_ids,
            part_first=[wave[5] for wave in waves],
            chunks=chunks,
            tile_size=tile_size,
            rows=rows,
            emit=emit,
        )

    vmem = pl.BlockSpec(memory_space=pltpu.VMEM)
    hbm = pl.BlockSpec(memory_space=pl.ANY)
    out_shape = [jax.ShapeDtypeStruct((n, cols), BF16) for _, n in chunks]
    out_shape += [jax.ShapeDtypeStruct((M, M), BF16)] * emit
    outs = pl.pallas_call(
        kernel,
        in_specs=[pl.BlockSpec(memory_space=pltpu.SMEM)]
        + [vmem] * (len(flat) + len(tables) + len(waves))
        + [hbm] * len(waves),
        out_specs=[vmem] * len(out_shape),
        out_shape=out_shape,
        scratch_shapes=[
            pltpu.VMEM((len(waves), amount, cols), BF16),
            pltpu.SemaphoreType.DMA((len(chunks), len(waves))),
        ]
        + [pltpu.VMEM((M, M), BF16)] * (built - emit),
        compiler_params=pltpu.CompilerParams(vmem_limit_bytes=24 << 20),
        cost_estimate=pl.CostEstimate(
            flops=2 * len(waves) * amount * M * (cols + M), bytes_accessed=6 * amount * cols, transcendentals=0
        ),
    )(tiles, *flat, *tables, *[wave[3] for wave in waves], *[wave[4] for wave in waves])
    return outs[: len(chunks)], outs[len(chunks) :]


def place_kernel(*refs, chunks, rows):
    sources = refs[: len(chunks)]
    out, sems = refs[-2:]
    half_at = lax.rem(lax.axis_index("wl"), 2)
    copies = []
    for k, (at, amount, side) in enumerate(chunks):
        where = half_at if side == 0 else 1 - half_at
        target = out.at[pl.ds(pl.multiple_of(where * rows + at, 16), amount), :]
        copies.append(pltpu.make_async_copy(sources[k], target, sems.at[k]))
    for copy in copies:
        copy.start()
    for copy in copies:
        copy.wait()


def place(flat, chunks, rows, into=None):
    cols = flat[0].shape[1]
    operands = flat + ([into] if into is not None else [])

    def kernel(*refs):
        place_kernel(*refs, chunks=chunks, rows=rows)

    hbm = pl.BlockSpec(memory_space=pl.ANY)
    return pl.pallas_call(
        kernel,
        in_specs=[hbm] * len(operands),
        out_specs=hbm,
        out_shape=jax.ShapeDtypeStruct((2 * rows, cols), BF16),
        scratch_shapes=[pltpu.SemaphoreType.DMA((len(chunks),))],
        input_output_aliases={len(flat): 0} if into is not None else {},
        compiler_params=pltpu.CompilerParams(vmem_limit_bytes=1 << 20),
        cost_estimate=pl.CostEstimate(
            flops=0, bytes_accessed=4 * cols * sum(n for _, n, _ in chunks), transcendentals=0
        ),
    )(*operands)


def own_slice(incident, begin):
    amount, cols = incident.shape[1] // 2 - begin, incident.shape[2]

    def kernel(source, out, sem):
        copy = slice_rows(source, out, sem, lax.rem(lax.axis_index("wl"), 2), begin)
        copy.start()
        copy.wait()

    return pl.pallas_call(
        kernel,
        in_specs=[pl.BlockSpec(memory_space=pltpu.HBM)],
        out_specs=pl.BlockSpec(memory_space=pltpu.VMEM),
        out_shape=jax.ShapeDtypeStruct((amount, cols), BF16),
        scratch_shapes=[pltpu.SemaphoreType.DMA],
        compiler_params=pltpu.CompilerParams(vmem_limit_bytes=4 << 20),
        cost_estimate=pl.CostEstimate(flops=4 << 30, bytes_accessed=4 * amount * cols, transcendentals=0),
        name="own_slice",
    )(in_hbm(incident))


BOUNDS = (0, 4, 7, 9, 13, 16)
EXCHANGED = 3


def all_steps(cotangent, incident, tiles, charge, wl_index):
    rows, cols = cotangent.shape[2:]
    n_row = lax.axis_size("row")
    n_col = lax.axis_size("col")
    tile_size = rows // tiles.shape[0]
    half = rows // 2
    bounds = [half * bound // 16 // 16 * 16 for bound in BOUNDS]
    chunks = [(low, high - low) for low, high in zip(bounds, bounds[1:])]
    n_first = EXCHANGED
    split = chunks[n_first][0]

    inc_straight = swap(own_slice(incident, split), "wl", 2)
    groups = slot_groups(n_row, n_col)
    parts, col_own, slice_other = forward(
        wl_index, charge, tiles, cotangent, incident, split, n_row, n_col, groups
    )
    mine = reduce_blocks(parts, groups, n_row)
    inc_core = swap(incident, "wl", 1)
    inc_cross = swap(slice_other, "wl", 3)
    col_core = swap(col_own, "wl", 1)
    near = jnp.concatenate([wl_index, swap(wl_index, "wl", 1)])
    far = swap(wl_index, "wl", 2)
    far_core = swap(far, "wl", 1)
    row_near = row_tables(near, half, n_row, n_col, rows)
    row_far = row_tables(jnp.concatenate([far, far_core]), half, n_row, n_col, rows)
    col_straight = col_table(far, cols, n_col)
    col_cross = swap(col_straight, "wl", 1)

    here = gather_row(mine, n_row)
    if n_row > 4:
        here = [jnp.concatenate(here, axis=0)]
    joined = jnp.concatenate(here, axis=0)
    pieces, pieces_core = [joined], [swap(joined, "wl", 1)]
    for ky in range(1, n_col):
        for piece in here:
            pieces.append(swap(piece, "col", ky))
            pieces_core.append(swap(pieces[-1], "wl", 1))

    straight = [swap(joined, "wl", 2)]
    straight += [swap(straight[0], "col", ky) for ky in range(1, n_col)]
    cross = [swap(piece, "wl", 1) for piece in straight]

    own = (aligned(pieces), row_near, 0, col_own, incident, None)
    mate = (aligned(pieces_core), row_near, 1, col_core, inc_core, None)
    first, matrices = backward(tiles, [own, mate], chunks[:1], tile_size, half, keep=True)
    if len(matrices) == 2:
        own = ([matrices[0]],) + own[1:]
        mate = ([matrices[1]],) + mate[1:]
    second, _ = backward(tiles, [own, mate], chunks[1:n_first], tile_size, half)
    straight = (aligned(straight), row_far, 0, col_straight, inc_straight, split)
    cross = (aligned(cross), row_far, 1, col_cross, inc_cross, split)
    both, _ = backward(tiles, [own, mate, straight, cross], chunks[n_first:], tile_size, half)
    done = []
    for pair in list(first) + list(second):
        total = add_up([pair, swap(pair, "wl", 2)]).astype(BF16)
        done.append((total, swap(total, "wl", 1)))
    ready = [(part, swap(part, "wl", 1)) for part in both]

    def sides(pairs, some):
        flat = [part for pair in pairs for part in pair]
        return flat, [(at, amount, side) for at, amount in some for side in range(2)]

    flat, where = sides(ready, chunks[n_first:])
    result = place(flat, where, half)
    flat, where = sides(done, chunks[:n_first])
    result = place(flat[:-1], where[:-1], half, result)
    return place(flat[-1:], where[-1:], half, result)


def solution(mesh):
    return jax.shard_map(
        all_steps,
        mesh=mesh,
        in_specs=(
            P("wl", None, "row", "col"),
            P("wl", "row", "col"),
            P("row", "col"),
            P("wl"),
            P("wl"),
        ),
        out_specs=P("row", "col"),
        check_vma=False,
    )
```
